32 devices in a mesh: wide: 8 (over z, y), narrow: 4 (over x, core).
Axes of the slice: x: 2, y: 2, z: 4, core: 2. Of those that a mesh axis runs over, the one named last changes fastest.
Arguments:
- layer_in: bfloat16 [128, 2048, 768], P(('wide', 'narrow')), may hold values from -6 to 6
- lengths: int32 [128], P(('wide', 'narrow')), may hold values from 1024 to 2048, as said below
- padding: int32 [128, 2048], P(('wide', 'narrow')), may hold values from 0 to 1, as said below
- picked: int32 [128, 256], P(('wide', 'narrow')), may hold values from 0 to 2047, as said below
- first_gain: bfloat16 [768], P(('wide', 'narrow')), may hold values from 0.5 to 1.5
- project_in: bfloat16 [768, 2304], P(('wide', 'narrow')), may hold values from -0.21875 to 0.21875
- project_out: bfloat16 [768, 768], P(None, ('wide', 'narrow')), may hold values from -0.875 to 0.875
- second_gain: bfloat16 [768], P(('wide', 'narrow')), may hold values from 0.5 to 1.5
- up_weight: bfloat16 [768, 3072], P(('wide', 'narrow')), may hold values from -0.21875 to 0.21875
- up_bias: bfloat16 [3072], P(('wide', 'narrow')), may hold values from -3 to 3
- down_weight: bfloat16 [3072, 768], P(None, ('wide', 'narrow')), may hold values from -0.109375 to 0.109375
- down_bias: bfloat16 [768], P(('wide', 'narrow')), may hold values from -3 to 3
- router: bfloat16 [768], P(('wide', 'narrow')), may hold values from -0.21875 to 0.21875
- cotangent: bfloat16 [128, 2048, 768], P(('wide', 'narrow')), may hold values from -6 to 6
Outputs:
- layer_out: bfloat16 [128, 2048, 768], P(('wide', 'narrow'))
- input_grad: bfloat16 [128, 2048, 768], P(('wide', 'narrow'))
- first_gain_grad: float32 [768], P(('wide', 'narrow'))
- project_in_grad: float32 [768, 2304], P(('wide', 'narrow'))
- project_out_grad: float32 [768, 768], P(None, ('wide', 'narrow'))
- second_gain_grad: float32 [768], P(('wide', 'narrow'))
- up_weight_grad: float32 [768, 3072], P(('wide', 'narrow'))
- up_bias_grad: float32 [3072], P(('wide', 'narrow'))
- down_weight_grad: float32 [3072, 768], P(None, ('wide', 'narrow'))
- down_bias_grad: float32 [768], P(('wide', 'narrow'))
- router_grad: float32 [768], P(('wide', 'narrow'))
The draws below stay inside these ranges and needn't reach their ends.
Inputs may be any that keep to these rules, and one draw needn't show every extreme that they name: `lengths`: each sequence's true token count; one sequence has exactly 2048, one exactly 1024. `padding`: row b is 1 on one contiguous run of lengths[b] positions and 0 elsewhere. `picked`: the first lengths[b] // 8 entries of row b are strictly increasing positions at which padding is 1; the other entries are 0.
All inputs are finite; a program needn't handle non-finite values.
Results may differ from the reference program's by a relative error of at most 0.01.
Values may be sent and summed in bfloat16 or wider, within the bound.
No kernel may reach another device: no remote copies, remote signals or barrier semaphores. Data moves between devices by JAX's collectives and lax.ppermute only.
A program may use at most 256 MiB of HBM per device.

```python
import math
import jax
import jax.numpy as jnp
from jax import lax

D = 768
HEAD_DIM = 64
FF = 3072
L = 2048
CAP = 256
SEQS = 128


def shuffled_row(row_key):
    return jax.random.permutation(row_key, L)


def selection_draw(key):
    length_key = jax.random.fold_in(key, 101)
    offset_key = jax.random.fold_in(key, 202)
    order_key = jax.random.fold_in(key, 303)
    seq_lengths = jax.random.randint(length_key, (SEQS,), L // 2, L + 1)
    seq_lengths = seq_lengths.at[0].set(L).at[1].set(L // 2)
    offsets = jax.random.randint(offset_key, (SEQS,), 0, L - seq_lengths + 1)
    positions = jnp.arange(L)[None, :]
    inside = (positions >= offsets[:, None]) & (positions < (offsets + seq_lengths)[:, None])
    padding_out = inside.astype(jnp.int32)
    row_keys = jax.random.split(order_key, SEQS)
    ranks = jax.vmap(shuffled_row)(row_keys).astype(jnp.int32)
    ranks = jnp.where(inside, ranks, ranks + L)
    ranks = ranks.at[0, L - 1].set(-1)
    order = jnp.argsort(ranks, axis=1, stable=True)[:, :CAP].astype(jnp.int32)
    counts = seq_lengths // 8
    used = jnp.arange(CAP)[None, :] < counts[:, None]
    chosen = jnp.sort(jnp.where(used, order, L), axis=1)
    picked_out = jnp.where(used, chosen, 0).astype(jnp.int32)
    return (seq_lengths.astype(jnp.int32), padding_out, picked_out)


def draw_lengths(key, part):
    return selection_draw(key)[0]


def draw_padding(key, part):
    return selection_draw(key)[1]


def draw_picked(key, part):
    return selection_draw(key)[2]


def raised(values, key, source, target, blocks, factor):
    def block_of(dim):
        return (jnp.arange(values.shape[dim]) // (values.shape[dim] // blocks)).reshape((-1,) + (1,) * (values.ndim - 1 - dim))

    one_side = jax.random.permutation(key, blocks)[block_of(target)]
    far = (block_of(target) + blocks // 2) % blocks
    return jnp.where((block_of(source) == one_side) | (block_of(source) == far), factor * values, values)


def steps_of(rng, extent, pieces, low, top_value):
    def one(dim, shards_of):
        steps = jax.random.uniform(jax.random.fold_in(jax.random.fold_in(rng, 6), dim), (shards_of,), jnp.float32, low / len(pieces), top_value / len(pieces))
        return jnp.repeat(jnp.exp(steps), extent[dim] // shards_of).reshape((-1,) + (1,) * (len(extent) - dim - 1))

    level = one(*pieces[0])
    for cut in pieces[1:]:
        level = level * one(*cut)
    return level


def centred(rng, dims, scale, limit, pieces=(), held_as=jnp.bfloat16):
    drawn = jax.random.normal(rng, dims, jnp.float32) * scale
    if len(pieces) > 0:
        drawn = steps_of(rng, dims, pieces, -0.22, 0.18) * drawn
    return jnp.clip(drawn, min=-limit, max=limit).astype(held_as)


def bell_draw_with(own_key, extent, width, most, cuts, heavy, dtype=jnp.bfloat16):
    array = width * jax.random.normal(own_key, extent, jnp.float32)
    if cuts:
        array = array * steps_of(own_key, extent, cuts, -0.22, 0.18)
    return jnp.clip(raised(array, jax.random.fold_in(own_key, 3), *heavy), -most, most).astype(dtype)


def setup_inputs(seed: int = 0) -> dict:
    streams_of = jax.random.split(jax.random.key(seed), 15)
    return {
        "layer_in": bell_draw_with(streams_of[0], (SEQS, L, D), 1.0, 6.0, ((0, 32),), (0, 2, 32, 2.75)),
        "lengths": draw_lengths(jax.random.fold_in(streams_of[14], 71), 0),
        "padding": draw_padding(jax.random.fold_in(streams_of[14], 71), 0),
        "picked": draw_picked(jax.random.fold_in(streams_of[14], 71), 0),
        "first_gain": jnp.clip(1.0 + 0.1 * jax.random.normal(streams_of[4], (D,), jnp.float32), 0.5, 1.5).astype(jnp.bfloat16),
        "project_in": centred(streams_of[5], (D, 3 * D), D ** -0.5, 0.21875, ((0, 32),)),
        "project_out": centred(streams_of[6], (D, D), (D // 16) ** -0.5, 0.875, ((1, 32),)),
        "second_gain": jnp.clip(1.0 + 0.1 * jax.random.normal(streams_of[7], (D,), jnp.float32), 0.5, 1.5).astype(jnp.bfloat16),
        "up_weight": centred(streams_of[8], (D, FF), D ** -0.5, 0.21875, ((0, 32),)),
        "up_bias": centred(streams_of[9], (FF,), 0.5, 3.0, ((0, 32),)),
        "down_weight": centred(streams_of[10], (FF, D), FF ** -0.5, 0.109375, ((1, 32),)),
        "down_bias": centred(streams_of[11], (D,), 0.5, 3.0, ((0, 32),)),
        "router": centred(streams_of[12], (D,), D ** -0.5, 0.21875, ((0, 32),)),
        "cotangent": bell_draw_with(streams_of[13], (SEQS, L, D), 1.0, 6.0, ((0, 32),), (0, 2, 32, 2.75)),
    }


@jax.custom_vjp
def low(v):
    return lax.optimization_barrier(v.astype(jnp.bfloat16)).astype(jnp.float32)

@jax.custom_vjp
def low_back(v):
    return v

def low_keep(v):
    return (low(v), None)

def low_pass(kept, grad):
    return (grad,)

def back_keep(v):
    return (v, None)

def back_low(kept, grad):
    return (low(grad),)
low.defvjp(low_keep, low_pass)
low_back.defvjp(back_keep, back_low)
EPSILON = 1e-06
NEG_FILL = -1e+30
HIGH = lax.Precision.HIGHEST

def rms_scale(values, gain_vec):
    inverse = lax.rsqrt(lax.optimization_barrier(jnp.mean(values * values, axis=-1, keepdims=True)) + EPSILON)
    return values * inverse * gain_vec

def mod_block(layer_x, params, pad_f, picked, valid_f):
    first_gain, proj_in, proj_out, second_gain, up_weight, up_bias, down_weight, down_bias, router = params
    seq_count = layer_x.shape[0]
    slot_count = picked.shape[1]
    model_width = layer_x.shape[2]
    head_count = model_width // HEAD_DIM
    seq_ids = jnp.arange(seq_count)[:, None]
    selected = layer_x[seq_ids, picked]
    normed_one = low(rms_scale(selected, first_gain))
    qkv_all = low(low_back(jnp.matmul(normed_one, proj_in, precision=HIGH)))
    head_shape = (seq_count, slot_count, head_count, HEAD_DIM)
    q_heads = qkv_all[..., :model_width].reshape(head_shape)
    k_heads = qkv_all[..., model_width:2 * model_width].reshape(head_shape)
    v_heads = qkv_all[..., 2 * model_width:].reshape(head_shape)
    raw_scores = low_back(jnp.einsum('gshe,gthe->ghst', q_heads, k_heads, precision=HIGH) * HEAD_DIM ** (-0.5))
    slot_ids = jnp.arange(slot_count)
    causal = slot_ids[None, :] <= slot_ids[:, None]
    allowed = causal[None, None] & (valid_f[:, None, None, :] > 0.5)
    masked_scores = jnp.where(allowed, raw_scores, NEG_FILL)
    probs = low(jax.nn.softmax(masked_scores, axis=-1))
    mixed = jnp.einsum('ghst,gthe->gshe', probs, v_heads, precision=HIGH)
    attended = low_back(low(mixed.reshape(seq_count, slot_count, model_width)))
    attn_out = low_back(jnp.matmul(attended, proj_out, precision=HIGH))
    mid_stream = selected + attn_out
    normed_two = low(rms_scale(mid_stream, second_gain))
    up_pre = low_back(jnp.matmul(normed_two, up_weight, precision=HIGH) + up_bias)
    up_act = low(jax.nn.gelu(up_pre, approximate=True))
    mlp_out = low_back(jnp.matmul(up_act, down_weight, precision=HIGH) + down_bias)
    router_rate = jax.nn.sigmoid(lax.optimization_barrier(jnp.sum(selected * router, axis=-1, keepdims=True)))
    update = router_rate * (attn_out + mlp_out) * valid_f[:, :, None]
    placed = jnp.zeros_like(layer_x).at[seq_ids, picked].add(update)
    return pad_f[:, :, None] * (layer_x + placed)

def reference(layer_in, lengths, padding, picked, first_gain, project_in, project_out, second_gain, up_weight, up_bias, down_weight, down_bias, router, cotangent):
    initials = (first_gain, project_in, project_out, second_gain, up_weight, up_bias, down_weight, down_bias, router)
    params = tuple((weight_arr.astype(jnp.float32) for weight_arr in initials))
    seq_total = layer_in.shape[0]
    group_size = math.gcd(seq_total, max(1, 4096 // L))
    group_count = seq_total // group_size

    def regroup(array_in):
        return array_in.reshape((group_count, group_size) + array_in.shape[1:])

    def one_group(grad_sum, group_data):
        group_x, group_len, group_pad, group_pick, group_cot = group_data
        valid_f = (jnp.arange(CAP)[None, :] < (group_len // 8)[:, None]).astype(jnp.float32)
        pad_f = group_pad.astype(jnp.float32)

        def inner_fn(layer_x, weights_now):
            return mod_block(layer_x, weights_now, pad_f, group_pick, valid_f)
        group_out, pullback = jax.vjp(inner_fn, group_x.astype(jnp.float32), params)
        group_dx, weight_grads = pullback(group_cot.astype(jnp.float32))
        grad_sum = jax.tree.map(jnp.add, grad_sum, weight_grads)
        return (grad_sum, (group_out.astype(jnp.bfloat16), group_dx.astype(jnp.bfloat16)))
    zero_grads = tuple((jnp.zeros(param_arr.shape, jnp.float32) for param_arr in params))
    group_data = (regroup(layer_in), regroup(lengths), regroup(padding), regroup(picked), regroup(cotangent))
    grad_total, (outs_grouped, dx_grouped) = lax.scan(one_group, zero_grads, group_data)
    layer_out = outs_grouped.reshape(layer_in.shape)
    input_grad = dx_grouped.reshape(layer_in.shape)
    return (layer_out, input_grad, grad_total[0], grad_total[1], grad_total[2], grad_total[3], grad_total[4], grad_total[5], grad_total[6], grad_total[7], grad_total[8])
```

```python
from functools import partial

import jax
import jax.numpy as jnp
from jax import lax
from jax.experimental import pallas as pl
from jax.experimental.pallas import tpu as pltpu
from jax.sharding import PartitionSpec as P

HEAD_DIM = 64
EPSILON = 1e-06
NEG_FILL = -1e30
F32 = jnp.float32
BF16 = jnp.bfloat16
AXES = ("wide", "narrow")
SCALE = HEAD_DIM**-0.5
GELU_A = 0.7978845608028654
GELU_B = 0.044715
LSE_LANE = 16
ANY = pl.BlockSpec(memory_space=pl.ANY)
VMEM_LIMIT = 62 * 1024 * 1024


def dot(left, right, left_dim=1, right_dim=0):
    return lax.dot_general(
        left, right, (((left_dim,), (right_dim,)), ((), ())), preferred_element_type=F32
    )


def params(*semantics):
    return pltpu.CompilerParams(
        dimension_semantics=semantics or None, vmem_limit_bytes=VMEM_LIMIT
    )


def whole(shape):
    return pl.BlockSpec(shape, lambda *_: (0,) * len(shape))


def cost(flops, bytes_accessed):
    return pl.CostEstimate(
        flops=int(flops), bytes_accessed=int(bytes_accessed), transcendentals=0
    )


def load_rows(blocks, target, perm, row, sems, columns):
    count, height, _ = blocks.shape
    copies = []
    for j in range(count):
        start = pl.multiple_of(perm[row, j] * height, 8)
        copies.append(
            pltpu.make_async_copy(
                blocks.at[j],
                target.at[pl.ds(start, height), columns],
                sems.at[j],
            )
        )
    return copies


def store_rows(target, value, inverse, row, count):
    height = value.shape[0] // count
    for c in range(count):
        start = pl.multiple_of(inverse[row, c] * height, 8)
        target[pl.ds(start, height), :] = value[c * height : (c + 1) * height, :]


def gather_kernel(target, x, cot, sel, grad):
    length = x.shape[1]
    places = lax.broadcasted_iota(jnp.int32, (target.shape[1], length), 1)
    chosen = jnp.where(target[0] == places, 1.0, 0.0).astype(BF16)
    sel[...] = dot(chosen, x[0]).astype(BF16)
    grad[...] = dot(chosen, cot[0]).astype(BF16)


def gather_rows(target, layer_in, cotangent):
    seqs, length, width = layer_in.shape
    slots = target.shape[1]
    big = pl.BlockSpec((1, length, width), lambda b: (b, 0, 0))
    out = pl.BlockSpec((slots, width), lambda b: (b, 0))
    return pl.pallas_call(
        gather_kernel,
        grid=(seqs,),
        in_specs=[pl.BlockSpec((1, slots, 1), lambda b: (b, 0, 0)), big, big],
        out_specs=[out, out],
        out_shape=[jax.ShapeDtypeStruct((seqs * slots, width), BF16)] * 2,
        compiler_params=params("arbitrary"),
        cost_estimate=cost(
            4 * seqs * slots * length * width, 4 * seqs * length * width
        ),
        name="gather_rows",
    )(target, layer_in, cotangent)


def allowed_keys(slots, valid):
    rows = lax.broadcasted_iota(jnp.int32, (2 * slots, slots), 0)
    rows = jnp.where(rows >= slots, rows - slots, rows)
    keys = lax.broadcasted_iota(jnp.int32, (2 * slots, slots), 1)
    return (keys <= rows) & (keys < valid)


def split_pair(pair):
    lane = lax.broadcasted_iota(jnp.int32, pair.shape, 1)
    zero = jnp.zeros_like(pair)
    first = lane < HEAD_DIM
    return jnp.concatenate(
        [jnp.where(first, pair, zero), jnp.where(first, zero, pair)], axis=0
    )


def join_pair(stacked):
    half = stacked.shape[0] // 2
    lane = lax.broadcasted_iota(jnp.int32, (half, stacked.shape[1]), 1)
    return jnp.where(lane < HEAD_DIM, stacked[:half], stacked[half:])


def pair_columns(pair, half_width):
    per_half = half_width // (2 * HEAD_DIM)
    side, place = divmod(pair, per_half)
    base = side * 3 * half_width + place * 2 * HEAD_DIM
    return tuple(slice(base + k * half_width, base + k * half_width + 2 * HEAD_DIM) for k in range(3))


def forward_kernel(
    perm, inverse, counts,
    sel, grad, vec, in_own, in_oth, out_own, out_oth,
    qkv, att, mid, n2, n2t, g, gt, n1t, stats,
    w_in, w_out, sem_in, sem_out,
    *, blocks,
):
    b = pl.program_id(0)
    slots, width = sel.shape
    half = in_own.shape[2]
    out_half = out_own.shape[2]

    def in_copies():
        return load_rows(in_own, w_in, perm, 0, sem_in.at[0], pl.ds(0, half)) + load_rows(
            in_oth, w_in, perm, 0, sem_in.at[1], pl.ds(half, half)
        )

    def out_copies():
        return load_rows(out_own, w_out, perm, 1, sem_out.at[0], pl.ds(0, out_half)) + load_rows(
            out_oth, w_out, perm, 1, sem_out.at[1], pl.ds(out_half, out_half)
        )

    @pl.when(b == 0)
    def _():
        first = in_copies()
        for c in first + out_copies():
            c.start()
        for c in first:
            c.wait()

    x = sel[...].astype(F32)
    r1 = lax.rsqrt(jnp.mean(x * x, axis=-1, keepdims=True) + EPSILON)
    n1 = (x * r1 * vec[0:1, :]).astype(BF16)
    logit = jnp.sum(x * vec[3:4, :], axis=-1, keepdims=True)
    rate = jax.nn.sigmoid(logit)
    d_mlp = (rate * grad[...].astype(F32)).astype(BF16)
    g[...] = d_mlp
    store_rows(gt, d_mlp.T, inverse, 1, blocks)
    store_rows(n1t, n1.T, inverse, 2, blocks)
    qkv[...] = dot(n1, w_in[...]).astype(BF16)

    allowed = allowed_keys(slots, counts[b])
    lane = lax.broadcasted_iota(jnp.int32, (slots, 128), 1)
    kept = jnp.where(lane == 0, r1, jnp.where(lane == 1, rate, 0.0))
    for pair in range(width // (2 * HEAD_DIM)):
        qc, kc, vc = pair_columns(pair, width // 2)
        scores = dot(split_pair(qkv[:, qc] * SCALE), qkv[:, kc], 1, 1)
        scores = jnp.where(allowed, scores, NEG_FILL)
        top = jnp.max(scores, axis=-1, keepdims=True)
        exps = jnp.exp(scores - top)
        total = jnp.sum(exps, axis=-1, keepdims=True)
        lse = top + jnp.log(total)
        probs = (exps * (1.0 / total)).astype(BF16)
        att[:, pair * 128 : (pair + 1) * 128] = join_pair(dot(probs, qkv[:, vc])).astype(BF16)
        kept = jnp.where(lane == LSE_LANE + 2 * pair, lse[:slots], kept)
        kept = jnp.where(lane == LSE_LANE + 2 * pair + 1, lse[slots:], kept)

    @pl.when(b == 0)
    def _():
        for c in out_copies():
            c.wait()

    stream = x + dot(att[...], w_out[...], 1, 1)
    mid[...] = stream
    r2 = lax.rsqrt(jnp.mean(stream * stream, axis=-1, keepdims=True) + EPSILON)
    normed = (stream * r2 * vec[1:2, :]).astype(BF16)
    n2[...] = normed
    store_rows(n2t, normed.T, inverse, 0, blocks)
    stats[...] = jnp.where(lane == 2, r2, kept)


def forward_block(perm, inverse, counts, sel, grad, vec, in_own, in_oth, out_own, out_oth):
    rows, width = sel.shape
    seqs = counts.shape[0]
    slots = rows // seqs
    blocks = in_own.shape[0]
    row = lambda w: pl.BlockSpec((slots, w), lambda b, *_: (b, 0))
    col = pl.BlockSpec((width, slots), lambda b, *_: (0, b))
    shape = jax.ShapeDtypeStruct
    return pl.pallas_call(
        partial(forward_kernel, blocks=blocks),
        grid_spec=pltpu.PrefetchScalarGridSpec(
            num_scalar_prefetch=3,
            grid=(seqs,),
            in_specs=[row(width), row(width), whole(vec.shape), ANY, ANY, ANY, ANY],
            out_specs=[row(3 * width), row(width), row(width), row(width), col, row(width), col, col, row(128)],
            scratch_shapes=[
                pltpu.VMEM((width, 3 * width), BF16),
                pltpu.VMEM((width, width), BF16),
                pltpu.SemaphoreType.DMA((2, blocks)),
                pltpu.SemaphoreType.DMA((2, blocks)),
            ],
        ),
        out_shape=[
            shape((rows, 3 * width), BF16),
            shape((rows, width), BF16),
            shape((rows, width), F32),
            shape((rows, width), BF16),
            shape((width, rows), BF16),
            shape((rows, width), BF16),
            shape((width, rows), BF16),
            shape((width, rows), BF16),
            shape((rows, 128), F32),
        ],
        compiler_params=params("arbitrary"),
        cost_estimate=cost(10 * rows * width * width, 30 * rows * width),
        name="forward_block",
    )(perm, inverse, counts, sel, grad, vec, in_own, in_oth, out_own, out_oth)


def mlp_kernel(
    perm, n2, n2t, g, gt, up, down, bias, *rest, carried, tile
):
    if carried:
        mlp_in, dn2_in, *rest = rest
    mlp, dn2, dup, ddown, dbias, w_up, w_down, sem_up, sem_down = rest
    i = pl.program_id(0)
    tiles = pl.num_programs(0)

    def copies(t):
        cols = pl.ds(pl.multiple_of(t * tile, 128), tile)
        return load_rows(up.at[:, :, cols], w_up, perm, 2, sem_up.at[t], cols) + load_rows(
            down.at[:, :, cols], w_down, perm, 3, sem_down.at[t], cols
        )

    @pl.when(i == 0)
    def _():
        for t in range(w_up.shape[1] // tile):
            for c in copies(t):
                c.start()

    for c in copies(i):
        c.wait()
    here = pl.ds(pl.multiple_of(i * tile, 128), tile)
    up_now = w_up[:, here]
    down_now = w_down[:, here]
    pre = dot(n2[...], up_now) + bias[...]
    square = pre * pre
    th = jnp.tanh(pre * (GELU_A + GELU_A * GELU_B * square))
    half = 0.5 * (1.0 + th)
    act = (pre * half).astype(BF16)
    slope = half + 0.5 * pre * (1.0 - th * th) * (GELU_A + 3 * GELU_A * GELU_B * square)
    d_pre = (slope * dot(g[...], down_now)).astype(BF16)
    dbias[...] = jnp.sum(d_pre.astype(F32), axis=0, keepdims=True)
    mlp_now = dot(act, down_now, 1, 1)
    dn2_now = dot(d_pre, up_now, 1, 1)

    @pl.when(i == 0)
    def _():
        if carried:
            mlp[...] = mlp_in[...] + mlp_now
            dn2[...] = dn2_in[...] + dn2_now
        else:
            mlp[...] = mlp_now
            dn2[...] = dn2_now

    @pl.when(i > 0)
    def _():
        mlp[...] += mlp_now
        dn2[...] += dn2_now

    dup[...] = dot(n2t[...], d_pre).astype(BF16)
    ddown[...] = dot(gt[...], act).astype(BF16)


def mlp_half(perm, n2, n2t, g, gt, up, down, bias, carry=()):
    rows, width = n2.shape
    blocks, height, hidden = up.shape
    tile = min(768, hidden)
    col = lambda r: pl.BlockSpec((r, tile), lambda i, *_: (0, i))
    shape = jax.ShapeDtypeStruct
    return pl.pallas_call(
        partial(mlp_kernel, carried=bool(carry), tile=tile),
        grid_spec=pltpu.PrefetchScalarGridSpec(
            num_scalar_prefetch=1,
            grid=(hidden // tile,),
            in_specs=[
                whole((rows, width)), whole((width, rows)), whole((rows, width)), whole((width, rows)),
                ANY, ANY, col(1),
            ] + [whole((rows, width))] * len(carry),
            out_specs=[whole((rows, width)), whole((rows, width)), col(width), col(width), col(1)],
            scratch_shapes=[
                pltpu.VMEM((width, hidden), BF16),
                pltpu.VMEM((width, hidden), BF16),
                pltpu.SemaphoreType.DMA((hidden // tile, blocks)),
                pltpu.SemaphoreType.DMA((hidden // tile, blocks)),
            ],
        ),
        out_shape=[
            shape((rows, width), F32),
            shape((rows, width), F32),
            shape((width, hidden), BF16),
            shape((width, hidden), BF16),
            shape((1, hidden), F32),
        ],
        compiler_params=params("arbitrary"),
        cost_estimate=cost(12 * rows * width * hidden, 8 * rows * width),
        name="mlp_half",
    )(perm, n2, n2t, g, gt, up, down, bias, *carry)


def norm_pull(values, inverse, scaled):
    return inverse * scaled - values * (
        inverse * inverse * inverse * jnp.mean(scaled * values, axis=-1, keepdims=True)
    )


def backward_kernel(
    perm, inverse, counts,
    sel, grad, vec, qkv, mid, stats, mlp, dn2, out_own, out_oth,
    dqkv, dattnt, dmid, new_rows, drouter,
    w_out, sem_out,
    *, blocks,
):
    b = pl.program_id(0)
    slots, width = sel.shape
    out_half = out_own.shape[2]

    @pl.when(b == 0)
    def _():
        copies = load_rows(out_own, w_out, perm, 1, sem_out.at[0], pl.ds(0, out_half)) + load_rows(
            out_oth, w_out, perm, 1, sem_out.at[1], pl.ds(out_half, out_half)
        )
        for c in copies:
            c.start()
        for c in copies:
            c.wait()

    x = sel[...].astype(F32)
    stream = mid[...]
    rate = stats[:, 1:2]
    r2 = stats[:, 2:3]
    slot_grad = grad[...].astype(F32)
    branch = (stream - x) + (mlp[...] + vec[2:3, :])
    new_rows[...] = (x + rate * branch).astype(BF16)
    d_logit = jnp.sum(slot_grad * branch, axis=-1, keepdims=True) * (rate * (1.0 - rate))
    router_now = jnp.sum(d_logit * x, axis=0, keepdims=True)

    @pl.when(b == 0)
    def _():
        drouter[...] = router_now

    @pl.when(b > 0)
    def _():
        drouter[...] += router_now

    d_mid = norm_pull(stream, r2, vec[1:2, :] * dn2[...])
    dmid[...] = d_mid + d_logit * vec[3:4, :]
    d_attn = (rate * slot_grad + d_mid).astype(BF16)
    store_rows(dattnt, d_attn.T, inverse, 2, blocks)
    d_att = dot(d_attn, w_out[...]).astype(BF16)

    allowed = allowed_keys(slots, counts[b])
    for pair in range(width // (2 * HEAD_DIM)):
        qc, kc, vc = pair_columns(pair, width // 2)
        queries = split_pair(qkv[:, qc] * SCALE)
        keys = qkv[:, kc]
        lse = jnp.concatenate(
            [
                stats[:, LSE_LANE + 2 * pair : LSE_LANE + 2 * pair + 1],
                stats[:, LSE_LANE + 2 * pair + 1 : LSE_LANE + 2 * pair + 2],
            ],
            axis=0,
        )
        upstream = split_pair(d_att[:, pair * 128 : (pair + 1) * 128])
        scores = dot(queries, keys, 1, 1)
        probs = jnp.exp(jnp.where(allowed, scores - lse, NEG_FILL))
        d_probs = dot(upstream, qkv[:, vc], 1, 1)
        d_scores = (probs * (d_probs - jnp.sum(probs * d_probs, axis=-1, keepdims=True))).astype(BF16)
        dqkv[:, qc] = (join_pair(dot(d_scores, keys)) * SCALE).astype(BF16)
        dqkv[:, kc] = dot(d_scores, queries, 0, 0).astype(BF16)
        dqkv[:, vc] = dot(probs.astype(BF16), upstream, 0, 0).astype(BF16)


def backward_block(perm, inverse, counts, sel, grad, vec, qkv, mid, stats, mlp, dn2, out_own, out_oth):
    rows, width = sel.shape
    seqs = counts.shape[0]
    slots = rows // seqs
    blocks = out_own.shape[0]
    row = lambda w: pl.BlockSpec((slots, w), lambda b, *_: (b, 0))
    col = pl.BlockSpec((width, slots), lambda b, *_: (0, b))
    shape = jax.ShapeDtypeStruct
    return pl.pallas_call(
        partial(backward_kernel, blocks=blocks),
        grid_spec=pltpu.PrefetchScalarGridSpec(
            num_scalar_prefetch=3,
            grid=(seqs,),
            in_specs=[
                row(width), row(width), whole(vec.shape), row(3 * width), row(width), row(128),
                row(width), row(width), ANY, ANY,
            ],
            out_specs=[row(3 * width), col, row(width), row(width), whole((1, width))],
            scratch_shapes=[
                pltpu.VMEM((width, width), BF16),
                pltpu.SemaphoreType.DMA((2, blocks)),
            ],
        ),
        out_shape=[
            shape((rows, 3 * width), BF16),
            shape((width, rows), BF16),
            shape((rows, width), F32),
            shape((rows, width), BF16),
            shape((1, width), F32),
        ],
        compiler_params=params("arbitrary"),
        cost_estimate=cost(20 * rows * width * width, 30 * rows * width),
        name="backward_block",
    )(perm, inverse, counts, sel, grad, vec, qkv, mid, stats, mlp, dn2, out_own, out_oth)


def project_kernel(n1t, dattnt, dqkv, att, small, out):
    half = dqkv.shape[1]
    third = att.shape[1]
    out[:, :half] = dot(n1t[...], dqkv[...]).astype(BF16)
    out[:, half : half + third] = dot(dattnt[...], att[...]).astype(BF16)
    out[:, half + third :] = small[...]


def project_grads(n1t, dattnt, dqkv, att, small, side):
    width, rows = n1t.shape
    half, third, extra = dqkv.shape[1] // 2, att.shape[1] // 2, small.shape[1]
    total = half + third + extra
    return pl.pallas_call(
        project_kernel,
        grid=(1,),
        in_specs=[
            whole((width, rows)), whole((width, rows)),
            pl.BlockSpec((rows, half), lambda i: (0, side)),
            pl.BlockSpec((rows, third), lambda i: (0, side)),
            whole((width, extra)),
        ],
        out_specs=whole((width, total)),
        out_shape=jax.ShapeDtypeStruct((width, total), BF16),
        compiler_params=params("arbitrary"),
        cost_estimate=cost(2 * width * rows * total, 2 * (2 * width * rows + rows * total + width * total)),
        name="project_grads",
    )(n1t, dattnt, dqkv, att, small)


def place(rows, target, x, start, count):
    length = x.shape[0]
    places = lax.broadcasted_iota(jnp.int32, (length, target.shape[1]), 0)
    hits = target == places
    moved = dot(jnp.where(hits, 1.0, 0.0).astype(BF16), rows)
    hit = jnp.max(jnp.where(hits, 1.0, 0.0), axis=-1, keepdims=True)
    at = lax.broadcasted_iota(jnp.int32, (length, 1), 0)
    kept = (at >= start) & (at < start + count) & (hit < 0.5)
    return jnp.where(kept, x.astype(F32), moved).astype(BF16)


def out_kernel(runs, rows, target, x, out):
    b = pl.program_id(0)
    out[0] = place(rows[...], target[0], x[0], runs[0, b], runs[1, b])


def place_rows(runs, rows, target, x):
    seqs, length, width = x.shape
    slots = target.shape[2]
    big = pl.BlockSpec((1, length, width), lambda b, *_: (b, 0, 0))
    return pl.pallas_call(
        out_kernel,
        grid_spec=pltpu.PrefetchScalarGridSpec(
            num_scalar_prefetch=1,
            grid=(seqs,),
            in_specs=[
                pl.BlockSpec((slots, width), lambda b, *_: (b, 0)),
                pl.BlockSpec((1, 1, slots), lambda b, *_: (b, 0, 0)),
                big,
            ],
            out_specs=big,
        ),
        out_shape=jax.ShapeDtypeStruct(x.shape, BF16),
        compiler_params=params("arbitrary"),
        cost_estimate=cost(2 * seqs * slots * length * width, 4 * seqs * length * width),
        name="place_rows",
    )(runs, rows, target, x)


def input_kernel(
    perm, runs, sel, grad, vec, stats, dmid, dqkv, target, x, in_own, in_oth, out, w_in, sem_in
):
    b = pl.program_id(0)
    half = in_own.shape[2]

    @pl.when(b == 0)
    def _():
        copies = load_rows(in_own, w_in, perm, 0, sem_in.at[0], pl.ds(0, half)) + load_rows(
            in_oth, w_in, perm, 0, sem_in.at[1], pl.ds(half, half)
        )
        for c in copies:
            c.start()
        for c in copies:
            c.wait()

    d_normed = dot(dqkv[...], w_in[...], 1, 1)
    d_sel = norm_pull(sel[...].astype(F32), stats[:, 0:1], vec[0:1, :] * d_normed) + dmid[...]
    rows = (grad[...].astype(F32) + d_sel).astype(BF16)
    out[0] = place(rows, target[0], x[0], runs[0, b], runs[1, b])


def input_rows(perm, runs, sel, grad, vec, stats, dmid, dqkv, target, x, in_own, in_oth):
    seqs, length, width = x.shape
    slots = target.shape[2]
    blocks = in_own.shape[0]
    row = lambda w: pl.BlockSpec((slots, w), lambda b, *_: (b, 0))
    big = pl.BlockSpec((1, length, width), lambda b, *_: (b, 0, 0))
    return pl.pallas_call(
        input_kernel,
        grid_spec=pltpu.PrefetchScalarGridSpec(
            num_scalar_prefetch=2,
            grid=(seqs,),
            in_specs=[
                row(width), row(width), whole(vec.shape), row(128), row(width), row(3 * width),
                pl.BlockSpec((1, 1, slots), lambda b, *_: (b, 0, 0)),
                big, ANY, ANY,
            ],
            out_specs=big,
            scratch_shapes=[
                pltpu.VMEM((width, 3 * width), BF16),
                pltpu.SemaphoreType.DMA((2, blocks)),
            ],
        ),
        out_shape=jax.ShapeDtypeStruct(x.shape, BF16),
        compiler_params=params("arbitrary"),
        cost_estimate=cost(8 * seqs * slots * length * width, 4 * seqs * length * width),
        name="input_rows",
    )(perm, runs, sel, grad, vec, stats, dmid, dqkv, target, x, in_own, in_oth)


class Hops:
    def __init__(self, wide, narrow):
        self.size = {"wide": wide, "narrow": narrow}
        self.chips = wide * narrow // 2
        self.across = [("narrow", 1 << k) for k in range(1, narrow.bit_length() - 1)]
        self.along = [("wide", 1 << k) for k in range(wide.bit_length() - 1)]

    def chip_mask(self, hop):
        axis, mask = hop
        return mask // 2 if axis == "narrow" else mask * (self.size["narrow"] // 2)

    def swap(self, value, hop):
        axis, mask = hop
        return lax.ppermute(value, axis, [(i, i ^ mask) for i in range(self.size[axis])])

    def gather(self, block, order):
        held = block[None]
        for hop in order:
            held = jnp.concatenate([held, self.swap(held, hop)], axis=0)
        return held

    def reduce(self, held, order):
        for k, hop in enumerate(order):
            half = held.shape[0] // 2
            got = self.swap(held[half:], hop)
            total = held[:half].astype(F32) + got.astype(F32)
            held = total if k == len(order) - 1 else total.astype(BF16)
        return held[0]

    def masks(self, order):
        found = [0]
        for hop in order:
            found = found + [m ^ self.chip_mask(hop) for m in found]
        return found


CORE = ("narrow", 1)


def per_device(
    layer_in,
    lengths,
    padding,
    picked,
    first_gain,
    project_in,
    project_out,
    second_gain,
    up_weight,
    up_bias,
    down_weight,
    down_bias,
    router,
    cotangent,
    *,
    wide,
    narrow,
):
    seqs, slots = picked.shape
    length = layer_in.shape[1]
    shard, in_width = project_in.shape
    width = in_width // 3
    hidden = up_weight.shape[1]
    devices = wide * narrow
    half = width // 2
    hidden_half = hidden // 2
    fast = (2 * shard) % 16 == 0 and all(n & (n - 1) == 0 for n in (wide, narrow))

    counts = lengths // 8
    valid = jnp.arange(slots)[None, :] < counts[:, None]
    target = jnp.where(valid, picked, -1)
    runs = jnp.stack([jnp.argmax(padding, axis=1).astype(jnp.int32), lengths])

    out_t = project_out.T
    down_t = down_weight.T
    extra = 128 * -(-(4 * shard) // 128)
    small = jnp.zeros((shard, extra), BF16)
    small = small.at[0, : 4 * shard].set(up_bias)
    small = small.at[1, : 4 * shard].set(
        jnp.concatenate([first_gain, second_gain, down_bias, router])
    )
    in_split = project_in.reshape(shard, 3, 2, half)

    def half_of(side):
        return (
            in_split[:, :, side].reshape(shard, 3 * half),
            jnp.concatenate([out_t[:, side * half : (side + 1) * half], small], axis=1),
            up_weight[:, side * hidden_half : (side + 1) * hidden_half],
            down_t[:, side * hidden_half : (side + 1) * hidden_half],
        )

    if fast:
        hops = Hops(wide, narrow)
        core = lax.axis_index("narrow") & 1
        chip = lax.axis_index("wide") * (narrow // 2) + (lax.axis_index("narrow") >> 1)
        zero_side = core == 0
        nx, nw = hops.across, hops.along
        ny = nw[: max(1, len(nw) // 2)] if len(nw) > 1 else nw
        nz = [h for h in nw if h not in ny]
        far = nz[::-1]
        gathers = (
            far + ny + nx,
            far + nx + ny,
            far + nx + ny,
            far[:1] + nx + ny + far[1:],
        )
        sums = (nx + ny + nz, ny + nx + nz, nz[:1] + ny + nx + nz[1:])
        perm = chip ^ jnp.array([hops.masks(o) for o in gathers], jnp.int32)
        back = jnp.array([hops.masks(o[::-1]) for o in sums], jnp.int32)
        where = chip ^ back
        inverse = jnp.argsort(where, axis=1).astype(jnp.int32)

        def pick(pair):
            return jnp.where(zero_side, pair[0], pair[1]), jnp.where(zero_side, pair[1], pair[0])

        packed = [jnp.concatenate(half_of(side), axis=1) for side in (0, 1)]
        mine, theirs = pick(packed)
        got = hops.swap(theirs, CORE)
        chip_rows = jnp.where(
            zero_side, jnp.concatenate([mine, got], 0), jnp.concatenate([got, mine], 0)
        )
        own, oth = [], []
        start = 0
        for order, piece in zip(gathers, half_of(0)):
            held = hops.gather(chip_rows[:, start : start + piece.shape[1]], order)
            start += piece.shape[1]
            own.append(held)
        small_rows = own[1][:, :, half:]
        own[1] = own[1][:, :, :half]
        oth = [hops.swap(held, CORE) for held in own]
        small_all = jnp.take(small_rows, jnp.argsort(perm[1]), axis=0)
        small_all = small_all.reshape(devices, shard, extra)
    else:
        zero_side = True
        perm = jnp.zeros((4, 1), jnp.int32)
        inverse = jnp.zeros((3, 1), jnp.int32)
        pieces = [half_of(0), half_of(1)]
        sizes = [p.shape[1] for p in pieces[0]]
        packed = jnp.concatenate(pieces[0] + pieces[1], axis=1)
        full = lax.all_gather(packed, AXES, axis=0, tiled=True)
        cuts = [0]
        for n in sizes * 2:
            cuts.append(cuts[-1] + n)
        parts = [full[None, :, a:b] for a, b in zip(cuts, cuts[1:])]
        own, oth = parts[:4], parts[4:]
        small_all = own[1][0, :, half:].reshape(devices, shard, extra)
        own[1] = own[1][:, :, :half]
        oth[1] = oth[1][:, :, :half]

    biases = small_all[:, 0, : 4 * shard].reshape(2, 1, hidden_half).astype(F32)
    vec = small_all[:, 1, : 4 * shard].reshape(devices, 4, shard).transpose(1, 0, 2)
    vec = vec.reshape(4, width).astype(F32)
    vec = jnp.concatenate([vec, jnp.zeros_like(vec)], axis=0)
    if fast:
        bias_own, bias_oth = pick(biases)
    else:
        bias_own, bias_oth = biases[0], biases[1]

    sel, slot_grad = gather_rows(target[:, :, None], layer_in, cotangent)
    qkv, att, mid, n2, n2t, g, gt, n1t, stats = forward_block(
        perm, inverse, counts, sel, slot_grad, vec, own[0], oth[0], own[1], oth[1]
    )
    mlp, dn2, dup_oth, ddown_oth, dbias_oth = mlp_half(
        perm, n2, n2t, g, gt, oth[2], oth[3], bias_oth
    )
    mlp, dn2, dup_own, ddown_own, dbias_own = mlp_half(
        perm, n2, n2t, g, gt, own[2], own[3], bias_own, (mlp, dn2)
    )
    dqkv, dattnt, dmid, new_rows, drouter = backward_block(
        perm, inverse, counts, sel, slot_grad, vec, qkv, mid, stats, mlp, dn2, own[1], oth[1]
    )
    target_row = target[:, None, :]
    layer_out = place_rows(runs, new_rows, target_row, layer_in)

    ddown_bias = jnp.sum(g.astype(F32), axis=0)
    if fast:
        dbias = jnp.concatenate(
            [
                jnp.where(zero_side, dbias_own, dbias_oth),
                jnp.where(zero_side, dbias_oth, dbias_own),
            ],
            axis=1,
        )
    else:
        dbias = jnp.concatenate([dbias_own, dbias_oth], axis=1)
    line_one = dbias.reshape(devices, 1, 4 * shard)
    line_two = jnp.concatenate(
        [ddown_bias.reshape(devices, 1, shard), drouter.reshape(devices, 1, shard)], axis=2
    )
    lines = jnp.concatenate(
        [
            jnp.pad(line_one, ((0, 0), (0, 0), (0, extra - 4 * shard))),
            jnp.pad(line_two, ((0, 0), (0, 0), (0, extra - 2 * shard))),
        ],
        axis=1,
    ).astype(BF16)
    lines = jnp.pad(lines, ((0, 0), (0, shard - 2), (0, 0)))

    if fast:
        lines = jnp.take(lines.reshape(hops.chips, 2 * shard, extra), where[2], axis=0)
    lines = lines.reshape(width, extra)
    proj_oth = project_grads(n1t, dattnt, dqkv, att, lines, 1)
    proj_own = project_grads(n1t, dattnt, dqkv, att, lines, 0)
    input_grad = input_rows(
        perm, runs, sel, slot_grad, vec, stats, dmid, dqkv, target_row, cotangent, own[0], oth[0]
    )

    if fast:
        results = []
        for order, mine, theirs in (
            (sums[0], dup_own, dup_oth),
            (sums[1], ddown_own, ddown_oth),
            (sums[2], proj_own, proj_oth),
        ):
            got = hops.swap(theirs, CORE)
            both = (mine.astype(F32) + got.astype(F32)).astype(BF16)
            both = both.reshape(hops.chips, 2 * shard, both.shape[1])
            results.append(hops.reduce(both, order))

        def finish(rows):
            top, bottom = rows[:shard], rows[shard:]
            keep = jnp.where(zero_side, top, bottom)
            got = hops.swap(jnp.where(zero_side, bottom, top), CORE)
            return jnp.where(zero_side, keep, got), jnp.where(zero_side, got, keep), keep

        up_a, up_b, _ = finish(results[0])
        down_a, down_b, _ = finish(results[1])
        proj_a, proj_b, keep = finish(results[2])
        lines = keep[:, 4 * half :]
    else:
        flat = jnp.concatenate(
            [dup_own, dup_oth, ddown_own, ddown_oth, proj_own, proj_oth], axis=1
        )
        total = lax.psum_scatter(flat.astype(F32), AXES, scatter_dimension=0, tiled=True)
        h = hidden_half
        up_a, up_b, down_a, down_b = (total[:, k * h : (k + 1) * h] for k in range(4))
        p = proj_own.shape[1]
        proj_a, proj_b = total[:, 4 * h : 4 * h + p], total[:, 4 * h + p :]
        lines = proj_a[:, 4 * half :]

    up_grad = jnp.concatenate([up_a, up_b], axis=1)
    down_grad = jnp.concatenate([down_a, down_b], axis=1).T
    in_grad = jnp.stack(
        [proj_a[:, : 3 * half].reshape(shard, 3, half), proj_b[:, : 3 * half].reshape(shard, 3, half)],
        axis=2,
    ).reshape(shard, in_width)
    out_grad = jnp.concatenate(
        [proj_a[:, 3 * half : 4 * half], proj_b[:, 3 * half : 4 * half]], axis=1
    ).T
    gain_one = jnp.sum(project_in.astype(F32) * in_grad, axis=1) / first_gain.astype(F32)
    gain_two = jnp.sum(up_weight.astype(F32) * up_grad, axis=1) / second_gain.astype(F32)
    return (
        layer_out,
        input_grad,
        gain_one,
        in_grad,
        out_grad,
        gain_two,
        up_grad,
        lines[0, : 4 * shard],
        down_grad,
        lines[1, :shard],
        lines[1, shard : 2 * shard],
    )


def solution(mesh):
    both = ("wide", "narrow")
    rows3, rows2, rows1, cols = P(both, None, None), P(both, None), P(both), P(None, both)
    in_specs = (
        rows3, rows1, rows2, rows2, rows1, rows2, cols, rows1, rows2, rows1, cols, rows1, rows1, rows3,
    )
    out_specs = (rows3, rows3, rows1, rows2, cols, rows1, rows2, rows1, cols, rows1, rows1)
    return jax.shard_map(
        partial(per_device, wide=mesh.shape["wide"], narrow=mesh.shape["narrow"]),
        mesh=mesh,
        in_specs=in_specs,
        out_specs=out_specs,
        check_vma=False,
    )
```

```python
from functools import partial

import jax
import jax.numpy as jnp
import numpy as np
from jax import lax
from jax.experimental import pallas as pl
from jax.experimental.pallas import tpu as pltpu
from jax.sharding import PartitionSpec as P

HEAD_DIM = 64
EPSILON = 1e-06
NEG_FILL = -1e30
F32 = jnp.float32
BF16 = jnp.bfloat16
AXES = ("wide", "narrow")
SCALE = HEAD_DIM**-0.5
GELU_A = 0.7978845608028654
GELU_B = 0.044715
LSE_LANE = 16
ANY = pl.BlockSpec(memory_space=pl.ANY)
VMEM_LIMIT = 62 * 1024 * 1024


def dot(left, right, left_dim=1, right_dim=0):
    return lax.dot_general(
        left, right, (((left_dim,), (right_dim,)), ((), ())), preferred_element_type=F32
    )


def params(*semantics):
    return pltpu.CompilerParams(
        dimension_semantics=semantics or None, vmem_limit_bytes=VMEM_LIMIT
    )


def whole(shape):
    return pl.BlockSpec(shape, lambda *_: (0,) * len(shape))


def cost(flops, bytes_accessed):
    return pl.CostEstimate(
        flops=int(flops), bytes_accessed=int(bytes_accessed), transcendentals=0
    )


def load_rows(blocks, target, order, sems, source, columns):
    height = blocks.shape[1]
    return [
        pltpu.make_async_copy(
            blocks.at[j, :, source],
            target.at[pl.ds(place * height, height), columns],
            sems.at[j],
        )
        for j, place in enumerate(order)
    ]


def store_rows(target, value, order):
    height = value.shape[0] // len(order)
    for j, place in enumerate(order):
        target[j * height : (j + 1) * height, :] = value[place * height : (place + 1) * height, :]


def gather_kernel(target, x, cot, sel, grad):
    length = x.shape[1]
    places = lax.broadcasted_iota(jnp.int32, (target.shape[1], length), 1)
    chosen = jnp.where(target[0] == places, 1.0, 0.0).astype(BF16)
    sel[...] = dot(chosen, x[0]).astype(BF16)
    grad[...] = dot(chosen, cot[0]).astype(BF16)


def gather_rows(target, layer_in, cotangent):
    seqs, length, width = layer_in.shape
    slots = target.shape[1]
    big = pl.BlockSpec((1, length, width), lambda b: (b, 0, 0))
    out = pl.BlockSpec((slots, width), lambda b: (b, 0))
    return pl.pallas_call(
        gather_kernel,
        grid=(seqs,),
        in_specs=[pl.BlockSpec((1, slots, 1), lambda b: (b, 0, 0)), big, big],
        out_specs=[out, out],
        out_shape=[jax.ShapeDtypeStruct((seqs * slots, width), BF16)] * 2,
        compiler_params=params("arbitrary"),
        cost_estimate=cost(
            4 * seqs * slots * length * width, 4 * seqs * length * width
        ),
        name="gather_rows",
    )(target, layer_in, cotangent)


def allowed_keys(slots, valid):
    rows = lax.broadcasted_iota(jnp.int32, (2 * slots, slots), 0)
    rows = jnp.where(rows >= slots, rows - slots, rows)
    keys = lax.broadcasted_iota(jnp.int32, (2 * slots, slots), 1)
    return (keys <= rows) & (keys < valid)


def split_pair(pair):
    lane = lax.broadcasted_iota(jnp.int32, pair.shape, 1)
    zero = jnp.zeros_like(pair)
    first = lane < HEAD_DIM
    return jnp.concatenate(
        [jnp.where(first, pair, zero), jnp.where(first, zero, pair)], axis=0
    )


def join_pair(stacked):
    half = stacked.shape[0] // 2
    lane = lax.broadcasted_iota(jnp.int32, (half, stacked.shape[1]), 1)
    return jnp.where(lane < HEAD_DIM, stacked[:half], stacked[half:])


def pair_columns(pair, half_width):
    per_half = half_width // (2 * HEAD_DIM)
    side, place = divmod(pair, per_half)
    base = side * 3 * half_width + place * 2 * HEAD_DIM
    return tuple(slice(base + k * half_width, base + k * half_width + 2 * HEAD_DIM) for k in range(3))


def forward_kernel(
    counts,
    sel, grad, ext, in_own, in_oth, out_own, out_oth,
    qkv, att, mid, n2, n2t, g, gt, n1t, stats, vec, bias, gsum,
    w_in, w_out, sem_in, sem_out,
    *, order, half, third,
):
    b = pl.program_id(0)
    slots, width = sel.shape

    def in_copies():
        here = pl.ds(0, half)
        return load_rows(in_own, w_in, order, sem_in.at[0], here, here) + load_rows(
            in_oth, w_in, order, sem_in.at[1], here, pl.ds(half, half)
        )

    def out_copies():
        here = pl.ds(0, third)
        return load_rows(out_own, w_out, order, sem_out.at[0], here, here) + load_rows(
            out_oth, w_out, order, sem_out.at[1], here, pl.ds(third, third)
        )

    @pl.when(b == 0)
    def _():
        first = in_copies()
        for c in first + out_copies():
            c.start()
        per = width // 128
        vec[...] = jnp.zeros_like(vec)
        for v in range(4):
            for k in range(per):
                vec[v : v + 1, k * 128 : (k + 1) * 128] = ext[0, v * per + k : v * per + k + 1, :]
        for k in range(bias.shape[1] // 128):
            bias[0:1, k * 128 : (k + 1) * 128] = ext[1, k : k + 1, :]
        for c in first:
            c.wait()

    x = sel[...].astype(F32)
    r1 = lax.rsqrt(jnp.mean(x * x, axis=-1, keepdims=True) + EPSILON)
    n1 = (x * r1 * vec[0:1, :]).astype(BF16)
    logit = jnp.sum(x * vec[3:4, :], axis=-1, keepdims=True)
    rate = jax.nn.sigmoid(logit)
    d_mlp = (rate * grad[...].astype(F32)).astype(BF16)
    g[...] = d_mlp
    gsum_now = jnp.sum(d_mlp.astype(F32), axis=0, keepdims=True)

    @pl.when(b == 0)
    def _():
        gsum[...] = gsum_now

    @pl.when(b > 0)
    def _():
        gsum[...] += gsum_now

    store_rows(gt, d_mlp.T, order)
    store_rows(n1t, n1.T, order)
    qkv[...] = dot(n1, w_in[...]).astype(BF16)

    allowed = allowed_keys(slots, counts[b])
    lane = lax.broadcasted_iota(jnp.int32, (slots, 128), 1)
    kept = jnp.where(lane == 0, r1, jnp.where(lane == 1, rate, 0.0))
    for pair in range(width // (2 * HEAD_DIM)):
        qc, kc, vc = pair_columns(pair, width // 2)
        scores = dot(split_pair(qkv[:, qc] * SCALE), qkv[:, kc], 1, 1)
        scores = jnp.where(allowed, scores, NEG_FILL)
        top = jnp.max(scores, axis=-1, keepdims=True)
        exps = jnp.exp(scores - top)
        total = jnp.sum(exps, axis=-1, keepdims=True)
        lse = top + jnp.log(total)
        probs = (exps * (1.0 / total)).astype(BF16)
        att[:, pair * 128 : (pair + 1) * 128] = join_pair(dot(probs, qkv[:, vc])).astype(BF16)
        kept = jnp.where(lane == LSE_LANE + 2 * pair, lse[:slots], kept)
        kept = jnp.where(lane == LSE_LANE + 2 * pair + 1, lse[slots:], kept)

    @pl.when(b == 0)
    def _():
        for c in out_copies():
            c.wait()

    stream = x + dot(att[...], w_out[...], 1, 1)
    mid[...] = stream
    r2 = lax.rsqrt(jnp.mean(stream * stream, axis=-1, keepdims=True) + EPSILON)
    normed = (stream * r2 * vec[1:2, :]).astype(BF16)
    n2[...] = normed
    store_rows(n2t, normed.T, order)
    stats[...] = jnp.where(lane == 2, r2, kept)


def forward_block(order, hidden, counts, sel, grad, ext, in_own, in_oth, out_own, out_oth):
    rows, width = sel.shape
    seqs = counts.shape[0]
    slots = rows // seqs
    blocks = len(order)
    row = lambda w: pl.BlockSpec((slots, w), lambda b, *_: (b, 0))
    col = pl.BlockSpec((width, slots), lambda b, *_: (0, b))
    shape = jax.ShapeDtypeStruct
    return pl.pallas_call(
        partial(forward_kernel, order=order, half=3 * width // 2, third=width // 2),
        grid_spec=pltpu.PrefetchScalarGridSpec(
            num_scalar_prefetch=1,
            grid=(seqs,),
            in_specs=[row(width), row(width), whole(ext.shape), ANY, ANY, ANY, ANY],
            out_specs=[
                row(3 * width), row(width), row(width), row(width), col, row(width), col, col, row(128),
                whole((8, width)), whole((1, hidden)), whole((1, width)),
            ],
            scratch_shapes=[
                pltpu.VMEM((width, 3 * width), BF16),
                pltpu.VMEM((width, width), BF16),
                pltpu.SemaphoreType.DMA((2, blocks)),
                pltpu.SemaphoreType.DMA((2, blocks)),
            ],
        ),
        out_shape=[
            shape((rows, 3 * width), BF16),
            shape((rows, width), BF16),
            shape((rows, width), F32),
            shape((rows, width), BF16),
            shape((width, rows), BF16),
            shape((rows, width), BF16),
            shape((width, rows), BF16),
            shape((width, rows), BF16),
            shape((rows, 128), F32),
            shape((8, width), F32),
            shape((1, hidden), F32),
            shape((1, width), F32),
        ],
        compiler_params=params("arbitrary"),
        cost_estimate=cost(10 * rows * width * width, 30 * rows * width),
        name="forward_block",
    )(counts, sel, grad, ext, in_own, in_oth, out_own, out_oth)


def mlp_kernel(core, n2, n2t, g, gt, own, oth, bias, *rest, order, carried, tile, start):
    if carried:
        mlp_in, dn2_in, *rest = rest
    mlp, dn2, d_own, d_oth, dbias, w_up, w_down, sems = rest
    i = pl.program_id(0)

    def copies(side):
        source = (own, oth)[side]
        return load_rows(
            source, w_up.at[side], order, sems.at[side, 0], pl.ds(start, tile), pl.ds(0, tile)
        ) + load_rows(
            source, w_down.at[side], order, sems.at[side, 1], pl.ds(start + tile, tile), pl.ds(0, tile)
        )

    @pl.when(i == 0)
    def _():
        for c in copies(0) + copies(1):
            c.start()
        for c in copies(0):
            c.wait()

    @pl.when(i == 1)
    def _():
        for c in copies(1):
            c.wait()

    up_now = w_up[i]
    down_now = w_down[i]
    pre = dot(n2[...], up_now) + bias[...]
    square = pre * pre
    th = jnp.tanh(pre * (GELU_A + GELU_A * GELU_B * square))
    half = 0.5 * (1.0 + th)
    act = (pre * half).astype(BF16)
    slope = half + 0.5 * pre * (1.0 - th * th) * (GELU_A + 3 * GELU_A * GELU_B * square)
    d_pre = (slope * dot(g[...], down_now)).astype(BF16)
    dbias[...] = jnp.sum(d_pre.astype(F32), axis=0, keepdims=True)
    mlp_now = dot(act, down_now, 1, 1)
    dn2_now = dot(d_pre, up_now, 1, 1)
    dup = dot(n2t[...], d_pre).astype(BF16)
    ddown = dot(gt[...], act).astype(BF16)

    @pl.when(i == 0)
    def _():
        if carried:
            mlp[...] = mlp_in[...] + mlp_now
            dn2[...] = dn2_in[...] + dn2_now
        else:
            mlp[...] = mlp_now
            dn2[...] = dn2_now
        d_own[:, :tile] = dup
        d_own[:, tile:] = ddown

    @pl.when(i > 0)
    def _():
        mlp[...] += mlp_now
        dn2[...] += dn2_now
        d_oth[:, :tile] = dup
        d_oth[:, tile:] = ddown


def mlp_part(order, core, part, tile, start, n2, n2t, g, gt, own, oth, bias, carry=()):
    rows, width = n2.shape
    parts = bias.shape[1] // (2 * tile)
    once = lambda s: pl.BlockSpec(s, lambda *_: (0, 0), pipeline_mode=pl.Buffered(1))
    shape = jax.ShapeDtypeStruct
    return pl.pallas_call(
        partial(mlp_kernel, order=order, carried=bool(carry), tile=tile, start=start),
        grid_spec=pltpu.PrefetchScalarGridSpec(
            num_scalar_prefetch=1,
            grid=(2,),
            in_specs=[
                once((rows, width)), once((width, rows)), once((rows, width)), once((width, rows)),
                ANY, ANY,
                pl.BlockSpec((1, tile), lambda i, core: (0, (core[0] ^ i) * parts + part)),
            ] + [once((rows, width))] * len(carry),
            out_specs=[
                whole((rows, width)), whole((rows, width)),
                whole((width, 2 * tile)), whole((width, 2 * tile)),
                pl.BlockSpec((1, tile), lambda i, core: (0, i)),
            ],
            scratch_shapes=[
                pltpu.VMEM((2, width, tile), BF16),
                pltpu.VMEM((2, width, tile), BF16),
                pltpu.SemaphoreType.DMA((2, 2, len(order))),
            ],
        ),
        out_shape=[
            shape((rows, width), F32),
            shape((rows, width), F32),
            shape((width, 2 * tile), BF16),
            shape((width, 2 * tile), BF16),
            shape((1, 2 * tile), F32),
        ],
        compiler_params=params("arbitrary"),
        cost_estimate=cost(24 * rows * width * tile, 8 * rows * width),
        name="mlp_part",
    )(core, n2, n2t, g, gt, own, oth, bias, *carry)


def norm_pull(values, inverse, scaled):
    return inverse * scaled - values * (
        inverse * inverse * inverse * jnp.mean(scaled * values, axis=-1, keepdims=True)
    )


def backward_kernel(
    counts,
    sel, grad, vec, qkv, mid, stats, mlp, dn2, out_own, out_oth,
    dqkv, dattnt, dmid, new_rows, drouter,
    w_out, sem_out,
    *, order, third,
):
    b = pl.program_id(0)
    slots, width = sel.shape

    @pl.when(b == 0)
    def _():
        here = pl.ds(0, third)
        copies = load_rows(out_own, w_out, order, sem_out.at[0], here, here) + load_rows(
            out_oth, w_out, order, sem_out.at[1], here, pl.ds(third, third)
        )
        for c in copies:
            c.start()
        for c in copies:
            c.wait()

    x = sel[...].astype(F32)
    stream = mid[...]
    rate = stats[:, 1:2]
    r2 = stats[:, 2:3]
    slot_grad = grad[...].astype(F32)
    branch = (stream - x) + (mlp[...] + vec[2:3, :])
    new_rows[...] = (x + rate * branch).astype(BF16)
    d_logit = jnp.sum(slot_grad * branch, axis=-1, keepdims=True) * (rate * (1.0 - rate))
    router_now = jnp.sum(d_logit * x, axis=0, keepdims=True)

    @pl.when(b == 0)
    def _():
        drouter[...] = router_now

    @pl.when(b > 0)
    def _():
        drouter[...] += router_now

    d_mid = norm_pull(stream, r2, vec[1:2, :] * dn2[...])
    dmid[...] = d_mid + d_logit * vec[3:4, :]
    d_attn = (rate * slot_grad + d_mid).astype(BF16)
    store_rows(dattnt, d_attn.T, order)
    d_att = dot(d_attn, w_out[...]).astype(BF16)

    allowed = allowed_keys(slots, counts[b])
    for pair in range(width // (2 * HEAD_DIM)):
        qc, kc, vc = pair_columns(pair, width // 2)
        queries = split_pair(qkv[:, qc] * SCALE)
        keys = qkv[:, kc]
        lse = jnp.concatenate(
            [
                stats[:, LSE_LANE + 2 * pair : LSE_LANE + 2 * pair + 1],
                stats[:, LSE_LANE + 2 * pair + 1 : LSE_LANE + 2 * pair + 2],
            ],
            axis=0,
        )
        upstream = split_pair(d_att[:, pair * 128 : (pair + 1) * 128])
        scores = dot(queries, keys, 1, 1)
        probs = jnp.exp(jnp.where(allowed, scores - lse, NEG_FILL))
        d_probs = dot(upstream, qkv[:, vc], 1, 1)
        d_scores = (probs * (d_probs - jnp.sum(probs * d_probs, axis=-1, keepdims=True))).astype(BF16)
        dqkv[:, qc] = (join_pair(dot(d_scores, keys)) * SCALE).astype(BF16)
        dqkv[:, kc] = dot(d_scores, queries, 0, 0).astype(BF16)
        dqkv[:, vc] = dot(probs.astype(BF16), upstream, 0, 0).astype(BF16)


def backward_block(order, counts, sel, grad, vec, qkv, mid, stats, mlp, dn2, out_own, out_oth):
    rows, width = sel.shape
    seqs = counts.shape[0]
    slots = rows // seqs
    blocks = len(order)
    row = lambda w: pl.BlockSpec((slots, w), lambda b, *_: (b, 0))
    col = pl.BlockSpec((width, slots), lambda b, *_: (0, b))
    shape = jax.ShapeDtypeStruct
    return pl.pallas_call(
        partial(backward_kernel, order=order, third=width // 2),
        grid_spec=pltpu.PrefetchScalarGridSpec(
            num_scalar_prefetch=1,
            grid=(seqs,),
            in_specs=[
                row(width), row(width), whole(vec.shape), row(3 * width), row(width), row(128),
                row(width), row(width), ANY, ANY,
            ],
            out_specs=[row(3 * width), col, row(width), row(width), whole((1, width))],
            scratch_shapes=[
                pltpu.VMEM((width, width), BF16),
                pltpu.SemaphoreType.DMA((2, blocks)),
            ],
        ),
        out_shape=[
            shape((rows, 3 * width), BF16),
            shape((width, rows), BF16),
            shape((rows, width), F32),
            shape((rows, width), BF16),
            shape((1, width), F32),
        ],
        compiler_params=params("arbitrary"),
        cost_estimate=cost(20 * rows * width * width, 30 * rows * width),
        name="backward_block",
    )(counts, sel, grad, vec, qkv, mid, stats, mlp, dn2, out_own, out_oth)


def project_kernel(n1t, dattnt, dqkv, att, small, out):
    half = dqkv.shape[1]
    third = att.shape[1]
    out[:, :half] = dot(n1t[...], dqkv[...]).astype(BF16)
    out[:, half : half + third] = dot(dattnt[...], att[...]).astype(BF16)
    out[:, half + third :] = small[...]


def project_grads(n1t, dattnt, dqkv, att, small, side):
    width, rows = n1t.shape
    half, third, extra = dqkv.shape[1] // 2, att.shape[1] // 2, small.shape[1]
    total = half + third + extra
    return pl.pallas_call(
        project_kernel,
        grid=(1,),
        in_specs=[
            whole((width, rows)), whole((width, rows)),
            pl.BlockSpec((rows, half), lambda i: (0, side)),
            pl.BlockSpec((rows, third), lambda i: (0, side)),
            whole((width, extra)),
        ],
        out_specs=whole((width, total)),
        out_shape=jax.ShapeDtypeStruct((width, total), BF16),
        compiler_params=params("arbitrary"),
        cost_estimate=cost(2 * width * rows * total, 2 * (2 * width * rows + rows * total + width * total)),
        name="project_grads",
    )(n1t, dattnt, dqkv, att, small)


def place(rows, target, x, start, count):
    length = x.shape[0]
    places = lax.broadcasted_iota(jnp.int32, (length, target.shape[1]), 0)
    hits = target == places
    moved = dot(jnp.where(hits, 1.0, 0.0).astype(BF16), rows)
    hit = jnp.max(jnp.where(hits, 1.0, 0.0), axis=-1, keepdims=True)
    at = lax.broadcasted_iota(jnp.int32, (length, 1), 0)
    kept = (at >= start) & (at < start + count) & (hit < 0.5)
    return jnp.where(kept, x.astype(F32), moved).astype(BF16)


def out_kernel(runs, rows, target, x, out):
    b = pl.program_id(0)
    out[0] = place(rows[...], target[0], x[0], runs[0, b], runs[1, b])


def place_rows(runs, rows, target, x):
    seqs, length, width = x.shape
    slots = target.shape[2]
    big = pl.BlockSpec((1, length, width), lambda b, *_: (b, 0, 0))
    return pl.pallas_call(
        out_kernel,
        grid_spec=pltpu.PrefetchScalarGridSpec(
            num_scalar_prefetch=1,
            grid=(seqs,),
            in_specs=[
                pl.BlockSpec((slots, width), lambda b, *_: (b, 0)),
                pl.BlockSpec((1, 1, slots), lambda b, *_: (b, 0, 0)),
                big,
            ],
            out_specs=big,
        ),
        out_shape=jax.ShapeDtypeStruct(x.shape, BF16),
        compiler_params=params("arbitrary"),
        cost_estimate=cost(2 * seqs * slots * length * width, 4 * seqs * length * width),
        name="place_rows",
    )(runs, rows, target, x)


def input_kernel(
    runs, sel, grad, vec, stats, dmid, dqkv, target, x, in_own, in_oth, out, w_in, sem_in, *, order
):
    b = pl.program_id(0)
    half = w_in.shape[1] // 2

    @pl.when(b == 0)
    def _():
        here = pl.ds(0, half)
        copies = load_rows(in_own, w_in, order, sem_in.at[0], here, here) + load_rows(
            in_oth, w_in, order, sem_in.at[1], here, pl.ds(half, half)
        )
        for c in copies:
            c.start()
        for c in copies:
            c.wait()

    d_normed = dot(dqkv[...], w_in[...], 1, 1)
    d_sel = norm_pull(sel[...].astype(F32), stats[:, 0:1], vec[0:1, :] * d_normed) + dmid[...]
    rows = (grad[...].astype(F32) + d_sel).astype(BF16)
    out[0] = place(rows, target[0], x[0], runs[0, b], runs[1, b])


def input_rows(order, runs, sel, grad, vec, stats, dmid, dqkv, target, x, in_own, in_oth):
    seqs, length, width = x.shape
    slots = target.shape[2]
    blocks = len(order)
    row = lambda w: pl.BlockSpec((slots, w), lambda b, *_: (b, 0))
    big = pl.BlockSpec((1, length, width), lambda b, *_: (b, 0, 0))
    return pl.pallas_call(
        partial(input_kernel, order=order),
        grid_spec=pltpu.PrefetchScalarGridSpec(
            num_scalar_prefetch=1,
            grid=(seqs,),
            in_specs=[
                row(width), row(width), whole(vec.shape), row(128), row(width), row(3 * width),
                pl.BlockSpec((1, 1, slots), lambda b, *_: (b, 0, 0)),
                big, ANY, ANY,
            ],
            out_specs=big,
            scratch_shapes=[
                pltpu.VMEM((width, 3 * width), BF16),
                pltpu.SemaphoreType.DMA((2, blocks)),
            ],
        ),
        out_shape=jax.ShapeDtypeStruct(x.shape, BF16),
        compiler_params=params("arbitrary"),
        cost_estimate=cost(8 * seqs * slots * length * width, 4 * seqs * length * width),
        name="input_rows",
    )(runs, sel, grad, vec, stats, dmid, dqkv, target, x, in_own, in_oth)


class Paths:
    def __init__(self, wide, narrow):
        self.depth, self.rows, self.across = wide // 2, 2, narrow // 2
        ids = np.arange(wide * narrow).reshape(self.depth, self.rows, self.across, 2)
        self.plane = self.rows * self.across
        self.line_groups = ids.transpose(1, 2, 0, 3).reshape(self.plane, -1).tolist()
        self.plane_groups = ids.transpose(0, 3, 1, 2).reshape(-1, self.plane).tolist()
        chips = np.arange(wide * narrow // 2).reshape(self.depth, self.plane)
        self.order = tuple(int(c) for c in chips.T.reshape(-1))
        self.pairs = [(i, i ^ 1) for i in range(narrow)]

    def swap(self, value):
        return lax.ppermute(value, "narrow", self.pairs)

    def along(self, value):
        return lax.all_to_all(value, AXES, 0, 0, axis_index_groups=self.line_groups, tiled=True)

    def over(self, value):
        return lax.all_to_all(value, AXES, 0, 0, axis_index_groups=self.plane_groups, tiled=True)

    def gather_line(self, halves):
        shard, cols = halves[0].shape
        sent = jnp.broadcast_to(jnp.stack(halves)[None], (self.depth, 2, shard, cols))
        return self.along(sent.reshape(self.depth * 2 * shard, cols))

    def gather_plane(self, held):
        rows, cols = held.shape
        sent = jnp.broadcast_to(held[None], (self.plane, rows, cols))
        got = self.over(sent.reshape(self.plane * rows, cols))
        return got.reshape(len(self.order), -1, cols)

    def reduce_plane(self, own, oth):
        both = (own.astype(F32) + self.swap(oth).astype(F32)).astype(BF16)
        got = self.over(both)
        return jnp.sum(got.reshape(self.plane, -1, got.shape[1]).astype(F32), axis=0).astype(BF16)

    def reduce_line(self, held):
        got = self.along(held)
        return jnp.sum(got.reshape(self.depth, 2, -1, got.shape[1]).astype(F32), axis=0)


def per_device(
    layer_in,
    lengths,
    padding,
    picked,
    first_gain,
    project_in,
    project_out,
    second_gain,
    up_weight,
    up_bias,
    down_weight,
    down_bias,
    router,
    cotangent,
    *,
    wide,
    narrow,
):
    seqs, slots = picked.shape
    shard, in_width = project_in.shape
    width = in_width // 3
    hidden = up_weight.shape[1]
    devices = wide * narrow
    half = 3 * width // 2
    third = width // 2
    tile = hidden // 4
    fast = shard * 128 == 4 * width == hidden and wide % 2 == 0 and narrow % 2 == 0
    core = lax.axis_index("narrow") & 1 if fast else jnp.int32(0)
    device = lax.axis_index("wide") * narrow + lax.axis_index("narrow")

    in_split = project_in.reshape(shard, 3, 2, third)
    in_halves = [in_split[:, :, side].reshape(shard, half) for side in (0, 1)]
    out_t = project_out.T
    down_t = down_weight.T
    vectors = jnp.stack([first_gain, second_gain, down_bias, router])

    def rest_of(side, part):
        at = (2 * side + part) * tile
        pieces = [up_weight[:, at : at + tile], down_t[:, at : at + tile]]
        if part == 0:
            pieces = [out_t[:, side * third : (side + 1) * third]] + pieces
        return jnp.concatenate(pieces, axis=1)

    cut = third + 2 * tile
    if fast:
        paths = Paths(wide, narrow)
        order = paths.order
        placed = lax.dynamic_update_slice(
            jnp.zeros((4, width), BF16), vectors, (0, device * shard)
        ).reshape(shard, 128)
        biases = lax.dynamic_update_slice(
            jnp.zeros((hidden,), BF16), up_bias, (device * 4 * shard,)
        ).reshape(shard, 128)
        first = [
            jnp.concatenate([in_halves[0], placed], axis=1),
            jnp.concatenate([in_halves[1], biases], axis=1),
        ]
        rest = [
            jnp.concatenate([rest_of(side, 0), rest_of(side, 1)], axis=1) for side in (0, 1)
        ]
        in_own = paths.gather_plane(paths.gather_line(first))
        held = paths.gather_line(rest)
        one_own = paths.gather_plane(held[:, :cut])
        two_own = paths.gather_plane(held[:, cut:])
        in_oth, one_oth, two_oth = (paths.swap(v) for v in (in_own, one_own, two_own))
        ext = jnp.stack(
            [
                jnp.sum(v[:, :, half:].reshape(devices, shard, 128).astype(F32), axis=0)
                for v in (in_own, in_oth)
            ]
        )
        ext = jnp.where(core == 0, ext, ext[::-1])
    else:
        order = (0,)
        packed = jnp.concatenate(
            in_halves + [rest_of(side, part) for part in (0, 1) for side in (0, 1)], axis=1
        )
        full = lax.all_gather(packed, AXES, axis=0, tiled=True)
        cuts = [0]
        for n in (half, half, cut, cut, 2 * tile, 2 * tile):
            cuts.append(cuts[-1] + n)
        in_own, in_oth, one_own, one_oth, two_own, two_oth = (
            full[None, :, a:b] for a, b in zip(cuts, cuts[1:])
        )
        every = lax.all_gather(vectors, AXES, axis=1, tiled=True).reshape(1, -1, 128)
        biases = lax.all_gather(up_bias, AXES, axis=0, tiled=True).reshape(1, -1, 128)
        ext = jnp.concatenate([every, biases], axis=0).astype(F32)

    counts = lengths // 8
    valid = jnp.arange(slots)[None, :] < counts[:, None]
    target = jnp.where(valid, picked, -1)
    runs = jnp.stack([jnp.argmax(padding, axis=1).astype(jnp.int32), lengths])
    which = jnp.reshape(core, (1,)).astype(jnp.int32)

    sel, slot_grad = gather_rows(target[:, :, None], layer_in, cotangent)
    qkv, att, mid, n2, n2t, g, gt, n1t, stats, vec, bias, ddown_bias = forward_block(
        order, hidden, counts, sel, slot_grad, ext, in_own, in_oth, one_own, one_oth
    )
    mlp, dn2, d_one_own, d_one_oth, dbias_one = mlp_part(
        order, which, 0, tile, third, n2, n2t, g, gt, one_own, one_oth, bias
    )
    mlp, dn2, d_two_own, d_two_oth, dbias_two = mlp_part(
        order, which, 1, tile, 0, n2, n2t, g, gt, two_own, two_oth, bias, (mlp, dn2)
    )
    dqkv, dattnt, dmid, new_rows, drouter = backward_block(
        order, counts, sel, slot_grad, vec, qkv, mid, stats, mlp, dn2, one_own, one_oth
    )
    target_row = target[:, None, :]
    layer_out = place_rows(runs, new_rows, target_row, layer_in)

    dbias = jnp.stack([dbias_one.reshape(2, tile), dbias_two.reshape(2, tile)], axis=1)
    dbias = jnp.where(core == 0, dbias, dbias[::-1])
    extra = 128 * -(-(4 * shard) // 128)
    line_one = dbias.reshape(devices, 1, 4 * shard)
    line_two = jnp.concatenate(
        [ddown_bias.reshape(devices, 1, shard), drouter.reshape(devices, 1, shard)], axis=2
    )
    lines = jnp.concatenate(
        [
            jnp.pad(line_one, ((0, 0), (0, 0), (0, extra - 4 * shard))),
            jnp.pad(line_two, ((0, 0), (0, 0), (0, extra - 2 * shard))),
        ],
        axis=1,
    ).astype(BF16)
    lines = jnp.pad(lines, ((0, 0), (0, shard - 2), (0, 0)))
    if fast:
        lines = lines.reshape(paths.depth, paths.plane, 2 * shard, extra).transpose(1, 0, 2, 3)
    lines = lines.reshape(width, extra)
    proj_oth = project_grads(n1t, dattnt, dqkv, att, lines, 1)
    proj_own = project_grads(n1t, dattnt, dqkv, att, lines, 0)
    input_grad = input_rows(
        order, runs, sel, slot_grad, vec, stats, dmid, dqkv, target_row, cotangent, in_own, in_oth
    )

    if fast:
        one = paths.reduce_plane(d_one_own, d_one_oth)
        two = paths.reduce_plane(d_two_own, d_two_oth)
        sums = paths.reduce_line(jnp.concatenate([one, two], axis=1))
        proj = paths.reduce_line(paths.reduce_plane(proj_own, proj_oth))
        one, two = sums[:, :, : 2 * tile], sums[:, :, 2 * tile :]
    else:
        flat = jnp.concatenate(
            [d_one_own, d_one_oth, d_two_own, d_two_oth, proj_own, proj_oth], axis=1
        )
        total = lax.psum_scatter(flat.astype(F32), AXES, scatter_dimension=0, tiled=True)
        p = proj_own.shape[1]
        one = total[:, : 4 * tile].reshape(shard, 2, 2 * tile).transpose(1, 0, 2)
        two = total[:, 4 * tile : 8 * tile].reshape(shard, 2, 2 * tile).transpose(1, 0, 2)
        proj = total[:, 8 * tile :].reshape(shard, 2, p).transpose(1, 0, 2)

    up_grad = jnp.concatenate(
        [v[side, :, :tile] for side in (0, 1) for v in (one, two)], axis=1
    )
    down_grad = jnp.concatenate(
        [v[side, :, tile:] for side in (0, 1) for v in (one, two)], axis=1
    ).T
    in_grad = jnp.stack(
        [proj[side, :, :half].reshape(shard, 3, third) for side in (0, 1)], axis=2
    ).reshape(shard, in_width)
    out_grad = jnp.concatenate([proj[side, :, half : half + third] for side in (0, 1)], axis=1).T
    lines = proj[0, :, half + third :]
    gain_one = jnp.sum(project_in.astype(F32) * in_grad, axis=1) / first_gain.astype(F32)
    gain_two = jnp.sum(up_weight.astype(F32) * up_grad, axis=1) / second_gain.astype(F32)
    return (
        layer_out,
        input_grad,
        gain_one,
        in_grad,
        out_grad,
        gain_two,
        up_grad,
        lines[0, : 4 * shard],
        down_grad,
        lines[1, :shard],
        lines[1, shard : 2 * shard],
    )


def solution(mesh):
    both = ("wide", "narrow")
    rows3, rows2, rows1, cols = P(both, None, None), P(both, None), P(both), P(None, both)
    in_specs = (
        rows3, rows1, rows2, rows2, rows1, rows2, cols, rows1, rows2, rows1, cols, rows1, rows1, rows3,
    )
    out_specs = (rows3, rows3, rows1, rows2, cols, rows1, rows2, rows1, cols, rows1, rows1)
    return jax.shard_map(
        partial(per_device, wide=mesh.shape["wide"], narrow=mesh.shape["narrow"]),
        mesh=mesh,
        in_specs=in_specs,
        out_specs=out_specs,
        check_vma=False,
    )
```

```python
from functools import partial

import jax
import jax.numpy as jnp
import numpy as np
from jax import lax
from jax.experimental import pallas as pl
from jax.experimental.pallas import tpu as pltpu
from jax.sharding import PartitionSpec as P

HEAD_DIM = 64
EPSILON = 1e-06
NEG_FILL = -1e30
F32 = jnp.float32
BF16 = jnp.bfloat16
AXES = ("wide", "narrow")
SCALE = HEAD_DIM**-0.5
GELU_A = 0.7978845608028654
GELU_B = 0.044715
LSE_LANE = 16
ANY = pl.BlockSpec(memory_space=pl.ANY)
VMEM_LIMIT = 62 * 1024 * 1024


def dot(left, right, left_dim=1, right_dim=0):
    return lax.dot_general(
        left, right, (((left_dim,), (right_dim,)), ((), ())), preferred_element_type=F32
    )


def params(*semantics):
    return pltpu.CompilerParams(
        dimension_semantics=semantics or None, vmem_limit_bytes=VMEM_LIMIT
    )


def whole(shape):
    return pl.BlockSpec(shape, lambda *_: (0,) * len(shape))


def cost(flops, bytes_accessed):
    return pl.CostEstimate(
        flops=int(flops) // 16, bytes_accessed=int(bytes_accessed) // 16, transcendentals=0
    )


class Layout:
    def __init__(self, height, plane, blocks):
        self.height, self.plane, self.blocks = height, plane, tuple(blocks)
        self.pieces = 1 + max(piece for piece, *_ in blocks)
        self.depth = len(blocks) // plane

    def natural(self, here, step, line):
        return pl.multiple_of((line * self.plane + (here ^ step)) * self.height, 8)


def load_rows(layout, here, pieces, target, sems, source, columns):
    height = layout.height
    return [
        pltpu.make_async_copy(
            pieces[piece].at[pl.ds(at * height, height), source],
            target.at[pl.ds(layout.natural(here, step, line), height), columns],
            sems.at[j],
        )
        for j, (piece, at, step, line) in enumerate(layout.blocks)
    ]


def both_halves(layout, here, own, oth, target, sems, start, count):
    source = pl.ds(start, count)
    return load_rows(layout, here, own, target, sems.at[0], source, pl.ds(0, count)) + load_rows(
        layout, here, oth, target, sems.at[1], source, pl.ds(count, count)
    )


def store_rows(layout, here, target, value):
    height = layout.height
    for line in range(layout.depth):
        for owner in range(layout.plane):
            start = pl.multiple_of(((owner ^ here) * layout.depth + line) * height, 8)
            c = line * layout.plane + owner
            target[pl.ds(start, height), :] = value[c * height : (c + 1) * height, :]


def gather_kernel(target, x, cot, sel, grad):
    length = x.shape[1]
    places = lax.broadcasted_iota(jnp.int32, (target.shape[1], length), 1)
    chosen = jnp.where(target[0] == places, 1.0, 0.0).astype(BF16)
    sel[...] = dot(chosen, x[0]).astype(BF16)
    grad[...] = dot(chosen, cot[0]).astype(BF16)


def gather_rows(target, layer_in, cotangent):
    seqs, length, width = layer_in.shape
    slots = target.shape[1]
    big = pl.BlockSpec((1, length, width), lambda b: (b, 0, 0))
    out = pl.BlockSpec((slots, width), lambda b: (b, 0))
    return pl.pallas_call(
        gather_kernel,
        grid=(seqs,),
        in_specs=[pl.BlockSpec((1, slots, 1), lambda b: (b, 0, 0)), big, big],
        out_specs=[out, out],
        out_shape=[jax.ShapeDtypeStruct((seqs * slots, width), BF16)] * 2,
        compiler_params=params("arbitrary"),
        cost_estimate=cost(
            4 * seqs * slots * length * width, 4 * seqs * length * width
        ),
        name="gather_rows",
    )(target, layer_in, cotangent)


def allowed_keys(slots, valid):
    rows = lax.broadcasted_iota(jnp.int32, (2 * slots, slots), 0)
    rows = jnp.where(rows >= slots, rows - slots, rows)
    keys = lax.broadcasted_iota(jnp.int32, (2 * slots, slots), 1)
    return (keys <= rows) & (keys < valid)


def split_pair(pair):
    lane = lax.broadcasted_iota(jnp.int32, pair.shape, 1)
    zero = jnp.zeros_like(pair)
    first = lane < HEAD_DIM
    return jnp.concatenate(
        [jnp.where(first, pair, zero), jnp.where(first, zero, pair)], axis=0
    )


def join_pair(stacked):
    half = stacked.shape[0] // 2
    lane = lax.broadcasted_iota(jnp.int32, (half, stacked.shape[1]), 1)
    return jnp.where(lane < HEAD_DIM, stacked[:half], stacked[half:])


def pair_columns(pair, half_width):
    per_half = half_width // (2 * HEAD_DIM)
    side, place = divmod(pair, per_half)
    base = side * 3 * half_width + place * 2 * HEAD_DIM
    return tuple(slice(base + k * half_width, base + k * half_width + 2 * HEAD_DIM) for k in range(3))


def forward_kernel(
    where, counts, sel, grad, *rest, layout, half, third
):
    own, oth = rest[: layout.pieces], rest[layout.pieces : 2 * layout.pieces]
    (
    qkv, att, mid, n2, n2t, g, gt, n1t, stats, vec, bias, gsum,
    w_in, w_out, w_ext, sem_in, sem_out, sem_ext,
    ) = rest[2 * layout.pieces :]
    b = pl.program_id(0)
    slots, width = sel.shape
    here = where[0]

    def in_copies():
        return both_halves(layout, here, own, oth, w_in, sem_in, 0, half)

    def out_copies():
        return both_halves(layout, here, own, oth, w_out, sem_out, half, third)

    @pl.when(b == 0)
    def _():
        small = both_halves(layout, here, own, oth, w_ext, sem_ext, half + third, 128)
        first = in_copies()
        for c in small + first + out_copies():
            c.start()
        for c in small:
            c.wait()
        per = width // 128
        high = 4 * per
        total = sum(w_ext[k * high : (k + 1) * high, :].astype(F32) for k in range(width // high))
        mine, others = total[:, :128], total[:, 128:]
        vectors = jnp.where(where[1] == 0, mine, others)
        biases = jnp.where(where[1] == 0, others, mine)
        vec[...] = jnp.zeros_like(vec)
        for v in range(4):
            for k in range(per):
                vec[v : v + 1, k * 128 : (k + 1) * 128] = vectors[v * per + k : v * per + k + 1, :]
        for k in range(bias.shape[1] // 128):
            bias[0:1, k * 128 : (k + 1) * 128] = biases[k : k + 1, :]
        for c in first:
            c.wait()

    x = sel[...].astype(F32)
    r1 = lax.rsqrt(jnp.mean(x * x, axis=-1, keepdims=True) + EPSILON)
    n1 = (x * r1 * vec[0:1, :]).astype(BF16)
    logit = jnp.sum(x * vec[3:4, :], axis=-1, keepdims=True)
    rate = jax.nn.sigmoid(logit)
    d_mlp = (rate * grad[...].astype(F32)).astype(BF16)
    g[...] = d_mlp
    gsum_now = jnp.sum(d_mlp.astype(F32), axis=0, keepdims=True)

    @pl.when(b == 0)
    def _():
        gsum[...] = gsum_now

    @pl.when(b > 0)
    def _():
        gsum[...] += gsum_now

    store_rows(layout, here, gt, d_mlp.T)
    store_rows(layout, here, n1t, n1.T)
    qkv[...] = dot(n1, w_in[...]).astype(BF16)

    allowed = allowed_keys(slots, counts[b])
    lane = lax.broadcasted_iota(jnp.int32, (slots, 128), 1)
    kept = jnp.where(lane == 0, r1, jnp.where(lane == 1, rate, 0.0))
    for pair in range(width // (2 * HEAD_DIM)):
        qc, kc, vc = pair_columns(pair, width // 2)
        scores = dot(split_pair(qkv[:, qc] * SCALE), qkv[:, kc], 1, 1)
        scores = jnp.where(allowed, scores, NEG_FILL)
        top = jnp.max(scores, axis=-1, keepdims=True)
        exps = jnp.exp(scores - top)
        total = jnp.sum(exps, axis=-1, keepdims=True)
        lse = top + jnp.log(total)
        probs = (exps * (1.0 / total)).astype(BF16)
        att[:, pair * 128 : (pair + 1) * 128] = join_pair(dot(probs, qkv[:, vc])).astype(BF16)
        kept = jnp.where(lane == LSE_LANE + 2 * pair, lse[:slots], kept)
        kept = jnp.where(lane == LSE_LANE + 2 * pair + 1, lse[slots:], kept)

    @pl.when(b == 0)
    def _():
        for c in out_copies():
            c.wait()

    stream = x + dot(att[...], w_out[...], 1, 1)
    mid[...] = stream
    r2 = lax.rsqrt(jnp.mean(stream * stream, axis=-1, keepdims=True) + EPSILON)
    normed = (stream * r2 * vec[1:2, :]).astype(BF16)
    n2[...] = normed
    store_rows(layout, here, n2t, normed.T)
    stats[...] = jnp.where(lane == 2, r2, kept)


def forward_block(layout, hidden, where, counts, sel, grad, own, oth):
    rows, width = sel.shape
    seqs = counts.shape[0]
    slots = rows // seqs
    blocks = len(layout.blocks)
    row = lambda w: pl.BlockSpec((slots, w), lambda b, *_: (b, 0))
    col = pl.BlockSpec((width, slots), lambda b, *_: (0, b))
    shape = jax.ShapeDtypeStruct
    return pl.pallas_call(
        partial(forward_kernel, layout=layout, half=3 * width // 2, third=width // 2),
        grid_spec=pltpu.PrefetchScalarGridSpec(
            num_scalar_prefetch=2,
            grid=(seqs,),
            in_specs=[row(width), row(width)] + [ANY] * (2 * layout.pieces),
            out_specs=[
                row(3 * width), row(width), row(width), row(width), col, row(width), col, col, row(128),
                whole((8, width)), whole((1, hidden)), whole((1, width)),
            ],
            scratch_shapes=[
                pltpu.VMEM((width, 3 * width), BF16),
                pltpu.VMEM((width, width), BF16),
                pltpu.VMEM((width, 256), BF16),
                pltpu.SemaphoreType.DMA((2, blocks)),
                pltpu.SemaphoreType.DMA((2, blocks)),
                pltpu.SemaphoreType.DMA((2, blocks)),
            ],
        ),
        out_shape=[
            shape((rows, 3 * width), BF16),
            shape((rows, width), BF16),
            shape((rows, width), F32),
            shape((rows, width), BF16),
            shape((width, rows), BF16),
            shape((rows, width), BF16),
            shape((width, rows), BF16),
            shape((width, rows), BF16),
            shape((rows, 128), F32),
            shape((8, width), F32),
            shape((1, hidden), F32),
            shape((1, width), F32),
        ],
        compiler_params=params("arbitrary"),
        cost_estimate=cost(10 * rows * width * width, 30 * rows * width),
        name="forward_block",
    )(where, counts, sel, grad, *own, *oth)


def mlp_kernel(where, bias, *rest, layout, tile):
    rows_in = rest[:4]
    own, oth = rest[4 : 4 + layout.pieces], rest[4 + layout.pieces : 4 + 2 * layout.pieces]
    mlp, dn2, d_own, d_oth, dbias, *held, w_up, w_down, d_first, sem_rows, sems, sem_out = rest[
        4 + 2 * layout.pieces :
    ]
    n2, n2t, g, gt = held
    i = pl.program_id(0)
    here = where[0]
    row_copies = [
        pltpu.make_async_copy(rows_in[k], held[k], sem_rows.at[k]) for k in range(4)
    ]
    out_copy = pltpu.make_async_copy(d_first, d_own, sem_out)

    def copies(side, kind):
        source, target = (own, oth)[side], (w_up, w_down)[kind].at[side]
        return load_rows(
            layout, here, source, target, sems.at[side, kind], pl.ds(kind * tile, tile), pl.ds(0, tile)
        )

    def wait_first(*waited):
        @pl.when(i == 0)
        def _():
            for c in waited:
                c.wait()

    @pl.when(i == 0)
    def _():
        started = copies(0, 0) + row_copies[:1] + copies(0, 1) + row_copies[2:3]
        started = started + row_copies[1:2] + row_copies[3:] + copies(1, 0) + copies(1, 1)
        for c in started:
            c.start()

    wait_first(*copies(0, 0), row_copies[0])

    @pl.when(i == 1)
    def _():
        out_copy.start()
        for c in copies(1, 0) + copies(1, 1):
            c.wait()

    up_now = w_up[i]
    pre = dot(n2[...], up_now) + bias[...]
    wait_first(*copies(0, 1), row_copies[2])
    down_now = w_down[i]
    square = pre * pre
    th = jnp.tanh(pre * (GELU_A + GELU_A * GELU_B * square))
    half = 0.5 * (1.0 + th)
    act = (pre * half).astype(BF16)
    slope = half + 0.5 * pre * (1.0 - th * th) * (GELU_A + 3 * GELU_A * GELU_B * square)
    d_pre = (slope * dot(g[...], down_now)).astype(BF16)
    dbias[...] = jnp.sum(d_pre.astype(F32), axis=0, keepdims=True)
    mlp_now = dot(act, down_now, 1, 1)
    dn2_now = dot(d_pre, up_now, 1, 1)
    wait_first(row_copies[1], row_copies[3])
    dup = dot(n2t[...], d_pre).astype(BF16)
    ddown = dot(gt[...], act).astype(BF16)

    @pl.when(i == 0)
    def _():
        mlp[...] = mlp_now
        dn2[...] = dn2_now
        d_first[:, :tile] = dup
        d_first[:, tile:] = ddown

    @pl.when(i == 1)
    def _():
        mlp[...] += mlp_now
        dn2[...] += dn2_now
        d_oth[:, :tile] = dup
        d_oth[:, tile:] = ddown
        out_copy.wait()


def mlp_part(layout, where, part, tile, n2, n2t, g, gt, own, oth, bias):
    rows, width = n2.shape
    parts = bias.shape[1] // (2 * tile)
    blocks = len(layout.blocks)
    shape = jax.ShapeDtypeStruct
    return pl.pallas_call(
        partial(mlp_kernel, layout=layout, tile=tile),
        grid_spec=pltpu.PrefetchScalarGridSpec(
            num_scalar_prefetch=1,
            grid=(2,),
            in_specs=[
                pl.BlockSpec((1, tile), lambda i, where: (0, (where[1] ^ i) * parts + part)),
            ] + [ANY] * (4 + 2 * layout.pieces),
            out_specs=[
                whole((rows, width)), whole((rows, width)), ANY, whole((width, 2 * tile)),
                pl.BlockSpec((1, tile), lambda i, where: (0, i)),
            ],
            scratch_shapes=[
                pltpu.VMEM((rows, width), BF16),
                pltpu.VMEM((width, rows), BF16),
                pltpu.VMEM((rows, width), BF16),
                pltpu.VMEM((width, rows), BF16),
                pltpu.VMEM((2, width, tile), BF16),
                pltpu.VMEM((2, width, tile), BF16),
                pltpu.VMEM((width, 2 * tile), BF16),
                pltpu.SemaphoreType.DMA((4,)),
                pltpu.SemaphoreType.DMA((2, 2, blocks)),
                pltpu.SemaphoreType.DMA,
            ],
        ),
        out_shape=[
            shape((rows, width), F32),
            shape((rows, width), F32),
            shape((width, 2 * tile), BF16),
            shape((width, 2 * tile), BF16),
            shape((1, 2 * tile), F32),
        ],
        compiler_params=params("arbitrary"),
        cost_estimate=cost(24 * rows * width * tile, 8 * rows * width),
        name="mlp_part",
    )(where, bias, n2, n2t, g, gt, *own, *oth)


def norm_pull(values, inverse, scaled):
    return inverse * scaled - values * (
        inverse * inverse * inverse * jnp.mean(scaled * values, axis=-1, keepdims=True)
    )


def backward_kernel(
    where, counts, sel, grad, vec, qkv, mid, stats, mlp, mlp_two, dn2, dn2_two, *rest, layout, half, third
):
    own, oth = rest[: layout.pieces], rest[layout.pieces : 2 * layout.pieces]
    dqkv, dattnt, dmid, new_rows, drouter, w_out, sem_out = rest[2 * layout.pieces :]
    b = pl.program_id(0)
    slots, width = sel.shape
    here = where[0]

    @pl.when(b == 0)
    def _():
        copies = both_halves(layout, here, own, oth, w_out, sem_out, half, third)
        for c in copies:
            c.start()
        for c in copies:
            c.wait()

    x = sel[...].astype(F32)
    stream = mid[...]
    rate = stats[:, 1:2]
    r2 = stats[:, 2:3]
    slot_grad = grad[...].astype(F32)
    branch = (stream - x) + ((mlp[...] + mlp_two[...]) + vec[2:3, :])
    new_rows[...] = (x + rate * branch).astype(BF16)
    d_logit = jnp.sum(slot_grad * branch, axis=-1, keepdims=True) * (rate * (1.0 - rate))
    router_now = jnp.sum(d_logit * x, axis=0, keepdims=True)

    @pl.when(b == 0)
    def _():
        drouter[...] = router_now

    @pl.when(b > 0)
    def _():
        drouter[...] += router_now

    d_mid = norm_pull(stream, r2, vec[1:2, :] * (dn2[...] + dn2_two[...]))
    dmid[...] = d_mid + d_logit * vec[3:4, :]
    d_attn = (rate * slot_grad + d_mid).astype(BF16)
    store_rows(layout, here, dattnt, d_attn.T)
    d_att = dot(d_attn, w_out[...]).astype(BF16)

    allowed = allowed_keys(slots, counts[b])
    for pair in range(width // (2 * HEAD_DIM)):
        qc, kc, vc = pair_columns(pair, width // 2)
        queries = split_pair(qkv[:, qc] * SCALE)
        keys = qkv[:, kc]
        lse = jnp.concatenate(
            [
                stats[:, LSE_LANE + 2 * pair : LSE_LANE + 2 * pair + 1],
                stats[:, LSE_LANE + 2 * pair + 1 : LSE_LANE + 2 * pair + 2],
            ],
            axis=0,
        )
        upstream = split_pair(d_att[:, pair * 128 : (pair + 1) * 128])
        scores = dot(queries, keys, 1, 1)
        probs = jnp.exp(jnp.where(allowed, scores - lse, NEG_FILL))
        d_probs = dot(upstream, qkv[:, vc], 1, 1)
        d_scores = (probs * (d_probs - jnp.sum(probs * d_probs, axis=-1, keepdims=True))).astype(BF16)
        dqkv[:, qc] = (join_pair(dot(d_scores, keys)) * SCALE).astype(BF16)
        dqkv[:, kc] = dot(d_scores, queries, 0, 0).astype(BF16)
        dqkv[:, vc] = dot(probs.astype(BF16), upstream, 0, 0).astype(BF16)


def backward_block(layout, where, counts, sel, grad, vec, qkv, mid, stats, sums, own, oth):
    rows, width = sel.shape
    seqs = counts.shape[0]
    slots = rows // seqs
    blocks = len(layout.blocks)
    row = lambda w: pl.BlockSpec((slots, w), lambda b, *_: (b, 0))
    col = pl.BlockSpec((width, slots), lambda b, *_: (0, b))
    shape = jax.ShapeDtypeStruct
    return pl.pallas_call(
        partial(backward_kernel, layout=layout, half=3 * width // 2, third=width // 2),
        grid_spec=pltpu.PrefetchScalarGridSpec(
            num_scalar_prefetch=2,
            grid=(seqs,),
            in_specs=[
                row(width), row(width), whole(vec.shape), row(3 * width), row(width), row(128),
            ] + [row(width)] * 4 + [ANY] * (2 * layout.pieces),
            out_specs=[row(3 * width), col, row(width), row(width), whole((1, width))],
            scratch_shapes=[
                pltpu.VMEM((width, width), BF16),
                pltpu.SemaphoreType.DMA((2, blocks)),
            ],
        ),
        out_shape=[
            shape((rows, 3 * width), BF16),
            shape((width, rows), BF16),
            shape((rows, width), F32),
            shape((rows, width), BF16),
            shape((1, width), F32),
        ],
        compiler_params=params("arbitrary"),
        cost_estimate=cost(20 * rows * width * width, 30 * rows * width),
        name="backward_block",
    )(where, counts, sel, grad, vec, qkv, mid, stats, *sums, *own, *oth)


def project_kernel(n1t, dattnt, dqkv, att, small, out):
    half = dqkv.shape[1]
    third = att.shape[1]
    out[:, :half] = dot(n1t[...], dqkv[...]).astype(BF16)
    out[:, half : half + third] = dot(dattnt[...], att[...]).astype(BF16)
    out[:, half + third :] = small[...]


def project_grads(n1t, dattnt, dqkv, att, small, side):
    width, rows = n1t.shape
    half, third, extra = dqkv.shape[1] // 2, att.shape[1] // 2, small.shape[1]
    total = half + third + extra
    return pl.pallas_call(
        project_kernel,
        grid=(1,),
        in_specs=[
            whole((width, rows)), whole((width, rows)),
            pl.BlockSpec((rows, half), lambda i: (0, side)),
            pl.BlockSpec((rows, third), lambda i: (0, side)),
            whole((width, extra)),
        ],
        out_specs=whole((width, total)),
        out_shape=jax.ShapeDtypeStruct((width, total), BF16),
        compiler_params=params("arbitrary"),
        cost_estimate=cost(2 * width * rows * total, 2 * (2 * width * rows + rows * total + width * total)),
        name="project_grads",
    )(n1t, dattnt, dqkv, att, small)


def place(rows, target, x, start, count):
    length = x.shape[0]
    places = lax.broadcasted_iota(jnp.int32, (length, target.shape[1]), 0)
    hits = target == places
    moved = dot(jnp.where(hits, 1.0, 0.0).astype(BF16), rows)
    hit = jnp.max(jnp.where(hits, 1.0, 0.0), axis=-1, keepdims=True)
    at = lax.broadcasted_iota(jnp.int32, (length, 1), 0)
    kept = (at >= start) & (at < start + count) & (hit < 0.5)
    return jnp.where(kept, x.astype(F32), moved).astype(BF16)


def out_kernel(runs, rows, target, x, out):
    b = pl.program_id(0)
    out[0] = place(rows[...], target[0], x[0], runs[0, b], runs[1, b])


def place_rows(runs, rows, target, x):
    seqs, length, width = x.shape
    slots = target.shape[2]
    big = pl.BlockSpec((1, length, width), lambda b, *_: (b, 0, 0))
    return pl.pallas_call(
        out_kernel,
        grid_spec=pltpu.PrefetchScalarGridSpec(
            num_scalar_prefetch=1,
            grid=(seqs,),
            in_specs=[
                pl.BlockSpec((slots, width), lambda b, *_: (b, 0)),
                pl.BlockSpec((1, 1, slots), lambda b, *_: (b, 0, 0)),
                big,
            ],
            out_specs=big,
        ),
        out_shape=jax.ShapeDtypeStruct(x.shape, BF16),
        compiler_params=params("arbitrary"),
        cost_estimate=cost(2 * seqs * slots * length * width, 4 * seqs * length * width),
        name="place_rows",
    )(runs, rows, target, x)


def input_kernel(
    where, runs, sel, grad, vec, stats, dmid, dqkv, target, x, *rest, layout, first
):
    own, oth = rest[: layout.pieces], rest[layout.pieces : 2 * layout.pieces]
    *_, out, w_in, sem_in = rest[2 * layout.pieces :]
    b = pl.program_id(0)

    @pl.when(b == 0)
    def _():
        copies = both_halves(layout, where[0], own, oth, w_in, sem_in, 0, w_in.shape[1] // 2)
        for c in copies:
            c.start()
        for c in copies:
            c.wait()

    d_normed = dot(dqkv[...], w_in[...], 1, 1)
    d_sel = norm_pull(sel[...].astype(F32), stats[:, 0:1], vec[0:1, :] * d_normed) + dmid[...]
    rows = (grad[...].astype(F32) + d_sel).astype(BF16)
    out[0] = place(rows, target[0], x[0], runs[0, first + b], runs[1, first + b])


def input_rows(layout, where, runs, sel, grad, vec, stats, dmid, dqkv, target, x, own, oth, first, count, begun=()):
    seqs, length, width = x.shape
    slots = target.shape[2]
    blocks = len(layout.blocks)
    row = lambda w: pl.BlockSpec((slots, w), lambda b, *_: (first + b, 0))
    big = pl.BlockSpec((1, length, width), lambda b, *_: (first + b, 0, 0))
    return pl.pallas_call(
        partial(input_kernel, layout=layout, first=first),
        grid_spec=pltpu.PrefetchScalarGridSpec(
            num_scalar_prefetch=2,
            grid=(count,),
            in_specs=[
                row(width), row(width), whole(vec.shape), row(128), row(width), row(3 * width),
                pl.BlockSpec((1, 1, slots), lambda b, *_: (first + b, 0, 0)),
                big,
            ] + [ANY] * (2 * layout.pieces + len(begun)),
            out_specs=big,
            scratch_shapes=[
                pltpu.VMEM((width, 3 * width), BF16),
                pltpu.SemaphoreType.DMA((2, blocks)),
            ],
        ),
        out_shape=jax.ShapeDtypeStruct(x.shape, BF16),
        compiler_params=params("arbitrary"),
        cost_estimate=cost(8 * seqs * slots * length * width, 4 * seqs * length * width),
        input_output_aliases={10 + 2 * layout.pieces: 0} if begun else {},
        name="input_rows",
    )(where, runs, sel, grad, vec, stats, dmid, dqkv, target, x, *own, *oth, *begun)


class Paths:
    def __init__(self, wide, narrow):
        self.wide, self.narrow, self.depth = wide, narrow, wide // 2
        ids = np.arange(wide * narrow).reshape(self.depth, 4, 2)
        self.lines = ids.transpose(1, 0, 2).reshape(4, -1).tolist()

    def swap(self, value):
        return lax.ppermute(value, "narrow", [(i, i ^ 1) for i in range(self.narrow)])

    def over(self, value, step):
        if step == 1:
            return lax.ppermute(value, "narrow", [(i, i ^ 2) for i in range(self.narrow)])
        if step == 2:
            return lax.ppermute(value, "wide", [(i, i ^ 1) for i in range(self.wide)])
        mask = self.narrow ^ 2
        return lax.ppermute(value, AXES, [(i, i ^ mask) for i in range(self.wide * self.narrow)])

    def along(self, value):
        return lax.all_to_all(value, AXES, 0, 0, axis_index_groups=self.lines, tiled=True)

    def to_line(self, halves):
        shard, cols = halves[0].shape
        sent = jnp.broadcast_to(jnp.stack(halves)[None], (self.depth, 2, shard, cols))
        return sent.reshape(self.depth * 2 * shard, cols)

    def gather_halved(self, held):
        near_x, near_y = self.over(held, 1), self.over(held, 2)
        mid = held.shape[0] // 2
        return [held, near_x, near_y, self.over(near_y[:mid], 1), self.over(near_x[mid:], 2)]

    def gather_direct(self, held):
        return [held] + [self.over(held, step) for step in (1, 2, 3)]

    def swap_all(self, pieces):
        return [self.swap(p) for p in pieces]

    def send_plane(self, both):
        rows = both.shape[0] // 4
        return [self.over(both[step * rows : (step + 1) * rows], step) for step in (1, 2, 3)]

    def sum_plane(self, both, got):
        rows = both.shape[0] // 4
        total = both[:rows].astype(F32)
        for v in got:
            total = total + v.astype(F32)
        return total.astype(BF16)

    def sum_line(self, got):
        return jnp.sum(got.reshape(self.depth, 2, -1, got.shape[1]).astype(F32), axis=0)


def halved(depth):
    return [(piece, z, piece, z) for piece in range(3) for z in range(depth)] + [
        (3 + (z >= depth // 2), z % (depth // 2), 3, z) for z in range(depth)
    ]


def direct(depth):
    return [(piece, z, piece, z) for piece in range(4) for z in range(depth)]


def add_halves(own, got):
    return (own.astype(F32) + got.astype(F32)).astype(BF16)


def tie(*values):
    return lax.optimization_barrier(values)


def per_device(
    layer_in,
    lengths,
    padding,
    picked,
    first_gain,
    project_in,
    project_out,
    second_gain,
    up_weight,
    up_bias,
    down_weight,
    down_bias,
    router,
    cotangent,
    *,
    wide,
    narrow,
):
    seqs, slots = picked.shape
    shard, in_width = project_in.shape
    width = in_width // 3
    hidden = up_weight.shape[1]
    devices = wide * narrow
    half = 3 * width // 2
    third = width // 2
    tile = hidden // 4
    fast = shard == 24 and wide % 4 == 0 and narrow == 4
    core = lax.axis_index("narrow") & 1 if fast else jnp.int32(0)
    device = lax.axis_index("wide") * narrow + lax.axis_index("narrow")

    in_split = project_in.reshape(shard, 3, 2, third)
    in_halves = [in_split[:, :, side].reshape(shard, half) for side in (0, 1)]
    out_t = project_out.T
    down_t = down_weight.T
    vectors = jnp.stack([first_gain, second_gain, down_bias, router])

    first = [
        jnp.concatenate([in_halves[side], out_t[:, side * third : (side + 1) * third]], axis=1)
        for side in (0, 1)
    ]

    def rest_of(side, part):
        at = (2 * side + part) * tile
        return jnp.concatenate([up_weight[:, at : at + tile], down_t[:, at : at + tile]], axis=1)

    counts = lengths // 8
    valid = jnp.arange(slots)[None, :] < counts[:, None]
    target = jnp.where(valid, picked, -1)
    runs = jnp.stack([jnp.argmax(padding, axis=1).astype(jnp.int32), lengths])
    columns = target[:, :, None]
    if fast:
        paths = Paths(wide, narrow)
        here = (lax.axis_index("wide") & 1) * 2 + (lax.axis_index("narrow") >> 1)
        lay_one = Layout(2 * shard, 4, halved(paths.depth))
        lay_two = Layout(2 * shard, 4, direct(paths.depth))
        placed = lax.dynamic_update_slice(
            jnp.zeros((4, width), BF16), vectors, (0, device * shard)
        ).reshape(shard, 128)
        biases = lax.dynamic_update_slice(
            jnp.zeros((hidden,), BF16), up_bias, (device * 4 * shard,)
        ).reshape(shard, 128)
        sent = paths.to_line(
            [
                jnp.concatenate([first[0], placed], axis=1),
                jnp.concatenate([first[1], biases], axis=1),
            ]
        )
        sent, columns = tie(sent, columns)
        line = paths.along(sent)
        sel, slot_grad = gather_rows(columns, layer_in, cotangent)
        rest = paths.to_line(
            [jnp.concatenate([rest_of(side, 0), rest_of(side, 1)], axis=1) for side in (0, 1)]
        )
        line, rest, sel, slot_grad = tie(line, rest, sel, slot_grad)
        own = paths.gather_halved(line)
        oth = paths.swap_all(own)
        rest = paths.along(rest)
        own, oth, rest, sel = tie(own, oth, rest, sel)
        one_own = paths.gather_direct(rest[:, : 2 * tile])
        two_own = paths.gather_direct(rest[:, 2 * tile :])
    else:
        here = jnp.int32(0)
        lay_one = lay_two = Layout(width, 1, [(0, 0, 0, 0)])
        packed = jnp.concatenate(
            first + [rest_of(side, part) for part in (0, 1) for side in (0, 1)], axis=1
        )
        full = lax.all_gather(packed, AXES, axis=0, tiled=True)
        cuts = [0]
        for n in (half + third,) * 2 + (2 * tile,) * 4:
            cuts.append(cuts[-1] + n)
        own, oth, one_own, one_oth, two_own, two_oth = (
            [full[:, a:b]] for a, b in zip(cuts, cuts[1:])
        )
        every = lax.all_gather(vectors, AXES, axis=1, tiled=True).reshape(-1, 128)
        biases = lax.all_gather(up_bias, AXES, axis=0, tiled=True).reshape(-1, 128)
        own, oth = (
            [jnp.concatenate([p[0], jnp.pad(v, ((0, width - v.shape[0]), (0, 0)))], axis=1)]
            for p, v in ((own, every), (oth, biases))
        )
        sel, slot_grad = gather_rows(columns, layer_in, cotangent)

    where = jnp.stack([here, core]).astype(jnp.int32)
    qkv, att, mid, n2, n2t, g, gt, n1t, stats, vec, bias, ddown_bias = forward_block(
        lay_one, hidden, where, counts, sel, slot_grad, own, oth
    )
    if fast:
        one_own, n2 = tie(one_own, n2)
        one_oth = paths.swap_all(one_own)
    mlp, dn2, d_one_own, d_one_oth, dbias_one = mlp_part(
        lay_two, where, 0, tile, n2, n2t, g, gt, one_own, one_oth, bias
    )
    if fast:
        two_own, mlp, n2 = tie(two_own, mlp, n2)
        two_oth = paths.swap_all(two_own)
        d_one_got = paths.swap(d_one_oth)
    mlp_two, dn2_two, d_two_own, d_two_oth, dbias_two = mlp_part(
        lay_two, where, 1, tile, n2, n2t, g, gt, two_own, two_oth, bias
    )
    if fast:
        d_two_got = paths.swap(d_two_oth)
        d_one_got, mlp_two = tie(d_one_got, mlp_two)
        d_one = add_halves(d_one_own, d_one_got)
        d_one_plane = paths.send_plane(d_one)
        d_two = add_halves(d_two_own, d_two_got)
        _, d_two, mlp_two = tie(d_one, d_two, mlp_two)
        d_two_plane = paths.send_plane(d_two)
    dqkv, dattnt, dmid, new_rows, drouter = backward_block(
        lay_one, where, counts, sel, slot_grad, vec, qkv, mid, stats, (mlp, mlp_two, dn2, dn2_two), own, oth
    )
    if fast:
        d_one_plane, dqkv = tie(d_one_plane, dqkv)
    target_row = target[:, None, :]

    dbias = jnp.stack([dbias_one.reshape(2, tile), dbias_two.reshape(2, tile)], axis=1)
    dbias = jnp.where(core == 0, dbias, dbias[::-1])
    extra = 128 * -(-(4 * shard) // 128)
    line_one = dbias.reshape(devices, 1, 4 * shard)
    line_two = jnp.concatenate(
        [ddown_bias.reshape(devices, 1, shard), drouter.reshape(devices, 1, shard)], axis=2
    )
    lines = jnp.concatenate(
        [
            jnp.pad(line_one, ((0, 0), (0, 0), (0, extra - 4 * shard))),
            jnp.pad(line_two, ((0, 0), (0, 0), (0, extra - 2 * shard))),
        ],
        axis=1,
    ).astype(BF16)
    lines = jnp.pad(lines, ((0, 0), (0, shard - 2), (0, 0)))
    if fast:
        lines = lines.reshape(paths.depth, 4, 2 * shard, extra).transpose(1, 0, 2, 3)
        lines = jnp.take(lines, jnp.arange(4) ^ here, axis=0)
    lines = lines.reshape(width, extra)
    proj_oth = project_grads(n1t, dattnt, dqkv, att, lines, 1)
    if fast:
        proj_got = paths.swap(proj_oth)
    proj_own = project_grads(n1t, dattnt, dqkv, att, lines, 0)
    if fast:
        proj = add_halves(proj_own, proj_got)
        proj_plane = paths.send_plane(proj)
        two = [
            paths.sum_plane(d_one, d_one_plane),
            paths.sum_plane(d_two, d_two_plane),
        ]
        sums = jnp.concatenate(two, axis=1)
        _, sums, new_rows, target_row = tie(proj, sums, new_rows, target_row)
        sums = paths.along(sums)
    layer_out = place_rows(runs, new_rows, target_row, layer_in)
    part = seqs // 2
    input_grad = input_rows(
        lay_one, where, runs, sel, slot_grad, vec, stats, dmid, dqkv, target_row, cotangent, own, oth, 0, part
    )
    if fast:
        proj = paths.sum_plane(proj, proj_plane)
        sums, proj, dmid, input_grad = tie(sums, proj, dmid, input_grad)
    input_grad = input_rows(
        lay_one, where, runs, sel, slot_grad, vec, stats, dmid, dqkv, target_row, cotangent, own, oth,
        part, seqs - part, (input_grad,),
    )

    if fast:
        sums = paths.sum_line(sums)
        proj = paths.sum_line(paths.along(proj))
        one, two = sums[:, :, : 2 * tile], sums[:, :, 2 * tile :]
    else:
        flat = jnp.concatenate(
            [d_one_own, d_one_oth, d_two_own, d_two_oth, proj_own, proj_oth], axis=1
        )
        total = lax.psum_scatter(flat.astype(F32), AXES, scatter_dimension=0, tiled=True)
        p = proj_own.shape[1]
        one = total[:, : 4 * tile].reshape(shard, 2, 2 * tile).transpose(1, 0, 2)
        two = total[:, 4 * tile : 8 * tile].reshape(shard, 2, 2 * tile).transpose(1, 0, 2)
        proj = total[:, 8 * tile :].reshape(shard, 2, p).transpose(1, 0, 2)

    up_grad = jnp.concatenate(
        [v[side, :, :tile] for side in (0, 1) for v in (one, two)], axis=1
    )
    down_grad = jnp.concatenate(
        [v[side, :, tile:] for side in (0, 1) for v in (one, two)], axis=1
    ).T
    in_grad = jnp.stack(
        [proj[side, :, :half].reshape(shard, 3, third) for side in (0, 1)], axis=2
    ).reshape(shard, in_width)
    out_grad = jnp.concatenate([proj[side, :, half : half + third] for side in (0, 1)], axis=1).T
    lines = proj[0, :, half + third :]
    gain_one = jnp.sum(project_in.astype(F32) * in_grad, axis=1) / first_gain.astype(F32)
    gain_two = jnp.sum(up_weight.astype(F32) * up_grad, axis=1) / second_gain.astype(F32)
    return (
        layer_out,
        input_grad,
        gain_one,
        in_grad,
        out_grad,
        gain_two,
        up_grad,
        lines[0, : 4 * shard],
        down_grad,
        lines[1, :shard],
        lines[1, shard : 2 * shard],
    )


def solution(mesh):
    both = ("wide", "narrow")
    rows3, rows2, rows1, cols = P(both, None, None), P(both, None), P(both), P(None, both)
    in_specs = (
        rows3, rows1, rows2, rows2, rows1, rows2, cols, rows1, rows2, rows1, cols, rows1, rows1, rows3,
    )
    out_specs = (rows3, rows3, rows1, rows2, cols, rows1, rows2, rows1, cols, rows1, rows1)
    return jax.shard_map(
        partial(per_device, wide=mesh.shape["wide"], narrow=mesh.shape["narrow"]),
        mesh=mesh,
        in_specs=in_specs,
        out_specs=out_specs,
        check_vma=False,
    )
```

```python
from functools import partial

import jax
import jax.numpy as jnp
import numpy as np
from jax import lax
from jax.experimental import pallas as pl
from jax.experimental.pallas import tpu as pltpu
from jax.sharding import PartitionSpec as P

HEAD_DIM = 64
EPSILON = 1e-06
NEG_FILL = -1e30
F32 = jnp.float32
BF16 = jnp.bfloat16
AXES = ("wide", "narrow")
SCALE = HEAD_DIM**-0.5
GELU_A = 0.7978845608028654
GELU_B = 0.044715
LSE_LANE = 16
MLP_CHUNKS = 4
PAIRS = 3
PLACE_ROWS = 512
ANY = pl.BlockSpec(memory_space=pl.ANY)
VMEM_LIMIT = 67043328


def dot(left, right, left_dim=1, right_dim=0):
    return lax.dot_general(
        left, right, (((left_dim,), (right_dim,)), ((), ())), preferred_element_type=F32
    )


def params(*semantics):
    return pltpu.CompilerParams(
        dimension_semantics=semantics or None, vmem_limit_bytes=VMEM_LIMIT
    )


def whole(shape):
    return pl.BlockSpec(shape, lambda *_: (0,) * len(shape))


def cost(flops, bytes_accessed):
    return pl.CostEstimate(
        flops=int(flops), bytes_accessed=int(bytes_accessed), transcendentals=0
    )


class Layout:
    def __init__(self, height, plane, blocks):
        self.height, self.plane, self.blocks = height, plane, tuple(blocks)
        self.pieces = 1 + max(piece for piece, *_ in blocks)
        self.depth = len(blocks) // plane

    def natural(self, here, step, line):
        return pl.multiple_of((line * self.plane + (here ^ step)) * self.height, 8)


def load_rows(layout, here, pieces, target, sems, source, columns):
    height = layout.height
    return [
        pltpu.make_async_copy(
            pieces[piece].at[pl.ds(at * height, height), source],
            target.at[pl.ds(layout.natural(here, step, line), height), columns],
            sems.at[j],
        )
        for j, (piece, at, step, line) in enumerate(layout.blocks)
    ]


def both_halves(layout, here, own, oth, target, sems, start, count):
    source = pl.ds(start, count)
    return load_rows(layout, here, own, target, sems.at[0], source, pl.ds(0, count)) + load_rows(
        layout, here, oth, target, sems.at[1], source, pl.ds(count, count)
    )


def store_rows(layout, here, target, value):
    height = layout.height
    for line in range(layout.depth):
        for owner in range(layout.plane):
            start = pl.multiple_of(((owner ^ here) * layout.depth + line) * height, 8)
            c = line * layout.plane + owner
            target[pl.ds(start, height), :] = value[c * height : (c + 1) * height, :]


def gather_kernel(target, x, cot, sel, grad):
    length = x.shape[1]
    places = lax.broadcasted_iota(jnp.int32, (target.shape[1], length), 1)
    chosen = jnp.where(target[0] == places, 1.0, 0.0).astype(BF16)
    sel[...] = dot(chosen, x[0]).astype(BF16)
    grad[...] = dot(chosen, cot[0]).astype(BF16)


def gather_rows(target, layer_in, cotangent):
    seqs, length, width = layer_in.shape
    slots = target.shape[1]
    big = pl.BlockSpec((1, length, width), lambda b: (b, 0, 0))
    out = pl.BlockSpec((slots, width), lambda b: (b, 0))
    return pl.pallas_call(
        gather_kernel,
        grid=(seqs,),
        in_specs=[pl.BlockSpec((1, slots, 1), lambda b: (b, 0, 0)), big, big],
        out_specs=[out, out],
        out_shape=[jax.ShapeDtypeStruct((seqs * slots, width), BF16)] * 2,
        compiler_params=params("arbitrary"),
        cost_estimate=cost(
            4 * seqs * slots * length * width, 4 * seqs * length * width
        ),
        name="gather_rows",
    )(target, layer_in, cotangent)


def allowed_keys(slots, valid):
    rows = lax.broadcasted_iota(jnp.int32, (2 * slots, slots), 0)
    rows = jnp.where(rows >= slots, rows - slots, rows)
    keys = lax.broadcasted_iota(jnp.int32, (2 * slots, slots), 1)
    return (keys <= rows) & (keys < valid)


def split_pair(pair):
    lane = lax.broadcasted_iota(jnp.int32, pair.shape, 1)
    zero = jnp.zeros_like(pair)
    first = lane < HEAD_DIM
    return jnp.concatenate(
        [jnp.where(first, pair, zero), jnp.where(first, zero, pair)], axis=0
    )


def join_pair(stacked):
    half = stacked.shape[0] // 2
    lane = lax.broadcasted_iota(jnp.int32, (half, stacked.shape[1]), 1)
    return jnp.where(lane < HEAD_DIM, stacked[:half], stacked[half:])


def pair_loop(pairs, body, carry):
    def step(k, carry):
        for p in range(PAIRS):
            carry = body(k * PAIRS + p, carry)
        return carry

    return lax.fori_loop(0, pairs // PAIRS, step, carry)


def pair_columns(pair, half_width):
    per_half = half_width // (2 * HEAD_DIM)
    base = (pair // per_half) * 3 * half_width + (pair % per_half) * 2 * HEAD_DIM
    return tuple(
        pl.ds(pl.multiple_of(base + k * half_width, 128), 2 * HEAD_DIM) for k in range(3)
    )


def forward_kernel(
    where, counts, sel, grad, *rest, layout, half, third
):
    own, oth = rest[: layout.pieces], rest[layout.pieces : 2 * layout.pieces]
    (
    qkv, att, mid, n2, n2t, g, gt, n1t, stats, vec, bias, gsum,
    w_in, w_out, w_ext, sem_in, sem_out, sem_ext,
    ) = rest[2 * layout.pieces :]
    b = pl.program_id(0)
    slots, width = sel.shape
    here = where[0]

    def in_copies():
        return both_halves(layout, here, own, oth, w_in, sem_in, 0, half)

    def out_copies():
        return both_halves(layout, here, own, oth, w_out, sem_out, half, third)

    @pl.when(b == 0)
    def _():
        small = both_halves(layout, here, own, oth, w_ext, sem_ext, half + third, 128)
        first = in_copies()
        for c in small + first + out_copies():
            c.start()
        for c in small:
            c.wait()
        per = width // 128
        high = 4 * per
        total = sum(w_ext[k * high : (k + 1) * high, :].astype(F32) for k in range(width // high))
        mine, others = total[:, :128], total[:, 128:]
        vectors = jnp.where(where[1] == 0, mine, others)
        biases = jnp.where(where[1] == 0, others, mine)
        vec[...] = jnp.zeros_like(vec)
        for v in range(4):
            for k in range(per):
                vec[v : v + 1, k * 128 : (k + 1) * 128] = vectors[v * per + k : v * per + k + 1, :]
        for k in range(bias.shape[1] // 128):
            bias[0:1, k * 128 : (k + 1) * 128] = biases[k : k + 1, :]
        for c in first:
            c.wait()

    x = sel[...].astype(F32)
    r1 = lax.rsqrt(jnp.mean(x * x, axis=-1, keepdims=True) + EPSILON)
    n1 = (x * r1 * vec[0:1, :]).astype(BF16)
    logit = jnp.sum(x * vec[3:4, :], axis=-1, keepdims=True)
    rate = jax.nn.sigmoid(logit)
    d_mlp = (rate * grad[...].astype(F32)).astype(BF16)
    g[...] = d_mlp
    gsum_now = jnp.sum(d_mlp.astype(F32), axis=0, keepdims=True)

    @pl.when(b == 0)
    def _():
        gsum[...] = gsum_now

    @pl.when(b > 0)
    def _():
        gsum[...] += gsum_now

    store_rows(layout, here, gt, d_mlp.T)
    store_rows(layout, here, n1t, n1.T)
    qkv[...] = dot(n1, w_in[...]).astype(BF16)

    allowed = allowed_keys(slots, counts[b])
    lane = lax.broadcasted_iota(jnp.int32, (slots, 128), 1)
    kept = jnp.where(lane == 0, r1, jnp.where(lane == 1, rate, 0.0))

    def attend(pair, kept):
        qc, kc, vc = pair_columns(pair, width // 2)
        scores = dot(split_pair(qkv[:, qc] * SCALE), qkv[:, kc], 1, 1)
        scores = jnp.where(allowed, scores, NEG_FILL)
        top = jnp.max(scores, axis=-1, keepdims=True)
        exps = jnp.exp(scores - top)
        total = jnp.sum(exps, axis=-1, keepdims=True)
        lse = top + jnp.log(total)
        probs = (exps * (1.0 / total)).astype(BF16)
        here_now = pl.ds(pl.multiple_of(pair * 128, 128), 128)
        att[:, here_now] = join_pair(dot(probs, qkv[:, vc])).astype(BF16)
        kept = jnp.where(lane == LSE_LANE + 2 * pair, lse[:slots], kept)
        return jnp.where(lane == LSE_LANE + 2 * pair + 1, lse[slots:], kept)

    kept = pair_loop(width // (2 * HEAD_DIM), attend, kept)

    @pl.when(b == 0)
    def _():
        for c in out_copies():
            c.wait()

    stream = x + dot(att[...], w_out[...], 1, 1)
    mid[...] = stream
    r2 = lax.rsqrt(jnp.mean(stream * stream, axis=-1, keepdims=True) + EPSILON)
    normed = (stream * r2 * vec[1:2, :]).astype(BF16)
    n2[...] = normed
    store_rows(layout, here, n2t, normed.T)
    stats[...] = jnp.where(lane == 2, r2, kept)


def forward_block(layout, hidden, where, counts, sel, grad, own, oth):
    rows, width = sel.shape
    seqs = counts.shape[0]
    slots = rows // seqs
    blocks = len(layout.blocks)
    row = lambda w: pl.BlockSpec((slots, w), lambda b, *_: (b, 0))
    col = pl.BlockSpec((width, slots), lambda b, *_: (0, b))
    shape = jax.ShapeDtypeStruct
    return pl.pallas_call(
        partial(forward_kernel, layout=layout, half=3 * width // 2, third=width // 2),
        grid_spec=pltpu.PrefetchScalarGridSpec(
            num_scalar_prefetch=2,
            grid=(seqs,),
            in_specs=[row(width), row(width)] + [ANY] * (2 * layout.pieces),
            out_specs=[
                row(3 * width), row(width), row(width), row(width), col, row(width), col, col, row(128),
                whole((8, width)), whole((1, hidden)), whole((1, width)),
            ],
            scratch_shapes=[
                pltpu.VMEM((width, 3 * width), BF16),
                pltpu.VMEM((width, width), BF16),
                pltpu.VMEM((width, 256), BF16),
                pltpu.SemaphoreType.DMA((2, blocks)),
                pltpu.SemaphoreType.DMA((2, blocks)),
                pltpu.SemaphoreType.DMA((2, blocks)),
            ],
        ),
        out_shape=[
            shape((rows, 3 * width), BF16),
            shape((rows, width), BF16),
            shape((rows, width), F32),
            shape((rows, width), BF16),
            shape((width, rows), BF16),
            shape((rows, width), BF16),
            shape((width, rows), BF16),
            shape((width, rows), BF16),
            shape((rows, 128), F32),
            shape((8, width), F32),
            shape((1, hidden), F32),
            shape((1, width), F32),
        ],
        compiler_params=params("arbitrary"),
        cost_estimate=cost(10 * rows * width * width, 30 * rows * width),
        name="forward_block",
    )(where, counts, sel, grad, *own, *oth)


def mlp_kernel(where, bias, *rest, layout, tile):
    rows_in = rest[:4]
    own, oth = rest[4 : 4 + layout.pieces], rest[4 + layout.pieces : 4 + 2 * layout.pieces]
    mlp, dn2, d_own, d_oth, dbias, *held, w_up, w_down, d_first, act, d_pre, sem_rows, sems, sem_out = rest[
        4 + 2 * layout.pieces :
    ]
    n2, n2t, g, gt = held
    i = pl.program_id(0)
    here = where[0]
    row_copies = [
        pltpu.make_async_copy(rows_in[k], held[k], sem_rows.at[k]) for k in range(4)
    ]
    out_copy = pltpu.make_async_copy(d_first, d_own, sem_out)

    def copies(side, kind):
        source, target = (own, oth)[side], (w_up, w_down)[kind].at[side]
        return load_rows(
            layout, here, source, target, sems.at[side, kind], pl.ds(kind * tile, tile), pl.ds(0, tile)
        )

    def wait_first(*waited):
        @pl.when(i == 0)
        def _():
            for c in waited:
                c.wait()

    @pl.when(i == 0)
    def _():
        started = copies(0, 0) + row_copies[:1] + copies(0, 1) + row_copies[2:3]
        started = started + row_copies[1:2] + row_copies[3:] + copies(1, 0) + copies(1, 1)
        for c in started:
            c.start()

    wait_first(*copies(0, 0), row_copies[0])

    @pl.when(i == 1)
    def _():
        out_copy.start()
        for c in copies(1, 0) + copies(1, 1):
            c.wait()

    wait_first(*copies(0, 1), row_copies[2])
    up_now = w_up.at[i]
    down_now = w_down.at[i]
    rows = n2.shape[0] // MLP_CHUNKS

    def chunk(c, total):
        here = pl.ds(pl.multiple_of(c * rows, rows), rows)
        pre = dot(n2[here, :], up_now[...]) + bias[...]
        square = pre * pre
        th = jnp.tanh(pre * (GELU_A + GELU_A * GELU_B * square))
        half = 0.5 * (1.0 + th)
        act_now = (pre * half).astype(BF16)
        act[here, :] = act_now
        slope = half + 0.5 * pre * (1.0 - th * th) * (GELU_A + 3 * GELU_A * GELU_B * square)
        d_pre_now = (slope * dot(g[here, :], down_now[...])).astype(BF16)
        d_pre[here, :] = d_pre_now
        mlp[here, :] = jnp.where(i == 0, 0.0, mlp[here, :]) + dot(act_now, down_now[...], 1, 1)
        dn2[here, :] = jnp.where(i == 0, 0.0, dn2[here, :]) + dot(d_pre_now, up_now[...], 1, 1)
        return total + jnp.sum(d_pre_now.astype(F32), axis=0, keepdims=True)

    dbias[...] = lax.fori_loop(0, MLP_CHUNKS, chunk, jnp.zeros_like(dbias))
    wait_first(row_copies[1], row_copies[3])
    dup = dot(n2t[...], d_pre[...]).astype(BF16)
    ddown = dot(gt[...], act[...]).astype(BF16)

    @pl.when(i == 0)
    def _():
        d_first[:, :tile] = dup
        d_first[:, tile:] = ddown

    @pl.when(i == 1)
    def _():
        d_oth[:, :tile] = dup
        d_oth[:, tile:] = ddown
        out_copy.wait()


def mlp_part(layout, where, part, tile, n2, n2t, g, gt, own, oth, bias):
    rows, width = n2.shape
    parts = bias.shape[1] // (2 * tile)
    blocks = len(layout.blocks)
    shape = jax.ShapeDtypeStruct
    return pl.pallas_call(
        partial(mlp_kernel, layout=layout, tile=tile),
        grid_spec=pltpu.PrefetchScalarGridSpec(
            num_scalar_prefetch=1,
            grid=(2,),
            in_specs=[
                pl.BlockSpec((1, tile), lambda i, where: (0, (where[1] ^ i) * parts + part)),
            ] + [ANY] * (4 + 2 * layout.pieces),
            out_specs=[
                whole((rows, width)), whole((rows, width)), ANY, whole((width, 2 * tile)),
                pl.BlockSpec((1, tile), lambda i, where: (0, i)),
            ],
            scratch_shapes=[
                pltpu.VMEM((rows, width), BF16),
                pltpu.VMEM((width, rows), BF16),
                pltpu.VMEM((rows, width), BF16),
                pltpu.VMEM((width, rows), BF16),
                pltpu.VMEM((2, width, tile), BF16),
                pltpu.VMEM((2, width, tile), BF16),
                pltpu.VMEM((width, 2 * tile), BF16),
                pltpu.VMEM((rows, tile), BF16),
                pltpu.VMEM((rows, tile), BF16),
                pltpu.SemaphoreType.DMA((4,)),
                pltpu.SemaphoreType.DMA((2, 2, blocks)),
                pltpu.SemaphoreType.DMA,
            ],
        ),
        out_shape=[
            shape((rows, width), F32),
            shape((rows, width), F32),
            shape((width, 2 * tile), BF16),
            shape((width, 2 * tile), BF16),
            shape((1, 2 * tile), F32),
        ],
        compiler_params=params("arbitrary"),
        cost_estimate=cost(24 * rows * width * tile, 8 * rows * width),
        name="mlp_part",
    )(where, bias, n2, n2t, g, gt, *own, *oth)


def norm_pull(values, inverse, scaled):
    return inverse * scaled - values * (
        inverse * inverse * inverse * jnp.mean(scaled * values, axis=-1, keepdims=True)
    )


def backward_kernel(
    where, counts, sel, grad, vec, qkv, mid, stats, mlp, mlp_two, dn2, dn2_two, *rest, layout, half, third
):
    own, oth = rest[: layout.pieces], rest[layout.pieces : 2 * layout.pieces]
    dqkv, dattnt, dmid, new_rows, drouter, w_out, d_att, sem_out = rest[2 * layout.pieces :]
    b = pl.program_id(0)
    slots, width = sel.shape
    here = where[0]

    @pl.when(b == 0)
    def _():
        copies = both_halves(layout, here, own, oth, w_out, sem_out, half, third)
        for c in copies:
            c.start()
        for c in copies:
            c.wait()

    x = sel[...].astype(F32)
    stream = mid[...]
    rate = stats[:, 1:2]
    r2 = stats[:, 2:3]
    slot_grad = grad[...].astype(F32)
    branch = (stream - x) + ((mlp[...] + mlp_two[...]) + vec[2:3, :])
    new_rows[...] = (x + rate * branch).astype(BF16)
    d_logit = jnp.sum(slot_grad * branch, axis=-1, keepdims=True) * (rate * (1.0 - rate))
    router_now = jnp.sum(d_logit * x, axis=0, keepdims=True)

    @pl.when(b == 0)
    def _():
        drouter[...] = router_now

    @pl.when(b > 0)
    def _():
        drouter[...] += router_now

    d_mid = norm_pull(stream, r2, vec[1:2, :] * (dn2[...] + dn2_two[...]))
    dmid[...] = d_mid + d_logit * vec[3:4, :]
    d_attn = (rate * slot_grad + d_mid).astype(BF16)
    store_rows(layout, here, dattnt, d_attn.T)
    d_att[...] = dot(d_attn, w_out[...]).astype(BF16)

    allowed = allowed_keys(slots, counts[b])
    lane = lax.broadcasted_iota(jnp.int32, (slots, 128), 1)

    def pull(pair, carry):
        qc, kc, vc = pair_columns(pair, width // 2)
        queries = split_pair(qkv[:, qc] * SCALE)
        keys = qkv[:, kc]
        lse = jnp.concatenate(
            [
                jnp.sum(jnp.where(lane == LSE_LANE + 2 * pair + k, stats[...], 0.0), axis=-1, keepdims=True)
                for k in (0, 1)
            ],
            axis=0,
        )
        upstream = split_pair(d_att[:, pl.ds(pl.multiple_of(pair * 128, 128), 128)])
        scores = dot(queries, keys, 1, 1)
        probs = jnp.exp(jnp.where(allowed, scores - lse, NEG_FILL))
        d_probs = dot(upstream, qkv[:, vc], 1, 1)
        d_scores = (probs * (d_probs - jnp.sum(probs * d_probs, axis=-1, keepdims=True))).astype(BF16)
        dqkv[:, qc] = (join_pair(dot(d_scores, keys)) * SCALE).astype(BF16)
        dqkv[:, kc] = dot(d_scores, queries, 0, 0).astype(BF16)
        dqkv[:, vc] = dot(probs.astype(BF16), upstream, 0, 0).astype(BF16)
        return carry

    pair_loop(width // (2 * HEAD_DIM), pull, 0)


def backward_block(layout, where, counts, sel, grad, vec, qkv, mid, stats, sums, own, oth):
    rows, width = sel.shape
    seqs = counts.shape[0]
    slots = rows // seqs
    blocks = len(layout.blocks)
    row = lambda w: pl.BlockSpec((slots, w), lambda b, *_: (b, 0))
    col = pl.BlockSpec((width, slots), lambda b, *_: (0, b))
    shape = jax.ShapeDtypeStruct
    return pl.pallas_call(
        partial(backward_kernel, layout=layout, half=3 * width // 2, third=width // 2),
        grid_spec=pltpu.PrefetchScalarGridSpec(
            num_scalar_prefetch=2,
            grid=(seqs,),
            in_specs=[
                row(width), row(width), whole(vec.shape), row(3 * width), row(width), row(128),
            ] + [row(width)] * 4 + [ANY] * (2 * layout.pieces),
            out_specs=[row(3 * width), col, row(width), row(width), whole((1, width))],
            scratch_shapes=[
                pltpu.VMEM((width, width), BF16),
                pltpu.VMEM((slots, width), BF16),
                pltpu.SemaphoreType.DMA((2, blocks)),
            ],
        ),
        out_shape=[
            shape((rows, 3 * width), BF16),
            shape((width, rows), BF16),
            shape((rows, width), F32),
            shape((rows, width), BF16),
            shape((1, width), F32),
        ],
        compiler_params=params("arbitrary"),
        cost_estimate=cost(20 * rows * width * width, 30 * rows * width),
        name="backward_block",
    )(where, counts, sel, grad, vec, qkv, mid, stats, *sums, *own, *oth)


def project_kernel(where, n1t, dattnt, dqkv, att, dbias_one, dbias_two, ddown, drouter, oth, own):
    half = dqkv.shape[1]
    third = att.shape[1]
    width = n1t.shape[0]
    high, tile = 4 * width // 128, dbias_one.shape[1] // 2
    in_now = dot(n1t[...], dqkv[...]).astype(BF16)
    out_now = dot(dattnt[...], att[...]).astype(BF16)
    first_core = where[1] == 0

    def bias_rows():
        rows = []
        for side in (0, 1):
            for part in (dbias_one, dbias_two):
                for k in range(tile // 128):
                    a, b = side * tile + k * 128, (1 - side) * tile + k * 128
                    rows.append(jnp.where(first_core, part[:, a : a + 128], part[:, b : b + 128]))
        return rows

    def vector_rows():
        rows = [v[:, k * 128 : (k + 1) * 128] for v in (ddown, drouter) for k in range(width // 128)]
        return rows + [jnp.zeros((1, 128), F32)] * (high - len(rows))

    def store(out, is_first):
        out[:, :half] = in_now
        out[:, half : half + third] = out_now
        small = jnp.where(
            is_first, jnp.concatenate(bias_rows(), axis=0), jnp.concatenate(vector_rows(), axis=0)
        )
        small = jnp.concatenate([small] * 2, axis=0).astype(BF16)
        for k in range(width // (2 * high)):
            out[2 * k * high : 2 * (k + 1) * high, half + third :] = small

    pl.when(pl.program_id(0) == 0)(lambda: store(oth, where[1] == 1))
    pl.when(pl.program_id(0) == 1)(lambda: store(own, where[1] == 0))


def project_grads(where, n1t, dattnt, dqkv, att, *vectors):
    width, rows = n1t.shape
    half, third = dqkv.shape[1] // 2, att.shape[1] // 2
    total = half + third + 128
    return pl.pallas_call(
        project_kernel,
        grid_spec=pltpu.PrefetchScalarGridSpec(
            num_scalar_prefetch=1,
            grid=(2,),
            in_specs=[
                whole((width, rows)), whole((width, rows)),
                pl.BlockSpec((rows, half), lambda i, where: (0, 1 - i)),
                pl.BlockSpec((rows, third), lambda i, where: (0, 1 - i)),
            ] + [whole(v.shape) for v in vectors],
            out_specs=[whole((width, total))] * 2,
        ),
        out_shape=[jax.ShapeDtypeStruct((width, total), BF16)] * 2,
        compiler_params=params("arbitrary"),
        cost_estimate=cost(4 * width * rows * total, 2 * (2 * width * rows + rows * total + width * total)),
        name="project_grads",
    )(where, n1t, dattnt, dqkv, att, *vectors)


def place(out, rows, target, x, start, count):
    chunk = min(PLACE_ROWS, x.shape[1])

    def one(c, carry):
        here = pl.ds(pl.multiple_of(c * chunk, chunk), chunk)
        places = lax.broadcasted_iota(jnp.int32, (chunk, target.shape[2]), 0) + c * chunk
        hits = target[0] == places
        moved = dot(jnp.where(hits, 1.0, 0.0).astype(BF16), rows[...])
        hit = jnp.max(jnp.where(hits, 1.0, 0.0), axis=-1, keepdims=True)
        at = lax.broadcasted_iota(jnp.int32, (chunk, 1), 0) + c * chunk
        kept = (at >= start) & (at < start + count) & (hit < 0.5)
        out[0, here, :] = jnp.where(kept, x[0, here, :].astype(F32), moved).astype(BF16)
        return carry

    lax.fori_loop(0, x.shape[1] // chunk, one, 0)


def out_kernel(runs, rows, target, x, out):
    b = pl.program_id(0)
    place(out, rows, target, x, runs[0, b], runs[1, b])


def place_rows(runs, rows, target, x):
    seqs, length, width = x.shape
    slots = target.shape[2]
    big = pl.BlockSpec((1, length, width), lambda b, *_: (b, 0, 0))
    return pl.pallas_call(
        out_kernel,
        grid_spec=pltpu.PrefetchScalarGridSpec(
            num_scalar_prefetch=1,
            grid=(seqs,),
            in_specs=[
                pl.BlockSpec((slots, width), lambda b, *_: (b, 0)),
                pl.BlockSpec((1, 1, slots), lambda b, *_: (b, 0, 0)),
                big,
            ],
            out_specs=big,
        ),
        out_shape=jax.ShapeDtypeStruct(x.shape, BF16),
        compiler_params=params("arbitrary"),
        cost_estimate=cost(2 * seqs * slots * length * width, 4 * seqs * length * width),
        name="place_rows",
    )(runs, rows, target, x)


def input_kernel(
    where, runs, sel, grad, vec, stats, dmid, dqkv, target, x, *rest, layout, first
):
    own, oth = rest[: layout.pieces], rest[layout.pieces : 2 * layout.pieces]
    *_, out, w_in, moved, sem_in = rest[2 * layout.pieces :]
    b = pl.program_id(0)

    @pl.when(b == 0)
    def _():
        copies = both_halves(layout, where[0], own, oth, w_in, sem_in, 0, w_in.shape[1] // 2)
        for c in copies:
            c.start()
        for c in copies:
            c.wait()

    d_normed = dot(dqkv[...], w_in[...], 1, 1)
    d_sel = norm_pull(sel[...].astype(F32), stats[:, 0:1], vec[0:1, :] * d_normed) + dmid[...]
    moved[...] = (grad[...].astype(F32) + d_sel).astype(BF16)
    place(out, moved, target, x, runs[0, first + b], runs[1, first + b])


def input_rows(layout, where, runs, sel, grad, vec, stats, dmid, dqkv, target, x, own, oth, first, count, begun=()):
    seqs, length, width = x.shape
    slots = target.shape[2]
    blocks = len(layout.blocks)
    row = lambda w: pl.BlockSpec((slots, w), lambda b, *_: (first + b, 0))
    big = pl.BlockSpec((1, length, width), lambda b, *_: (first + b, 0, 0))
    return pl.pallas_call(
        partial(input_kernel, layout=layout, first=first),
        grid_spec=pltpu.PrefetchScalarGridSpec(
            num_scalar_prefetch=2,
            grid=(count,),
            in_specs=[
                row(width), row(width), whole(vec.shape), row(128), row(width), row(3 * width),
                pl.BlockSpec((1, 1, slots), lambda b, *_: (first + b, 0, 0)),
                big,
            ] + [ANY] * (2 * layout.pieces + len(begun)),
            out_specs=big,
            scratch_shapes=[
                pltpu.VMEM((width, 3 * width), BF16),
                pltpu.VMEM((slots, width), BF16),
                pltpu.SemaphoreType.DMA((2, blocks)),
            ],
        ),
        out_shape=jax.ShapeDtypeStruct(x.shape, BF16),
        compiler_params=params("arbitrary"),
        cost_estimate=cost(8 * seqs * slots * length * width, 4 * seqs * length * width),
        input_output_aliases={10 + 2 * layout.pieces: 0} if begun else {},
        name="input_rows",
    )(where, runs, sel, grad, vec, stats, dmid, dqkv, target, x, *own, *oth, *begun)


class Paths:
    def __init__(self, wide, narrow):
        self.wide, self.narrow, self.depth = wide, narrow, wide // 2
        ids = np.arange(wide * narrow).reshape(self.depth, 4, 2)
        self.lines = ids.transpose(1, 0, 2).reshape(4, -1).tolist()

    def swap(self, value):
        return lax.ppermute(value, "narrow", [(i, i ^ 1) for i in range(self.narrow)])

    def over(self, value, step):
        if step == 1:
            return lax.ppermute(value, "narrow", [(i, i ^ 2) for i in range(self.narrow)])
        if step == 2:
            return lax.ppermute(value, "wide", [(i, i ^ 1) for i in range(self.wide)])
        mask = self.narrow ^ 2
        return lax.ppermute(value, AXES, [(i, i ^ mask) for i in range(self.wide * self.narrow)])

    def along(self, value):
        return lax.all_to_all(value, AXES, 0, 0, axis_index_groups=self.lines, tiled=True)

    def to_line(self, halves):
        shard, cols = halves[0].shape
        sent = jnp.broadcast_to(jnp.stack(halves)[None], (self.depth, 2, shard, cols))
        return sent.reshape(self.depth * 2 * shard, cols)

    def gather_halved(self, held):
        near_x, near_y = self.over(held, 1), self.over(held, 2)
        mid = held.shape[0] // 2
        return [held, near_x, near_y, self.over(near_y[:mid], 1), self.over(near_x[mid:], 2)]

    def gather_direct(self, held):
        return [held] + [self.over(held, step) for step in (1, 2, 3)]

    def swap_all(self, pieces):
        return [self.swap(p) for p in pieces]

    def chip_sums(self, own, got):
        rows = own.shape[0] // 4
        return [
            add_halves(own[step * rows : (step + 1) * rows], got[step * rows : (step + 1) * rows])
            for step in range(4)
        ]

    def send_plane(self, sums):
        return [self.over(sums[step], step) for step in (1, 2, 3)]

    def sum_plane(self, mine, got):
        total = mine.astype(F32)
        for v in got:
            total = total + v.astype(F32)
        return total.astype(BF16)

    def sum_line(self, got):
        return jnp.sum(got.reshape(self.depth, 2, -1, got.shape[1]).astype(F32), axis=0)


def halved(depth):
    return [(piece, z, piece, z) for piece in range(3) for z in range(depth)] + [
        (3 + (z >= depth // 2), z % (depth // 2), 3, z) for z in range(depth)
    ]


def direct(depth):
    return [(piece, z, piece, z) for piece in range(4) for z in range(depth)]


def add_halves(own, got):
    return (own.astype(F32) + got.astype(F32)).astype(BF16)


def tie(*values):
    return lax.optimization_barrier(values)


def per_device(
    layer_in,
    lengths,
    padding,
    picked,
    first_gain,
    project_in,
    project_out,
    second_gain,
    up_weight,
    up_bias,
    down_weight,
    down_bias,
    router,
    cotangent,
    *,
    wide,
    narrow,
):
    seqs, slots = picked.shape
    shard, in_width = project_in.shape
    width = in_width // 3
    hidden = up_weight.shape[1]
    devices = wide * narrow
    half = 3 * width // 2
    third = width // 2
    tile = hidden // 4
    fast = shard == 24 and wide % 4 == 0 and narrow == 4
    core = lax.axis_index("narrow") & 1 if fast else jnp.int32(0)
    device = lax.axis_index("wide") * narrow + lax.axis_index("narrow")

    in_split = project_in.reshape(shard, 3, 2, third)
    in_halves = [in_split[:, :, side].reshape(shard, half) for side in (0, 1)]
    out_t = project_out.T
    down_t = down_weight.T
    vectors = jnp.stack([first_gain, second_gain, down_bias, router])

    first = [
        jnp.concatenate([in_halves[side], out_t[:, side * third : (side + 1) * third]], axis=1)
        for side in (0, 1)
    ]

    def rest_of(side, part):
        at = (2 * side + part) * tile
        return jnp.concatenate([up_weight[:, at : at + tile], down_t[:, at : at + tile]], axis=1)

    def places(lengths):
        counts = lengths // 8
        valid = jnp.arange(slots)[None, :] < counts[:, None]
        target = jnp.where(valid, picked, -1)
        runs = jnp.stack([jnp.argmax(padding, axis=1).astype(jnp.int32), lengths])
        return counts, runs, target[:, :, None], target[:, None, :]

    if fast:
        paths = Paths(wide, narrow)
        here = (lax.axis_index("wide") & 1) * 2 + (lax.axis_index("narrow") >> 1)
        lay_one = Layout(2 * shard, 4, halved(paths.depth))
        lay_two = Layout(2 * shard, 4, direct(paths.depth))
        placed = lax.dynamic_update_slice(
            jnp.zeros((4, width), BF16), vectors, (0, device * shard)
        ).reshape(shard, 128)
        biases = lax.dynamic_update_slice(
            jnp.zeros((hidden,), BF16), up_bias, (device * 4 * shard,)
        ).reshape(shard, 128)
        sent = paths.to_line(
            [
                jnp.concatenate([first[0], placed], axis=1),
                jnp.concatenate([first[1], biases], axis=1),
            ]
        )
        sent, lengths = tie(sent, lengths)
        line = paths.along(sent)
        counts, runs, columns, target_row = places(lengths)
        sel, slot_grad = gather_rows(columns, layer_in, cotangent)
        rest = paths.to_line(
            [jnp.concatenate([rest_of(side, 0), rest_of(side, 1)], axis=1) for side in (0, 1)]
        )
        line, rest, sel, slot_grad, runs, target_row = tie(line, rest, sel, slot_grad, runs, target_row)
        own = paths.gather_halved(line)
        oth = paths.swap_all(own)
        rest = paths.along(rest)
        own, oth, rest, sel = tie(own, oth, rest, sel)
        one_own = paths.gather_direct(rest[:, : 2 * tile])
        two_own = paths.gather_direct(rest[:, 2 * tile :])
    else:
        counts, runs, columns, target_row = places(lengths)
        here = jnp.int32(0)
        lay_one = lay_two = Layout(width, 1, [(0, 0, 0, 0)])
        packed = jnp.concatenate(
            first + [rest_of(side, part) for part in (0, 1) for side in (0, 1)], axis=1
        )
        full = lax.all_gather(packed, AXES, axis=0, tiled=True)
        cuts = [0]
        for n in (half + third,) * 2 + (2 * tile,) * 4:
            cuts.append(cuts[-1] + n)
        own, oth, one_own, one_oth, two_own, two_oth = (
            [full[:, a:b]] for a, b in zip(cuts, cuts[1:])
        )
        every = lax.all_gather(vectors, AXES, axis=1, tiled=True).reshape(-1, 128)
        biases = lax.all_gather(up_bias, AXES, axis=0, tiled=True).reshape(-1, 128)
        own, oth = (
            [jnp.concatenate([p[0], jnp.pad(v, ((0, width - v.shape[0]), (0, 0)))], axis=1)]
            for p, v in ((own, every), (oth, biases))
        )
        sel, slot_grad = gather_rows(columns, layer_in, cotangent)

    where = jnp.stack([here, core]).astype(jnp.int32)
    qkv, att, mid, n2, n2t, g, gt, n1t, stats, vec, bias, ddown_bias = forward_block(
        lay_one, hidden, where, counts, sel, slot_grad, own, oth
    )
    if fast:
        one_own, n2 = tie(one_own, n2)
        one_oth = paths.swap_all(one_own)
    mlp, dn2, d_one_own, d_one_oth, dbias_one = mlp_part(
        lay_two, where, 0, tile, n2, n2t, g, gt, one_own, one_oth, bias
    )
    if fast:
        two_own, mlp, n2 = tie(two_own, mlp, n2)
        two_oth = paths.swap_all(two_own)
        d_one_got = paths.swap(d_one_oth)
    mlp_two, dn2_two, d_two_own, d_two_oth, dbias_two = mlp_part(
        lay_two, where, 1, tile, n2, n2t, g, gt, two_own, two_oth, bias
    )
    if fast:
        d_two_got = paths.swap(d_two_oth)
        d_one_got, mlp_two = tie(d_one_got, mlp_two)
        d_one = paths.chip_sums(d_one_own, d_one_got)
        d_one_plane = paths.send_plane(d_one)
        d_two = paths.chip_sums(d_two_own, d_two_got)
        _, d_two, mlp_two = tie(d_one, d_two, mlp_two)
        d_two_plane = paths.send_plane(d_two)
    dqkv, dattnt, dmid, new_rows, drouter = backward_block(
        lay_one, where, counts, sel, slot_grad, vec, qkv, mid, stats, (mlp, mlp_two, dn2, dn2_two), own, oth
    )
    if fast:
        d_one_plane, dqkv = tie(d_one_plane, dqkv)

    if fast:
        one = paths.sum_plane(d_one[0], d_one_plane)
        one, new_rows = tie(one, new_rows)
        one = paths.along(one)
    layer_out = place_rows(runs, new_rows, target_row, layer_in)
    if fast:
        dqkv, layer_out = tie(dqkv, layer_out)
    proj_oth, proj_own = project_grads(
        where, n1t, dattnt, dqkv, att, dbias_one, dbias_two, ddown_bias, drouter
    )
    if fast:
        one, d_two_plane, proj_oth = tie(one, d_two_plane, proj_oth)
        proj = paths.chip_sums(proj_own, paths.swap(proj_oth))
        two = paths.sum_plane(d_two[0], d_two_plane)
        two, proj, dmid = tie(two, proj, dmid)
        proj_plane = paths.send_plane(proj)
        two = paths.along(two)
    part = seqs // 2
    input_grad = input_rows(
        lay_one, where, runs, sel, slot_grad, vec, stats, dmid, dqkv, target_row, cotangent, own, oth, 0, part
    )
    if fast:
        proj = paths.sum_plane(proj[0], proj_plane)
        two, proj, dmid, input_grad = tie(two, proj, dmid, input_grad)
    input_grad = input_rows(
        lay_one, where, runs, sel, slot_grad, vec, stats, dmid, dqkv, target_row, cotangent, own, oth,
        part, seqs - part, (input_grad,),
    )

    if fast:
        one, two = paths.sum_line(one), paths.sum_line(two)
        proj = paths.sum_line(paths.along(proj))
    else:
        flat = jnp.concatenate(
            [d_one_own, d_one_oth, d_two_own, d_two_oth, proj_own, proj_oth], axis=1
        )
        total = lax.psum_scatter(flat.astype(F32), AXES, scatter_dimension=0, tiled=True)
        p = proj_own.shape[1]
        one = total[:, : 4 * tile].reshape(shard, 2, 2 * tile).transpose(1, 0, 2)
        two = total[:, 4 * tile : 8 * tile].reshape(shard, 2, 2 * tile).transpose(1, 0, 2)
        proj = total[:, 8 * tile :].reshape(shard, 2, p).transpose(1, 0, 2)

    up_grad = jnp.concatenate(
        [v[side, :, :tile] for side in (0, 1) for v in (one, two)], axis=1
    )
    down_grad = jnp.concatenate(
        [v[side, :, tile:] for side in (0, 1) for v in (one, two)], axis=1
    ).T
    in_grad = jnp.stack(
        [proj[side, :, :half].reshape(shard, 3, third) for side in (0, 1)], axis=2
    ).reshape(shard, in_width)
    out_grad = jnp.concatenate([proj[side, :, half : half + third] for side in (0, 1)], axis=1).T
    if fast:
        every, vectors = proj[0, :, half + third :], proj[1, :, half + third :]
    else:
        high = 4 * width // 128
        mine = proj_own[:high, half + third :], proj_oth[:high, half + third :]
        every, vectors = lax.psum(tuple(v.astype(F32) for v in mine), AXES)
    d_up_bias = lax.dynamic_slice(every.reshape(-1), (device * 4 * shard,), (4 * shard,))
    vectors = vectors.reshape(4, width)
    d_down_bias, d_router = (
        lax.dynamic_slice(vectors[k], (device * shard,), (shard,)) for k in (0, 1)
    )
    gain_one = jnp.sum(project_in.astype(F32) * in_grad, axis=1) / first_gain.astype(F32)
    gain_two = jnp.sum(up_weight.astype(F32) * up_grad, axis=1) / second_gain.astype(F32)
    return (
        layer_out,
        input_grad,
        gain_one,
        in_grad,
        out_grad,
        gain_two,
        up_grad,
        d_up_bias,
        down_grad,
        d_down_bias,
        d_router,
    )


def solution(mesh):
    both = ("wide", "narrow")
    rows3, rows2, rows1, cols = P(both, None, None), P(both, None), P(both), P(None, both)
    in_specs = (
        rows3, rows1, rows2, rows2, rows1, rows2, cols, rows1, rows2, rows1, cols, rows1, rows1, rows3,
    )
    out_specs = (rows3, rows3, rows1, rows2, cols, rows1, rows2, rows1, cols, rows1, rows1)
    return jax.shard_map(
        partial(per_device, wide=mesh.shape["wide"], narrow=mesh.shape["narrow"]),
        mesh=mesh,
        in_specs=in_specs,
        out_specs=out_specs,
        check_vma=False,
    )
```

```python
from functools import partial

import jax
import jax.numpy as jnp
import numpy as np
from jax import lax
from jax.experimental import pallas as pl
from jax.experimental.pallas import tpu as pltpu
from jax.sharding import PartitionSpec as P

HEAD_DIM = 64
EPSILON = 1e-06
NEG_FILL = -1e30
F32 = jnp.float32
BF16 = jnp.bfloat16
AXES = ("wide", "narrow")
SCALE = HEAD_DIM**-0.5
GELU_A = 0.7978845608028654
GELU_B = 0.044715
LSE_LANE = 16
MLP_CHUNKS = 4
PAIRS = 3
PLACE_ROWS = 512
ANY = pl.BlockSpec(memory_space=pl.ANY)
VMEM_LIMIT = 67043328


def dot(left, right, left_dim=1, right_dim=0):
    return lax.dot_general(
        left, right, (((left_dim,), (right_dim,)), ((), ())), preferred_element_type=F32
    )


def params(*semantics):
    return pltpu.CompilerParams(
        dimension_semantics=semantics or None, vmem_limit_bytes=VMEM_LIMIT
    )


def whole(shape):
    return pl.BlockSpec(shape, lambda *_: (0,) * len(shape))


def cost(flops, bytes_accessed):
    return pl.CostEstimate(
        flops=int(flops), bytes_accessed=int(bytes_accessed), transcendentals=0
    )


class Layout:
    def __init__(self, height, plane, blocks):
        self.height, self.plane, self.blocks = height, plane, tuple(blocks)
        self.pieces = 1 + max(piece for piece, *_ in blocks)
        self.depth = len(blocks) // plane

    def natural(self, here, step, line):
        return pl.multiple_of((line * self.plane + (here ^ step)) * self.height, 8)


def load_rows(layout, here, pieces, target, sems, source, columns):
    height = layout.height
    return [
        pltpu.make_async_copy(
            pieces[piece].at[pl.ds(at * height, height), source],
            target.at[pl.ds(layout.natural(here, step, line), height), columns],
            sems.at[j],
        )
        for j, (piece, at, step, line) in enumerate(layout.blocks)
    ]


def both_halves(layout, here, own, oth, target, sems, start, count):
    source = pl.ds(start, count)
    return load_rows(layout, here, own, target, sems.at[0], source, pl.ds(0, count)) + load_rows(
        layout, here, oth, target, sems.at[1], source, pl.ds(count, count)
    )


def store_rows(layout, target, value):
    height = layout.height
    for line in range(layout.depth):
        for owner in range(layout.plane):
            start = (owner * layout.depth + line) * height
            c = line * layout.plane + owner
            target[start : start + height, :] = value[c * height : (c + 1) * height, :]


def gather_kernel(target, x, cot, sel, grad):
    length = x.shape[1]
    places = lax.broadcasted_iota(jnp.int32, (target.shape[1], length), 1)
    chosen = jnp.where(target[0] == places, 1.0, 0.0).astype(BF16)
    sel[...] = dot(chosen, x[0]).astype(BF16)
    grad[...] = dot(chosen, cot[0]).astype(BF16)


def gather_rows(target, layer_in, cotangent):
    seqs, length, width = layer_in.shape
    slots = target.shape[1]
    big = pl.BlockSpec((1, length, width), lambda b: (b, 0, 0))
    out = pl.BlockSpec((slots, width), lambda b: (b, 0))
    return pl.pallas_call(
        gather_kernel,
        grid=(seqs,),
        in_specs=[pl.BlockSpec((1, slots, 1), lambda b: (b, 0, 0)), big, big],
        out_specs=[out, out],
        out_shape=[jax.ShapeDtypeStruct((seqs * slots, width), BF16)] * 2,
        compiler_params=params("arbitrary"),
        cost_estimate=cost(
            4 * seqs * slots * length * width, 4 * seqs * length * width
        ),
        name="gather_rows",
    )(target, layer_in, cotangent)


def allowed_keys(slots, valid):
    rows = lax.broadcasted_iota(jnp.int32, (2 * slots, slots), 0)
    rows = jnp.where(rows >= slots, rows - slots, rows)
    keys = lax.broadcasted_iota(jnp.int32, (2 * slots, slots), 1)
    return (keys <= rows) & (keys < valid)


def split_pair(pair):
    lane = lax.broadcasted_iota(jnp.int32, pair.shape, 1)
    zero = jnp.zeros_like(pair)
    first = lane < HEAD_DIM
    return jnp.concatenate(
        [jnp.where(first, pair, zero), jnp.where(first, zero, pair)], axis=0
    )


def join_pair(stacked):
    half = stacked.shape[0] // 2
    lane = lax.broadcasted_iota(jnp.int32, (half, stacked.shape[1]), 1)
    return jnp.where(lane < HEAD_DIM, stacked[:half], stacked[half:])


def pair_loop(pairs, body, carry):
    def step(k, carry):
        for p in range(PAIRS):
            carry = body(k * PAIRS + p, carry)
        return carry

    return lax.fori_loop(0, pairs // PAIRS, step, carry)


def pair_columns(pair, half_width):
    per_half = half_width // (2 * HEAD_DIM)
    base = (pair // per_half) * 3 * half_width + (pair % per_half) * 2 * HEAD_DIM
    return tuple(
        pl.ds(pl.multiple_of(base + k * half_width, 128), 2 * HEAD_DIM) for k in range(3)
    )


def forward_kernel(
    where, counts, sel, grad, *rest, layout, half, third
):
    own, oth = rest[: layout.pieces], rest[layout.pieces : 2 * layout.pieces]
    (
    qkv, att, mid, n2, n2t, g, gt, n1t, stats, vec, bias, gsum,
    w_in, w_out, w_ext, sem_in, sem_out, sem_ext,
    ) = rest[2 * layout.pieces :]
    b = pl.program_id(0)
    slots, width = sel.shape
    here = where[0]

    def in_copies():
        return both_halves(layout, here, own, oth, w_in, sem_in, 0, half)

    def out_copies():
        return both_halves(layout, here, own, oth, w_out, sem_out, half, third)

    @pl.when(b == 0)
    def _():
        small = both_halves(layout, here, own, oth, w_ext, sem_ext, half + third, 128)
        first = in_copies()
        for c in small + first + out_copies():
            c.start()
        for c in small:
            c.wait()
        per = width // 128
        high = 4 * per
        total = sum(w_ext[k * high : (k + 1) * high, :].astype(F32) for k in range(width // high))
        mine, others = total[:, :128], total[:, 128:]
        vectors = jnp.where(where[1] == 0, mine, others)
        biases = jnp.where(where[1] == 0, others, mine)
        vec[...] = jnp.zeros_like(vec)
        for v in range(4):
            for k in range(per):
                vec[v : v + 1, k * 128 : (k + 1) * 128] = vectors[v * per + k : v * per + k + 1, :]
        for k in range(bias.shape[1] // 128):
            bias[0:1, k * 128 : (k + 1) * 128] = biases[k : k + 1, :]
        for c in first:
            c.wait()

    x = sel[...].astype(F32)
    r1 = lax.rsqrt(jnp.mean(x * x, axis=-1, keepdims=True) + EPSILON)
    n1 = (x * r1 * vec[0:1, :]).astype(BF16)
    logit = jnp.sum(x * vec[3:4, :], axis=-1, keepdims=True)
    rate = jax.nn.sigmoid(logit)
    d_mlp = (rate * grad[...].astype(F32)).astype(BF16)
    g[...] = d_mlp
    gsum_now = jnp.sum(d_mlp.astype(F32), axis=0, keepdims=True)

    @pl.when(b == 0)
    def _():
        gsum[...] = gsum_now

    @pl.when(b > 0)
    def _():
        gsum[...] += gsum_now

    store_rows(layout, gt, d_mlp.T)
    store_rows(layout, n1t, n1.T)
    qkv[...] = dot(n1, w_in[...]).astype(BF16)

    allowed = allowed_keys(slots, counts[b])
    lane = lax.broadcasted_iota(jnp.int32, (slots, 128), 1)
    kept = jnp.where(lane == 0, r1, jnp.where(lane == 1, rate, 0.0))

    def attend(pair, kept):
        qc, kc, vc = pair_columns(pair, width // 2)
        scores = dot(split_pair(qkv[:, qc] * SCALE), qkv[:, kc], 1, 1)
        scores = jnp.where(allowed, scores, NEG_FILL)
        top = jnp.max(scores, axis=-1, keepdims=True)
        exps = jnp.exp(scores - top)
        total = jnp.sum(exps, axis=-1, keepdims=True)
        lse = top + jnp.log(total)
        probs = (exps * (1.0 / total)).astype(BF16)
        here_now = pl.ds(pl.multiple_of(pair * 128, 128), 128)
        att[:, here_now] = join_pair(dot(probs, qkv[:, vc])).astype(BF16)
        kept = jnp.where(lane == LSE_LANE + 2 * pair, lse[:slots], kept)
        return jnp.where(lane == LSE_LANE + 2 * pair + 1, lse[slots:], kept)

    kept = pair_loop(width // (2 * HEAD_DIM), attend, kept)

    @pl.when(b == 0)
    def _():
        for c in out_copies():
            c.wait()

    stream = x + dot(att[...], w_out[...], 1, 1)
    mid[...] = stream
    r2 = lax.rsqrt(jnp.mean(stream * stream, axis=-1, keepdims=True) + EPSILON)
    normed = (stream * r2 * vec[1:2, :]).astype(BF16)
    n2[...] = normed
    store_rows(layout, n2t, normed.T)
    stats[...] = jnp.where(lane == 2, r2, kept)


def forward_block(layout, hidden, where, counts, sel, grad, own, oth):
    rows, width = sel.shape
    seqs = counts.shape[0]
    slots = rows // seqs
    blocks = len(layout.blocks)
    row = lambda w: pl.BlockSpec((slots, w), lambda b, *_: (b, 0))
    col = pl.BlockSpec((width, slots), lambda b, *_: (0, b))
    shape = jax.ShapeDtypeStruct
    return pl.pallas_call(
        partial(forward_kernel, layout=layout, half=3 * width // 2, third=width // 2),
        grid_spec=pltpu.PrefetchScalarGridSpec(
            num_scalar_prefetch=2,
            grid=(seqs,),
            in_specs=[row(width), row(width)] + [ANY] * (2 * layout.pieces),
            out_specs=[
                row(3 * width), row(width), row(width), row(width), col, row(width), col, col, row(128),
                whole((8, width)), whole((1, hidden)), whole((1, width)),
            ],
            scratch_shapes=[
                pltpu.VMEM((width, 3 * width), BF16),
                pltpu.VMEM((width, width), BF16),
                pltpu.VMEM((width, 256), BF16),
                pltpu.SemaphoreType.DMA((2, blocks)),
                pltpu.SemaphoreType.DMA((2, blocks)),
                pltpu.SemaphoreType.DMA((2, blocks)),
            ],
        ),
        out_shape=[
            shape((rows, 3 * width), BF16),
            shape((rows, width), BF16),
            shape((rows, width), F32),
            shape((rows, width), BF16),
            shape((width, rows), BF16),
            shape((rows, width), BF16),
            shape((width, rows), BF16),
            shape((width, rows), BF16),
            shape((rows, 128), F32),
            shape((8, width), F32),
            shape((1, hidden), F32),
            shape((1, width), F32),
        ],
        compiler_params=params("arbitrary"),
        cost_estimate=cost(10 * rows * width * width, 30 * rows * width),
        name="forward_block",
    )(where, counts, sel, grad, *own, *oth)


def mlp_kernel(where, bias, *rest, layout, tile):
    rows_in = rest[:4]
    own, oth = rest[4 : 4 + layout.pieces], rest[4 + layout.pieces : 4 + 2 * layout.pieces]
    mlp, dn2, d_own, d_oth, dbias, *held, w_up, w_down, d_first, act, d_pre, sem_rows, sems, sem_out = rest[
        4 + 2 * layout.pieces :
    ]
    n2, n2t, g, gt, mlp_sum, dn2_sum = held
    i = pl.program_id(0)
    here = where[0]
    row_copies = [
        pltpu.make_async_copy(rows_in[k], held[k], sem_rows.at[k]) for k in range(4)
    ]
    out_copy = pltpu.make_async_copy(d_first, d_own, sem_out)

    def copies(side, kind):
        source, target = (own, oth)[side], (w_up, w_down)[kind].at[side]
        return load_rows(
            layout, here, source, target, sems.at[side, kind], pl.ds(kind * tile, tile), pl.ds(0, tile)
        )

    def wait_first(*waited):
        @pl.when(i == 0)
        def _():
            for c in waited:
                c.wait()

    @pl.when(i == 0)
    def _():
        started = copies(0, 0) + row_copies[:1] + copies(0, 1) + row_copies[2:3]
        started = started + row_copies[1:2] + row_copies[3:] + copies(1, 0) + copies(1, 1)
        for c in started:
            c.start()

    wait_first(*copies(0, 0), row_copies[0])

    @pl.when(i == 1)
    def _():
        out_copy.start()
        for c in copies(1, 0) + copies(1, 1):
            c.wait()

    wait_first(*copies(0, 1), row_copies[2])
    up_now = w_up.at[i]
    down_now = w_down.at[i]
    rows = n2.shape[0] // MLP_CHUNKS

    def chunk(c, total):
        here = pl.ds(pl.multiple_of(c * rows, rows), rows)
        pre = dot(n2[here, :], up_now[...]) + bias[...]
        square = pre * pre
        th = jnp.tanh(pre * (GELU_A + GELU_A * GELU_B * square))
        half = 0.5 * (1.0 + th)
        act_now = (pre * half).astype(BF16)
        act[here, :] = act_now
        slope = half + 0.5 * pre * (1.0 - th * th) * (GELU_A + 3 * GELU_A * GELU_B * square)
        d_pre_now = (slope * dot(g[here, :], down_now[...])).astype(BF16)
        d_pre[here, :] = d_pre_now
        mlp_now = jnp.where(i == 0, 0.0, mlp_sum[here, :]) + dot(act_now, down_now[...], 1, 1)
        mlp_sum[here, :] = mlp_now
        mlp[here, :] = mlp_now.astype(BF16)
        dn2_now = jnp.where(i == 0, 0.0, dn2_sum[here, :]) + dot(d_pre_now, up_now[...], 1, 1)
        dn2_sum[here, :] = dn2_now
        dn2[here, :] = dn2_now.astype(BF16)
        return total + jnp.sum(d_pre_now.astype(F32), axis=0, keepdims=True)

    dbias[...] = lax.fori_loop(0, MLP_CHUNKS, chunk, jnp.zeros_like(dbias))
    wait_first(row_copies[1], row_copies[3])
    dup = dot(n2t[...], d_pre[...]).astype(BF16)
    ddown = dot(gt[...], act[...]).astype(BF16)

    @pl.when(i == 0)
    def _():
        d_first[:, :tile] = dup
        d_first[:, tile:] = ddown

    @pl.when(i == 1)
    def _():
        d_oth[:, :tile] = dup
        d_oth[:, tile:] = ddown
        out_copy.wait()


def mlp_part(layout, where, part, tile, n2, n2t, g, gt, own, oth, bias):
    rows, width = n2.shape
    parts = bias.shape[1] // (2 * tile)
    blocks = len(layout.blocks)
    shape = jax.ShapeDtypeStruct
    return pl.pallas_call(
        partial(mlp_kernel, layout=layout, tile=tile),
        grid_spec=pltpu.PrefetchScalarGridSpec(
            num_scalar_prefetch=1,
            grid=(2,),
            in_specs=[
                pl.BlockSpec((1, tile), lambda i, where: (0, (where[1] ^ i) * parts + part)),
            ] + [ANY] * (4 + 2 * layout.pieces),
            out_specs=[
                whole((rows, width)), whole((rows, width)), ANY, whole((width, 2 * tile)),
                pl.BlockSpec((1, tile), lambda i, where: (0, i)),
            ],
            scratch_shapes=[
                pltpu.VMEM((rows, width), BF16),
                pltpu.VMEM((width, rows), BF16),
                pltpu.VMEM((rows, width), BF16),
                pltpu.VMEM((width, rows), BF16),
                pltpu.VMEM((rows, width), F32),
                pltpu.VMEM((rows, width), F32),
                pltpu.VMEM((2, width, tile), BF16),
                pltpu.VMEM((2, width, tile), BF16),
                pltpu.VMEM((width, 2 * tile), BF16),
                pltpu.VMEM((rows, tile), BF16),
                pltpu.VMEM((rows, tile), BF16),
                pltpu.SemaphoreType.DMA((4,)),
                pltpu.SemaphoreType.DMA((2, 2, blocks)),
                pltpu.SemaphoreType.DMA,
            ],
        ),
        out_shape=[
            shape((rows, width), BF16),
            shape((rows, width), BF16),
            shape((width, 2 * tile), BF16),
            shape((width, 2 * tile), BF16),
            shape((1, 2 * tile), F32),
        ],
        compiler_params=params("arbitrary"),
        cost_estimate=cost(24 * rows * width * tile, 8 * rows * width),
        name="mlp_part",
    )(where, bias, n2, n2t, g, gt, *own, *oth)


def norm_pull(values, inverse, scaled):
    return inverse * scaled - values * (
        inverse * inverse * inverse * jnp.mean(scaled * values, axis=-1, keepdims=True)
    )


def backward_kernel(
    where, counts, sel, grad, vec, qkv, mid, stats, mlp, mlp_two, dn2, dn2_two, *rest, layout, half, third
):
    own, oth = rest[: layout.pieces], rest[layout.pieces : 2 * layout.pieces]
    dqkv, dattnt, dmid, new_rows, drouter, w_out, d_att, sem_out = rest[2 * layout.pieces :]
    b = pl.program_id(0)
    slots, width = sel.shape
    here = where[0]

    @pl.when(b == 0)
    def _():
        copies = both_halves(layout, here, own, oth, w_out, sem_out, half, third)
        for c in copies:
            c.start()
        for c in copies:
            c.wait()

    x = sel[...].astype(F32)
    stream = mid[...]
    rate = stats[:, 1:2]
    r2 = stats[:, 2:3]
    slot_grad = grad[...].astype(F32)
    branch = (stream - x) + (mlp[...].astype(F32) + mlp_two[...].astype(F32) + vec[2:3, :])
    new_rows[...] = (x + rate * branch).astype(BF16)
    d_logit = jnp.sum(slot_grad * branch, axis=-1, keepdims=True) * (rate * (1.0 - rate))
    router_now = jnp.sum(d_logit * x, axis=0, keepdims=True)

    @pl.when(b == 0)
    def _():
        drouter[...] = router_now

    @pl.when(b > 0)
    def _():
        drouter[...] += router_now

    d_mid = norm_pull(stream, r2, vec[1:2, :] * (dn2[...].astype(F32) + dn2_two[...].astype(F32)))
    dmid[...] = d_mid + d_logit * vec[3:4, :]
    d_attn = (rate * slot_grad + d_mid).astype(BF16)
    store_rows(layout, dattnt, d_attn.T)
    d_att[...] = dot(d_attn, w_out[...]).astype(BF16)

    allowed = allowed_keys(slots, counts[b])
    lane = lax.broadcasted_iota(jnp.int32, (slots, 128), 1)

    def pull(pair, carry):
        qc, kc, vc = pair_columns(pair, width // 2)
        queries = split_pair(qkv[:, qc] * SCALE)
        keys = qkv[:, kc]
        lse = jnp.concatenate(
            [
                jnp.sum(jnp.where(lane == LSE_LANE + 2 * pair + k, stats[...], 0.0), axis=-1, keepdims=True)
                for k in (0, 1)
            ],
            axis=0,
        )
        upstream = split_pair(d_att[:, pl.ds(pl.multiple_of(pair * 128, 128), 128)])
        scores = dot(queries, keys, 1, 1)
        probs = jnp.exp(jnp.where(allowed, scores - lse, NEG_FILL))
        d_probs = dot(upstream, qkv[:, vc], 1, 1)
        d_scores = (probs * (d_probs - jnp.sum(probs * d_probs, axis=-1, keepdims=True))).astype(BF16)
        dqkv[:, qc] = (join_pair(dot(d_scores, keys)) * SCALE).astype(BF16)
        dqkv[:, kc] = dot(d_scores, queries, 0, 0).astype(BF16)
        dqkv[:, vc] = dot(probs.astype(BF16), upstream, 0, 0).astype(BF16)
        return carry

    pair_loop(width // (2 * HEAD_DIM), pull, 0)


def backward_block(layout, where, counts, sel, grad, vec, qkv, mid, stats, sums, own, oth):
    rows, width = sel.shape
    seqs = counts.shape[0]
    slots = rows // seqs
    blocks = len(layout.blocks)
    row = lambda w: pl.BlockSpec((slots, w), lambda b, *_: (b, 0))
    col = pl.BlockSpec((width, slots), lambda b, *_: (0, b))
    shape = jax.ShapeDtypeStruct
    return pl.pallas_call(
        partial(backward_kernel, layout=layout, half=3 * width // 2, third=width // 2),
        grid_spec=pltpu.PrefetchScalarGridSpec(
            num_scalar_prefetch=2,
            grid=(seqs,),
            in_specs=[
                row(width), row(width), whole(vec.shape), row(3 * width), row(width), row(128),
            ] + [row(width)] * 4 + [ANY] * (2 * layout.pieces),
            out_specs=[row(3 * width), col, row(width), row(width), whole((1, width))],
            scratch_shapes=[
                pltpu.VMEM((width, width), BF16),
                pltpu.VMEM((slots, width), BF16),
                pltpu.SemaphoreType.DMA((2, blocks)),
            ],
        ),
        out_shape=[
            shape((rows, 3 * width), BF16),
            shape((width, rows), BF16),
            shape((rows, width), F32),
            shape((rows, width), BF16),
            shape((1, width), F32),
        ],
        compiler_params=params("arbitrary"),
        cost_estimate=cost(2 * 20 * rows * width * width, 2 * 30 * rows * width),
        name="backward_block",
    )(where, counts, sel, grad, vec, qkv, mid, stats, *sums, *own, *oth)


def project_kernel(where, n1t, dattnt, dqkv, att, dbias_one, dbias_two, ddown, drouter, oth, own):
    half = dqkv.shape[1]
    third = att.shape[1]
    width = n1t.shape[0]
    high, tile = 4 * width // 128, dbias_one.shape[1] // 2
    in_now = dot(n1t[...], dqkv[...]).astype(BF16)
    out_now = dot(dattnt[...], att[...]).astype(BF16)
    first_core = where[1] == 0

    def bias_rows():
        rows = []
        for side in (0, 1):
            for part in (dbias_one, dbias_two):
                for k in range(tile // 128):
                    a, b = side * tile + k * 128, (1 - side) * tile + k * 128
                    rows.append(jnp.where(first_core, part[:, a : a + 128], part[:, b : b + 128]))
        return rows

    def vector_rows():
        rows = [v[:, k * 128 : (k + 1) * 128] for v in (ddown, drouter) for k in range(width // 128)]
        return rows + [jnp.zeros((1, 128), F32)] * (high - len(rows))

    def store(out, is_first):
        out[:, :half] = in_now
        out[:, half : half + third] = out_now
        small = jnp.where(
            is_first, jnp.concatenate(bias_rows(), axis=0), jnp.concatenate(vector_rows(), axis=0)
        )
        small = jnp.concatenate([small] * 2, axis=0).astype(BF16)
        for k in range(width // (2 * high)):
            out[2 * k * high : 2 * (k + 1) * high, half + third :] = small

    pl.when(pl.program_id(0) == 0)(lambda: store(oth, where[1] == 1))
    pl.when(pl.program_id(0) == 1)(lambda: store(own, where[1] == 0))


def project_grads(where, n1t, dattnt, dqkv, att, *vectors):
    width, rows = n1t.shape
    half, third = dqkv.shape[1] // 2, att.shape[1] // 2
    total = half + third + 128
    return pl.pallas_call(
        project_kernel,
        grid_spec=pltpu.PrefetchScalarGridSpec(
            num_scalar_prefetch=1,
            grid=(2,),
            in_specs=[
                whole((width, rows)), whole((width, rows)),
                pl.BlockSpec((rows, half), lambda i, where: (0, 1 - i)),
                pl.BlockSpec((rows, third), lambda i, where: (0, 1 - i)),
            ] + [whole(v.shape) for v in vectors],
            out_specs=[whole((width, total))] * 2,
        ),
        out_shape=[jax.ShapeDtypeStruct((width, total), BF16)] * 2,
        compiler_params=params("arbitrary"),
        cost_estimate=cost(2 * 4 * width * rows * total, 2 * 4 * width * rows),
        name="project_grads",
    )(where, n1t, dattnt, dqkv, att, *vectors)


def place(out, rows, target, x, start, count):
    chunk = min(PLACE_ROWS, x.shape[1])

    def one(c, carry):
        here = pl.ds(pl.multiple_of(c * chunk, chunk), chunk)
        places = lax.broadcasted_iota(jnp.int32, (chunk, target.shape[2]), 0) + c * chunk
        hits = target[0] == places
        moved = dot(jnp.where(hits, 1.0, 0.0).astype(BF16), rows[...])
        hit = jnp.max(jnp.where(hits, 1.0, 0.0), axis=-1, keepdims=True)
        at = lax.broadcasted_iota(jnp.int32, (chunk, 1), 0) + c * chunk
        kept = (at >= start) & (at < start + count) & (hit < 0.5)
        out[0, here, :] = jnp.where(kept, x[0, here, :].astype(F32), moved).astype(BF16)
        return carry

    lax.fori_loop(0, x.shape[1] // chunk, one, 0)


def out_kernel(runs, rows, target, x, out):
    b = pl.program_id(0)
    place(out, rows, target, x, runs[0, b], runs[1, b])


def place_rows(runs, rows, target, x):
    seqs, length, width = x.shape
    slots = target.shape[2]
    big = pl.BlockSpec((1, length, width), lambda b, *_: (b, 0, 0))
    return pl.pallas_call(
        out_kernel,
        grid_spec=pltpu.PrefetchScalarGridSpec(
            num_scalar_prefetch=1,
            grid=(seqs,),
            in_specs=[
                pl.BlockSpec((slots, width), lambda b, *_: (b, 0)),
                pl.BlockSpec((1, 1, slots), lambda b, *_: (b, 0, 0)),
                big,
            ],
            out_specs=big,
        ),
        out_shape=jax.ShapeDtypeStruct(x.shape, BF16),
        compiler_params=params("arbitrary"),
        cost_estimate=cost(2 * seqs * slots * length * width, 4 * seqs * length * width),
        name="place_rows",
    )(runs, rows, target, x)


def input_kernel(
    where, runs, sel, grad, vec, stats, dmid, dqkv, target, x, *rest, layout, first
):
    own, oth = rest[: layout.pieces], rest[layout.pieces : 2 * layout.pieces]
    *_, out, w_in, moved, sem_in = rest[2 * layout.pieces :]
    b = pl.program_id(0)

    @pl.when(b == 0)
    def _():
        copies = both_halves(layout, where[0], own, oth, w_in, sem_in, 0, w_in.shape[1] // 2)
        for c in copies:
            c.start()
        for c in copies:
            c.wait()

    d_normed = dot(dqkv[...], w_in[...], 1, 1)
    d_sel = norm_pull(sel[...].astype(F32), stats[:, 0:1], vec[0:1, :] * d_normed) + dmid[...]
    moved[...] = (grad[...].astype(F32) + d_sel).astype(BF16)
    place(out, moved, target, x, runs[0, first + b], runs[1, first + b])


def input_rows(layout, where, runs, sel, grad, vec, stats, dmid, dqkv, target, x, own, oth, first, count, begun=()):
    seqs, length, width = x.shape
    slots = target.shape[2]
    blocks = len(layout.blocks)
    row = lambda w: pl.BlockSpec((slots, w), lambda b, *_: (first + b, 0))
    big = pl.BlockSpec((1, length, width), lambda b, *_: (first + b, 0, 0))
    return pl.pallas_call(
        partial(input_kernel, layout=layout, first=first),
        grid_spec=pltpu.PrefetchScalarGridSpec(
            num_scalar_prefetch=2,
            grid=(count,),
            in_specs=[
                row(width), row(width), whole(vec.shape), row(128), row(width), row(3 * width),
                pl.BlockSpec((1, 1, slots), lambda b, *_: (first + b, 0, 0)),
                big,
            ] + [ANY] * (2 * layout.pieces + len(begun)),
            out_specs=big,
            scratch_shapes=[
                pltpu.VMEM((width, 3 * width), BF16),
                pltpu.VMEM((slots, width), BF16),
                pltpu.SemaphoreType.DMA((2, blocks)),
            ],
        ),
        out_shape=jax.ShapeDtypeStruct(x.shape, BF16),
        compiler_params=params("arbitrary"),
        cost_estimate=cost(1, 1),
        input_output_aliases={10 + 2 * layout.pieces: 0} if begun else {},
        name="input_rows",
    )(where, runs, sel, grad, vec, stats, dmid, dqkv, target, x, *own, *oth, *begun)


class Paths:
    def __init__(self, wide, narrow, here):
        self.wide, self.narrow, self.depth, self.here = wide, narrow, wide // 2, here
        ids = np.arange(wide * narrow).reshape(self.depth, 4, 2)
        self.lines = ids.transpose(1, 0, 2).reshape(4, -1).tolist()
        self.planes = ids.transpose(0, 2, 1).reshape(-1, 4).tolist()

    def swap(self, value):
        return lax.ppermute(value, "narrow", [(i, i ^ 1) for i in range(self.narrow)])

    def over(self, value, step):
        if step == 1:
            return lax.ppermute(value, "narrow", [(i, i ^ 2) for i in range(self.narrow)])
        if step == 2:
            return lax.ppermute(value, "wide", [(i, i ^ 1) for i in range(self.wide)])
        mask = self.narrow ^ 2
        return lax.ppermute(value, AXES, [(i, i ^ mask) for i in range(self.wide * self.narrow)])

    def along(self, value):
        return lax.all_to_all(value, AXES, 0, 0, axis_index_groups=self.lines, tiled=True)

    def to_line(self, halves):
        shard, cols = halves[0].shape
        sent = jnp.broadcast_to(jnp.stack(halves)[None], (self.depth, 2, shard, cols))
        return sent.reshape(self.depth * 2 * shard, cols)

    def gather_halved(self, held):
        near_x, near_y = self.over(held, 1), self.over(held, 2)
        mid = held.shape[0] // 2
        return [held, near_x, near_y, self.over(near_y[:mid], 1), self.over(near_x[mid:], 2)]

    def gather_direct(self, held):
        return [held] + [self.over(held, step) for step in (1, 2, 3)]

    def swap_all(self, pieces):
        return [self.swap(p) for p in pieces]

    def chip_sums(self, own, got):
        rows = own.shape[0] // 4
        starts = [(self.here ^ step) * rows for step in range(4)]
        return [
            add_halves(
                lax.dynamic_slice(own, (start, 0), (rows, own.shape[1])),
                lax.dynamic_slice(got, (start, 0), (rows, own.shape[1])),
            )
            for start in starts
        ]

    def exchange_plane(self, both):
        return lax.all_to_all(both, AXES, 0, 0, axis_index_groups=self.planes, tiled=True)

    def send_plane(self, sums):
        return [self.over(sums[step], step) for step in (1, 2, 3)]

    def sum_plane(self, mine, got):
        total = mine.astype(F32)
        for v in got:
            total = total + v.astype(F32)
        return total.astype(BF16)

    def sum_line(self, got):
        return jnp.sum(got.reshape(self.depth, 2, -1, got.shape[1]).astype(F32), axis=0)


def halved(depth):
    return [(piece, z, piece, z) for piece in range(3) for z in range(depth)] + [
        (3 + (z >= depth // 2), z % (depth // 2), 3, z) for z in range(depth)
    ]


def direct(depth):
    return [(piece, z, piece, z) for piece in range(4) for z in range(depth)]


def add_halves(own, got):
    return (own.astype(F32) + got.astype(F32)).astype(BF16)


def tie(*values):
    return lax.optimization_barrier(values)


def per_device(
    layer_in,
    lengths,
    padding,
    picked,
    first_gain,
    project_in,
    project_out,
    second_gain,
    up_weight,
    up_bias,
    down_weight,
    down_bias,
    router,
    cotangent,
    *,
    wide,
    narrow,
):
    seqs, slots = picked.shape
    shard, in_width = project_in.shape
    width = in_width // 3
    hidden = up_weight.shape[1]
    devices = wide * narrow
    half = 3 * width // 2
    third = width // 2
    tile = hidden // 4
    fast = shard == 24 and wide % 4 == 0 and narrow == 4
    core = lax.axis_index("narrow") & 1 if fast else jnp.int32(0)
    device = lax.axis_index("wide") * narrow + lax.axis_index("narrow")

    in_split = project_in.reshape(shard, 3, 2, third)
    in_halves = [in_split[:, :, side].reshape(shard, half) for side in (0, 1)]
    out_t = project_out.T
    down_t = down_weight.T
    vectors = jnp.stack([first_gain, second_gain, down_bias, router])

    first = [
        jnp.concatenate([in_halves[side], out_t[:, side * third : (side + 1) * third]], axis=1)
        for side in (0, 1)
    ]

    def rest_of(side, part):
        at = (2 * side + part) * tile
        return jnp.concatenate([up_weight[:, at : at + tile], down_t[:, at : at + tile]], axis=1)

    def places(lengths):
        counts = lengths // 8
        valid = jnp.arange(slots)[None, :] < counts[:, None]
        target = jnp.where(valid, picked, -1)
        runs = jnp.stack([jnp.argmax(padding, axis=1).astype(jnp.int32), lengths])
        return counts, runs, target[:, :, None], target[:, None, :]

    if fast:
        here = (lax.axis_index("wide") & 1) * 2 + (lax.axis_index("narrow") >> 1)
        paths = Paths(wide, narrow, here)
        lay_one = Layout(2 * shard, 4, halved(paths.depth))
        lay_two = Layout(2 * shard, 4, direct(paths.depth))
        placed = lax.dynamic_update_slice(
            jnp.zeros((4, width), BF16), vectors, (0, device * shard)
        ).reshape(shard, 128)
        biases = lax.dynamic_update_slice(
            jnp.zeros((hidden,), BF16), up_bias, (device * 4 * shard,)
        ).reshape(shard, 128)
        sent = paths.to_line(
            [
                jnp.concatenate([first[0], placed], axis=1),
                jnp.concatenate([first[1], biases], axis=1),
            ]
        )
        sent, lengths = tie(sent, lengths)
        line = paths.along(sent)
        counts, runs, columns, target_row = places(lengths)
        rest = paths.to_line(
            [jnp.concatenate([rest_of(side, 0), rest_of(side, 1)], axis=1) for side in (0, 1)]
        )
        rest, columns = tie(rest, columns)
        sel, slot_grad = gather_rows(columns, layer_in, cotangent)
        line, rest, sel, slot_grad, runs, target_row = tie(line, rest, sel, slot_grad, runs, target_row)
        own = paths.gather_halved(line)
        oth = paths.swap_all(own)
        rest = paths.along(rest)
        own, oth, rest, sel = tie(own, oth, rest, sel)
        one_own = paths.gather_direct(rest[:, : 2 * tile])
        two_own = paths.gather_direct(rest[:, 2 * tile :])
    else:
        counts, runs, columns, target_row = places(lengths)
        here = jnp.int32(0)
        lay_one = lay_two = Layout(width, 1, [(0, 0, 0, 0)])
        packed = jnp.concatenate(
            first + [rest_of(side, part) for part in (0, 1) for side in (0, 1)], axis=1
        )
        full = lax.all_gather(packed, AXES, axis=0, tiled=True)
        cuts = [0]
        for n in (half + third,) * 2 + (2 * tile,) * 4:
            cuts.append(cuts[-1] + n)
        own, oth, one_own, one_oth, two_own, two_oth = (
            [full[:, a:b]] for a, b in zip(cuts, cuts[1:])
        )
        every = lax.all_gather(vectors, AXES, axis=1, tiled=True).reshape(-1, 128)
        biases = lax.all_gather(up_bias, AXES, axis=0, tiled=True).reshape(-1, 128)
        own, oth = (
            [jnp.concatenate([p[0], jnp.pad(v, ((0, width - v.shape[0]), (0, 0)))], axis=1)]
            for p, v in ((own, every), (oth, biases))
        )
        sel, slot_grad = gather_rows(columns, layer_in, cotangent)

    where = jnp.stack([here, core]).astype(jnp.int32)
    qkv, att, mid, n2, n2t, g, gt, n1t, stats, vec, bias, ddown_bias = forward_block(
        lay_one, hidden, where, counts, sel, slot_grad, own, oth
    )
    if fast:
        one_own, n2 = tie(one_own, n2)
        one_oth = paths.swap_all(one_own)
    mlp, dn2, d_one_own, d_one_oth, dbias_one = mlp_part(
        lay_two, where, 0, tile, n2, n2t, g, gt, one_own, one_oth, bias
    )
    if fast:
        two_own, mlp, n2 = tie(two_own, mlp, n2)
        two_oth = paths.swap_all(two_own)
        d_one_got = paths.swap(d_one_oth)
    mlp_two, dn2_two, d_two_own, d_two_oth, dbias_two = mlp_part(
        lay_two, where, 1, tile, n2, n2t, g, gt, two_own, two_oth, bias
    )
    if fast:
        d_one_got, mlp_two = tie(d_one_got, mlp_two)
        d_one = paths.chip_sums(d_one_own, d_one_got)
        d_one_plane = paths.send_plane(d_one)
        d_two = add_halves(d_two_own, paths.swap(d_two_oth))
        d_two, mlp_two = tie(d_two, mlp_two)
        d_two = paths.exchange_plane(d_two)
    dqkv, dattnt, dmid, new_rows, drouter = backward_block(
        lay_one, where, counts, sel, slot_grad, vec, qkv, mid, stats, (mlp, mlp_two, dn2, dn2_two), own, oth
    )

    proj_oth, proj_own = project_grads(
        where, n1t, dattnt, dqkv, att, dbias_one, dbias_two, ddown_bias, drouter
    )
    if fast:
        d_one_plane, d_two, proj_oth = tie(d_one_plane, d_two, proj_oth)
        proj_got = paths.swap(proj_oth)
        proj = paths.chip_sums(proj_own, proj_got)
        d_two = d_two.reshape(4, -1, 2 * tile)
        sums = jnp.concatenate(
            [paths.sum_plane(d_one[0], d_one_plane), paths.sum_plane(d_two[0], list(d_two[1:]))], axis=1
        )
        sums, proj, new_rows = tie(sums, proj, new_rows)
        proj_plane = paths.send_plane(proj)
        sums = paths.along(sums)
    layer_out = place_rows(runs, new_rows, target_row, layer_in)
    if fast:
        dmid, layer_out = tie(dmid, layer_out)
    part = seqs // 2
    input_grad = input_rows(
        lay_one, where, runs, sel, slot_grad, vec, stats, dmid, dqkv, target_row, cotangent, own, oth, 0, part
    )
    if fast:
        proj = paths.sum_plane(proj[0], proj_plane)
        sums, proj, dmid, input_grad = tie(sums, proj, dmid, input_grad)
    input_grad = input_rows(
        lay_one, where, runs, sel, slot_grad, vec, stats, dmid, dqkv, target_row, cotangent, own, oth,
        part, seqs - part, (input_grad,),
    )

    if fast:
        sums = paths.sum_line(sums)
        one, two = sums[:, :, : 2 * tile], sums[:, :, 2 * tile :]
        proj = paths.sum_line(paths.along(proj))
    else:
        flat = jnp.concatenate(
            [d_one_own, d_one_oth, d_two_own, d_two_oth, proj_own, proj_oth], axis=1
        )
        total = lax.psum_scatter(flat.astype(F32), AXES, scatter_dimension=0, tiled=True)
        p = proj_own.shape[1]
        one = total[:, : 4 * tile].reshape(shard, 2, 2 * tile).transpose(1, 0, 2)
        two = total[:, 4 * tile : 8 * tile].reshape(shard, 2, 2 * tile).transpose(1, 0, 2)
        proj = total[:, 8 * tile :].reshape(shard, 2, p).transpose(1, 0, 2)

    up_grad = jnp.concatenate(
        [v[side, :, :tile] for side in (0, 1) for v in (one, two)], axis=1
    )
    down_grad = jnp.concatenate(
        [v[side, :, tile:] for side in (0, 1) for v in (one, two)], axis=1
    ).T
    in_grad = jnp.stack(
        [proj[side, :, :half].reshape(shard, 3, third) for side in (0, 1)], axis=2
    ).reshape(shard, in_width)
    out_grad = jnp.concatenate([proj[side, :, half : half + third] for side in (0, 1)], axis=1).T
    if fast:
        every, vectors = proj[0, :, half + third :], proj[1, :, half + third :]
    else:
        high = 4 * width // 128
        mine = proj_own[:high, half + third :], proj_oth[:high, half + third :]
        every, vectors = lax.psum(tuple(v.astype(F32) for v in mine), AXES)
    d_up_bias = lax.dynamic_slice(every.reshape(-1), (device * 4 * shard,), (4 * shard,))
    vectors = vectors.reshape(4, width)
    vectors = lax.dynamic_slice(vectors, (0, device * shard), (2, shard))
    gain_one = jnp.sum(project_in.astype(F32) * in_grad, axis=1) / first_gain.astype(F32)
    gain_two = jnp.sum(up_weight.astype(F32) * up_grad, axis=1) / second_gain.astype(F32)
    return (
        layer_out,
        input_grad,
        gain_one,
        in_grad,
        out_grad,
        gain_two,
        up_grad,
        d_up_bias,
        down_grad,
        vectors[0],
        vectors[1],
    )


def solution(mesh):
    both = ("wide", "narrow")
    rows3, rows2, rows1, cols = P(both, None, None), P(both, None), P(both), P(None, both)
    in_specs = (
        rows3, rows1, rows2, rows2, rows1, rows2, cols, rows1, rows2, rows1, cols, rows1, rows1, rows3,
    )
    out_specs = (rows3, rows3, rows1, rows2, cols, rows1, rows2, rows1, cols, rows1, rows1)
    return jax.shard_map(
        partial(per_device, wide=mesh.shape["wide"], narrow=mesh.shape["narrow"]),
        mesh=mesh,
        in_specs=in_specs,
        out_specs=out_specs,
        check_vma=False,
    )
```

```python
from functools import partial

import jax
import jax.numpy as jnp
import numpy as np
from jax import lax
from jax.experimental import pallas as pl
from jax.experimental.pallas import tpu as pltpu
from jax.sharding import PartitionSpec as P

HEAD_DIM = 64
EPSILON = 1e-06
NEG_FILL = -1e30
F32 = jnp.float32
BF16 = jnp.bfloat16
AXES = ("wide", "narrow")
SCALE = HEAD_DIM**-0.5
GELU_A = 0.7978845608028654
GELU_B = 0.044715
LSE_LANE = 16
MLP_CHUNKS = 4
PAIRS = 3
PLACE_ROWS = 512
ANY = pl.BlockSpec(memory_space=pl.ANY)
VMEM_LIMIT = 67043328


def dot(left, right, left_dim=1, right_dim=0):
    return lax.dot_general(
        left, right, (((left_dim,), (right_dim,)), ((), ())), preferred_element_type=F32
    )


def params(*semantics):
    return pltpu.CompilerParams(
        dimension_semantics=semantics or None, vmem_limit_bytes=VMEM_LIMIT
    )


def whole(shape):
    return pl.BlockSpec(shape, lambda *_: (0,) * len(shape))


def cost(flops, bytes_accessed):
    return pl.CostEstimate(
        flops=int(flops), bytes_accessed=int(bytes_accessed), transcendentals=0
    )


class Layout:
    def __init__(self, height, plane, blocks):
        self.height, self.plane, self.blocks = height, plane, tuple(blocks)
        self.pieces = 1 + max(piece for piece, *_ in blocks)
        self.depth = len(blocks) // plane

    def natural(self, here, step, line):
        return pl.multiple_of((line * self.plane + (here ^ step)) * self.height, 8)


def load_rows(layout, here, pieces, target, sems, source, columns):
    height = layout.height
    return [
        pltpu.make_async_copy(
            pieces[piece].at[pl.ds(at * height, height), source],
            target.at[pl.ds(layout.natural(here, step, line), height), columns],
            sems.at[j],
        )
        for j, (piece, at, step, line) in enumerate(layout.blocks)
    ]


def both_halves(layout, here, own, oth, target, sems, start, count):
    source = pl.ds(start, count)
    return load_rows(layout, here, own, target, sems.at[0], source, pl.ds(0, count)) + load_rows(
        layout, here, oth, target, sems.at[1], source, pl.ds(count, count)
    )


def store_rows(layout, target, value):
    height = layout.height
    for line in range(layout.depth):
        for owner in range(layout.plane):
            start = (owner * layout.depth + line) * height
            c = line * layout.plane + owner
            target[start : start + height, :] = value[c * height : (c + 1) * height, :]


def gather_kernel(target, x, cot, sel, grad):
    length = x.shape[1]
    places = lax.broadcasted_iota(jnp.int32, (target.shape[1], length), 1)
    chosen = jnp.where(target[0] == places, 1.0, 0.0).astype(BF16)
    sel[...] = dot(chosen, x[0]).astype(BF16)
    grad[...] = dot(chosen, cot[0]).astype(BF16)


def gather_rows(target, layer_in, cotangent):
    seqs, length, width = layer_in.shape
    slots = target.shape[1]
    big = pl.BlockSpec((1, length, width), lambda b: (b, 0, 0))
    out = pl.BlockSpec((slots, width), lambda b: (b, 0))
    return pl.pallas_call(
        gather_kernel,
        grid=(seqs,),
        in_specs=[pl.BlockSpec((1, slots, 1), lambda b: (b, 0, 0)), big, big],
        out_specs=[out, out],
        out_shape=[jax.ShapeDtypeStruct((seqs * slots, width), BF16)] * 2,
        compiler_params=params("arbitrary"),
        cost_estimate=cost(
            4 * seqs * slots * length * width, 4 * seqs * length * width
        ),
        name="gather_rows",
    )(target, layer_in, cotangent)


def allowed_keys(slots, valid):
    rows = lax.broadcasted_iota(jnp.int32, (2 * slots, slots), 0)
    rows = jnp.where(rows >= slots, rows - slots, rows)
    keys = lax.broadcasted_iota(jnp.int32, (2 * slots, slots), 1)
    return (keys <= rows) & (keys < valid)


def split_pair(pair):
    lane = lax.broadcasted_iota(jnp.int32, pair.shape, 1)
    zero = jnp.zeros_like(pair)
    first = lane < HEAD_DIM
    return jnp.concatenate(
        [jnp.where(first, pair, zero), jnp.where(first, zero, pair)], axis=0
    )


def join_pair(stacked):
    half = stacked.shape[0] // 2
    lane = lax.broadcasted_iota(jnp.int32, (half, stacked.shape[1]), 1)
    return jnp.where(lane < HEAD_DIM, stacked[:half], stacked[half:])


def pair_loop(pairs, body, carry, at_once=PAIRS):
    def step(k, carry):
        for p in range(at_once):
            carry = body(k * at_once + p, carry)
        return carry

    return lax.fori_loop(0, pairs // at_once, step, carry)


def pair_columns(pair, half_width):
    per_half = half_width // (2 * HEAD_DIM)
    base = (pair // per_half) * 3 * half_width + (pair % per_half) * 2 * HEAD_DIM
    return tuple(
        pl.ds(pl.multiple_of(base + k * half_width, 128), 2 * HEAD_DIM) for k in range(3)
    )


def forward_kernel(
    where, counts, sel, grad, *rest, layout, half, third
):
    own, oth = rest[: layout.pieces], rest[layout.pieces : 2 * layout.pieces]
    (
    qkv, att, mid, n2, n2t, g, gt, n1t, stats, vec, bias, gsum,
    w_in, w_out, w_ext, sem_in, sem_out, sem_ext,
    ) = rest[2 * layout.pieces :]
    b = pl.program_id(0)
    slots, width = sel.shape
    here = where[0]

    def in_copies():
        return both_halves(layout, here, own, oth, w_in, sem_in, 0, half)

    def out_copies():
        return both_halves(layout, here, own, oth, w_out, sem_out, half, third)

    @pl.when(b == 0)
    def _():
        small = both_halves(layout, here, own, oth, w_ext, sem_ext, half + third, 128)
        first = in_copies()
        for c in small + first + out_copies():
            c.start()
        for c in small:
            c.wait()
        per = width // 128
        high = 4 * per
        total = sum(w_ext[k * high : (k + 1) * high, :].astype(F32) for k in range(width // high))
        mine, others = total[:, :128], total[:, 128:]
        vectors = jnp.where(where[1] == 0, mine, others)
        biases = jnp.where(where[1] == 0, others, mine)
        vec[...] = jnp.zeros_like(vec)
        for v in range(4):
            for k in range(per):
                vec[v : v + 1, k * 128 : (k + 1) * 128] = vectors[v * per + k : v * per + k + 1, :]
        for k in range(bias.shape[1] // 128):
            bias[0:1, k * 128 : (k + 1) * 128] = biases[k : k + 1, :]
        for c in first:
            c.wait()

    x = sel[...].astype(F32)
    r1 = lax.rsqrt(jnp.mean(x * x, axis=-1, keepdims=True) + EPSILON)
    n1 = (x * r1 * vec[0:1, :]).astype(BF16)
    logit = jnp.sum(x * vec[3:4, :], axis=-1, keepdims=True)
    rate = jax.nn.sigmoid(logit)
    d_mlp = (rate * grad[...].astype(F32)).astype(BF16)
    g[...] = d_mlp
    gsum_now = jnp.sum(d_mlp.astype(F32), axis=0, keepdims=True)

    @pl.when(b == 0)
    def _():
        gsum[...] = gsum_now

    @pl.when(b > 0)
    def _():
        gsum[...] += gsum_now

    store_rows(layout, gt, d_mlp.T)
    store_rows(layout, n1t, n1.T)
    qkv[...] = dot(n1, w_in[...]).astype(BF16)

    allowed = allowed_keys(slots, counts[b])
    lane = lax.broadcasted_iota(jnp.int32, (slots, 128), 1)
    kept = jnp.where(lane == 0, r1, jnp.where(lane == 1, rate, 0.0))

    def attend(pair, kept):
        qc, kc, vc = pair_columns(pair, width // 2)
        scores = dot(split_pair(qkv[:, qc] * SCALE), qkv[:, kc], 1, 1)
        scores = jnp.where(allowed, scores, NEG_FILL)
        top = jnp.max(scores, axis=-1, keepdims=True)
        exps = jnp.exp(scores - top)
        total = jnp.sum(exps, axis=-1, keepdims=True)
        lse = top + jnp.log(total)
        probs = (exps * (1.0 / total)).astype(BF16)
        here_now = pl.ds(pl.multiple_of(pair * 128, 128), 128)
        att[:, here_now] = join_pair(dot(probs, qkv[:, vc])).astype(BF16)
        kept = jnp.where(lane == LSE_LANE + 2 * pair, lse[:slots], kept)
        return jnp.where(lane == LSE_LANE + 2 * pair + 1, lse[slots:], kept)

    kept = pair_loop(width // (2 * HEAD_DIM), attend, kept, 2 * PAIRS)

    @pl.when(b == 0)
    def _():
        for c in out_copies():
            c.wait()

    stream = x + dot(att[...], w_out[...], 1, 1)
    mid[...] = stream
    r2 = lax.rsqrt(jnp.mean(stream * stream, axis=-1, keepdims=True) + EPSILON)
    normed = (stream * r2 * vec[1:2, :]).astype(BF16)
    n2[...] = normed
    store_rows(layout, n2t, normed.T)
    stats[...] = jnp.where(lane == 2, r2, kept)


def forward_block(layout, hidden, where, counts, sel, grad, own, oth):
    rows, width = sel.shape
    seqs = counts.shape[0]
    slots = rows // seqs
    blocks = len(layout.blocks)
    row = lambda w: pl.BlockSpec((slots, w), lambda b, *_: (b, 0))
    col = pl.BlockSpec((width, slots), lambda b, *_: (0, b))
    shape = jax.ShapeDtypeStruct
    return pl.pallas_call(
        partial(forward_kernel, layout=layout, half=3 * width // 2, third=width // 2),
        grid_spec=pltpu.PrefetchScalarGridSpec(
            num_scalar_prefetch=2,
            grid=(seqs,),
            in_specs=[row(width), row(width)] + [ANY] * (2 * layout.pieces),
            out_specs=[
                row(3 * width), row(width), row(width), row(width), col, row(width), col, col, row(128),
                whole((8, width)), whole((1, hidden)), whole((1, width)),
            ],
            scratch_shapes=[
                pltpu.VMEM((width, 3 * width), BF16),
                pltpu.VMEM((width, width), BF16),
                pltpu.VMEM((width, 256), BF16),
                pltpu.SemaphoreType.DMA((2, blocks)),
                pltpu.SemaphoreType.DMA((2, blocks)),
                pltpu.SemaphoreType.DMA((2, blocks)),
            ],
        ),
        out_shape=[
            shape((rows, 3 * width), BF16),
            shape((rows, width), BF16),
            shape((rows, width), F32),
            shape((rows, width), BF16),
            shape((width, rows), BF16),
            shape((rows, width), BF16),
            shape((width, rows), BF16),
            shape((width, rows), BF16),
            shape((rows, 128), F32),
            shape((8, width), F32),
            shape((1, hidden), F32),
            shape((1, width), F32),
        ],
        compiler_params=params("arbitrary"),
        cost_estimate=cost(10 * rows * width * width, 30 * rows * width),
        name="forward_block",
    )(where, counts, sel, grad, *own, *oth)


def mlp_kernel(where, bias, *rest, layout, tile):
    rows_in = rest[:4]
    own, oth = rest[4 : 4 + layout.pieces], rest[4 + layout.pieces : 4 + 2 * layout.pieces]
    mlp, dn2, d_own, d_oth, dbias, *held, w_up, w_down, d_first, act, d_pre, sem_rows, sems, sem_out = rest[
        4 + 2 * layout.pieces :
    ]
    n2, n2t, g, gt, mlp_sum, dn2_sum = held
    i = pl.program_id(0)
    here = where[0]
    row_copies = [
        pltpu.make_async_copy(rows_in[k], held[k], sem_rows.at[k]) for k in range(4)
    ]
    out_copy = pltpu.make_async_copy(d_first, d_own, sem_out)

    def copies(side, kind):
        source, target = (own, oth)[side], (w_up, w_down)[kind].at[side]
        return load_rows(
            layout, here, source, target, sems.at[side, kind], pl.ds(kind * tile, tile), pl.ds(0, tile)
        )

    def wait_first(*waited):
        @pl.when(i == 0)
        def _():
            for c in waited:
                c.wait()

    @pl.when(i == 0)
    def _():
        started = copies(0, 0) + row_copies[:1] + copies(0, 1) + row_copies[2:3]
        started = started + row_copies[1:2] + row_copies[3:] + copies(1, 0) + copies(1, 1)
        for c in started:
            c.start()

    wait_first(*copies(0, 0), row_copies[0])

    @pl.when(i == 1)
    def _():
        out_copy.start()
        for c in copies(1, 0) + copies(1, 1):
            c.wait()

    wait_first(*copies(0, 1), row_copies[2])
    up_now = w_up.at[i]
    down_now = w_down.at[i]
    rows = n2.shape[0] // MLP_CHUNKS

    def chunk(c, total):
        here = pl.ds(pl.multiple_of(c * rows, rows), rows)
        pre = dot(n2[here, :], up_now[...]) + bias[...]
        square = pre * pre
        th = jnp.tanh(pre * (GELU_A + GELU_A * GELU_B * square))
        half = 0.5 * (1.0 + th)
        act_now = (pre * half).astype(BF16)
        act[here, :] = act_now
        slope = half + 0.5 * pre * (1.0 - th * th) * (GELU_A + 3 * GELU_A * GELU_B * square)
        d_pre_now = (slope * dot(g[here, :], down_now[...])).astype(BF16)
        d_pre[here, :] = d_pre_now
        mlp_now = jnp.where(i == 0, 0.0, mlp_sum[here, :]) + dot(act_now, down_now[...], 1, 1)
        mlp_sum[here, :] = mlp_now
        mlp[here, :] = mlp_now.astype(BF16)
        dn2_now = jnp.where(i == 0, 0.0, dn2_sum[here, :]) + dot(d_pre_now, up_now[...], 1, 1)
        dn2_sum[here, :] = dn2_now
        dn2[here, :] = dn2_now.astype(BF16)
        return total + jnp.sum(d_pre_now.astype(F32), axis=0, keepdims=True)

    dbias[...] = lax.fori_loop(0, MLP_CHUNKS, chunk, jnp.zeros_like(dbias))
    wait_first(row_copies[1], row_copies[3])
    dup = dot(n2t[...], d_pre[...]).astype(BF16)
    ddown = dot(gt[...], act[...]).astype(BF16)

    @pl.when(i == 0)
    def _():
        d_first[:, :tile] = dup
        d_first[:, tile:] = ddown

    @pl.when(i == 1)
    def _():
        d_oth[:, :tile] = dup
        d_oth[:, tile:] = ddown
        out_copy.wait()


def mlp_part(layout, where, part, tile, n2, n2t, g, gt, own, oth, bias):
    rows, width = n2.shape
    parts = bias.shape[1] // (2 * tile)
    blocks = len(layout.blocks)
    shape = jax.ShapeDtypeStruct
    return pl.pallas_call(
        partial(mlp_kernel, layout=layout, tile=tile),
        grid_spec=pltpu.PrefetchScalarGridSpec(
            num_scalar_prefetch=1,
            grid=(2,),
            in_specs=[
                pl.BlockSpec((1, tile), lambda i, where: (0, (where[1] ^ i) * parts + part)),
            ] + [ANY] * (4 + 2 * layout.pieces),
            out_specs=[
                whole((rows, width)), whole((rows, width)), ANY, whole((width, 2 * tile)),
                pl.BlockSpec((1, tile), lambda i, where: (0, i)),
            ],
            scratch_shapes=[
                pltpu.VMEM((rows, width), BF16),
                pltpu.VMEM((width, rows), BF16),
                pltpu.VMEM((rows, width), BF16),
                pltpu.VMEM((width, rows), BF16),
                pltpu.VMEM((rows, width), F32),
                pltpu.VMEM((rows, width), F32),
                pltpu.VMEM((2, width, tile), BF16),
                pltpu.VMEM((2, width, tile), BF16),
                pltpu.VMEM((width, 2 * tile), BF16),
                pltpu.VMEM((rows, tile), BF16),
                pltpu.VMEM((rows, tile), BF16),
                pltpu.SemaphoreType.DMA((4,)),
                pltpu.SemaphoreType.DMA((2, 2, blocks)),
                pltpu.SemaphoreType.DMA,
            ],
        ),
        out_shape=[
            shape((rows, width), BF16),
            shape((rows, width), BF16),
            shape((width, 2 * tile), BF16),
            shape((width, 2 * tile), BF16),
            shape((1, 2 * tile), F32),
        ],
        compiler_params=params("arbitrary"),
        cost_estimate=cost(24 * rows * width * tile, 8 * rows * width),
        name="mlp_part",
    )(where, bias, n2, n2t, g, gt, *own, *oth)


def norm_pull(values, inverse, scaled):
    return inverse * scaled - values * (
        inverse * inverse * inverse * jnp.mean(scaled * values, axis=-1, keepdims=True)
    )


def backward_kernel(
    where, counts, sel, grad, vec, qkv, mid, stats, mlp, mlp_two, dn2, dn2_two, *rest, layout, half, third
):
    own, oth = rest[: layout.pieces], rest[layout.pieces : 2 * layout.pieces]
    dqkv, dattnt, dmid, new_rows, drouter, w_out, d_att, sem_out = rest[2 * layout.pieces :]
    b = pl.program_id(0)
    slots, width = sel.shape
    here = where[0]

    @pl.when(b == 0)
    def _():
        copies = both_halves(layout, here, own, oth, w_out, sem_out, half, third)
        for c in copies:
            c.start()
        for c in copies:
            c.wait()

    x = sel[...].astype(F32)
    stream = mid[...]
    rate = stats[:, 1:2]
    r2 = stats[:, 2:3]
    slot_grad = grad[...].astype(F32)
    branch = (stream - x) + (mlp[...].astype(F32) + mlp_two[...].astype(F32) + vec[2:3, :])
    new_rows[...] = (x + rate * branch).astype(BF16)
    d_logit = jnp.sum(slot_grad * branch, axis=-1, keepdims=True) * (rate * (1.0 - rate))
    router_now = jnp.sum(d_logit * x, axis=0, keepdims=True)

    @pl.when(b == 0)
    def _():
        drouter[...] = router_now

    @pl.when(b > 0)
    def _():
        drouter[...] += router_now

    d_mid = norm_pull(stream, r2, vec[1:2, :] * (dn2[...].astype(F32) + dn2_two[...].astype(F32)))
    dmid[...] = d_mid + d_logit * vec[3:4, :]
    d_attn = (rate * slot_grad + d_mid).astype(BF16)
    store_rows(layout, dattnt, d_attn.T)
    d_att[...] = dot(d_attn, w_out[...]).astype(BF16)

    allowed = allowed_keys(slots, counts[b])
    lane = lax.broadcasted_iota(jnp.int32, (slots, 128), 1)

    def pull(pair, carry):
        qc, kc, vc = pair_columns(pair, width // 2)
        queries = split_pair(qkv[:, qc] * SCALE)
        keys = qkv[:, kc]
        lse = jnp.concatenate(
            [
                jnp.sum(jnp.where(lane == LSE_LANE + 2 * pair + k, stats[...], 0.0), axis=-1, keepdims=True)
                for k in (0, 1)
            ],
            axis=0,
        )
        upstream = split_pair(d_att[:, pl.ds(pl.multiple_of(pair * 128, 128), 128)])
        scores = dot(queries, keys, 1, 1)
        probs = jnp.exp(jnp.where(allowed, scores - lse, NEG_FILL))
        d_probs = dot(upstream, qkv[:, vc], 1, 1)
        d_scores = (probs * (d_probs - jnp.sum(probs * d_probs, axis=-1, keepdims=True))).astype(BF16)
        dqkv[:, qc] = (join_pair(dot(d_scores, keys)) * SCALE).astype(BF16)
        dqkv[:, kc] = dot(d_scores, queries, 0, 0).astype(BF16)
        dqkv[:, vc] = dot(probs.astype(BF16), upstream, 0, 0).astype(BF16)
        return carry

    pair_loop(width // (2 * HEAD_DIM), pull, 0)


def backward_block(layout, where, counts, sel, grad, vec, qkv, mid, stats, sums, own, oth):
    rows, width = sel.shape
    seqs = counts.shape[0]
    slots = rows // seqs
    blocks = len(layout.blocks)
    row = lambda w: pl.BlockSpec((slots, w), lambda b, *_: (b, 0))
    col = pl.BlockSpec((width, slots), lambda b, *_: (0, b))
    shape = jax.ShapeDtypeStruct
    return pl.pallas_call(
        partial(backward_kernel, layout=layout, half=3 * width // 2, third=width // 2),
        grid_spec=pltpu.PrefetchScalarGridSpec(
            num_scalar_prefetch=2,
            grid=(seqs,),
            in_specs=[
                row(width), row(width), whole(vec.shape), row(3 * width), row(width), row(128),
            ] + [row(width)] * 4 + [ANY] * (2 * layout.pieces),
            out_specs=[row(3 * width), col, row(width), row(width), whole((1, width))],
            scratch_shapes=[
                pltpu.VMEM((width, width), BF16),
                pltpu.VMEM((slots, width), BF16),
                pltpu.SemaphoreType.DMA((2, blocks)),
            ],
        ),
        out_shape=[
            shape((rows, 3 * width), BF16),
            shape((width, rows), BF16),
            shape((rows, width), F32),
            shape((rows, width), BF16),
            shape((1, width), F32),
        ],
        compiler_params=params("arbitrary"),
        cost_estimate=cost(2 * 20 * rows * width * width, 2 * 30 * rows * width),
        name="backward_block",
    )(where, counts, sel, grad, vec, qkv, mid, stats, *sums, *own, *oth)


def project_kernel(where, n1t, dattnt, dqkv, att, dbias_one, dbias_two, ddown, drouter, oth, own):
    half = dqkv.shape[1]
    third = att.shape[1]
    width = n1t.shape[0]
    high, tile = 4 * width // 128, dbias_one.shape[1] // 2
    in_now = dot(n1t[...], dqkv[...]).astype(BF16)
    out_now = dot(dattnt[...], att[...]).astype(BF16)
    first_core = where[1] == 0

    def bias_rows():
        rows = []
        for side in (0, 1):
            for part in (dbias_one, dbias_two):
                for k in range(tile // 128):
                    a, b = side * tile + k * 128, (1 - side) * tile + k * 128
                    rows.append(jnp.where(first_core, part[:, a : a + 128], part[:, b : b + 128]))
        return rows

    def vector_rows():
        rows = [v[:, k * 128 : (k + 1) * 128] for v in (ddown, drouter) for k in range(width // 128)]
        return rows + [jnp.zeros((1, 128), F32)] * (high - len(rows))

    def store(out, is_first):
        out[:, :half] = in_now
        out[:, half : half + third] = out_now
        small = jnp.where(
            is_first, jnp.concatenate(bias_rows(), axis=0), jnp.concatenate(vector_rows(), axis=0)
        )
        small = jnp.concatenate([small] * 2, axis=0).astype(BF16)
        for k in range(width // (2 * high)):
            out[2 * k * high : 2 * (k + 1) * high, half + third :] = small

    pl.when(pl.program_id(0) == 0)(lambda: store(oth, where[1] == 1))
    pl.when(pl.program_id(0) == 1)(lambda: store(own, where[1] == 0))


def project_grads(where, n1t, dattnt, dqkv, att, *vectors):
    width, rows = n1t.shape
    half, third = dqkv.shape[1] // 2, att.shape[1] // 2
    total = half + third + 128
    return pl.pallas_call(
        project_kernel,
        grid_spec=pltpu.PrefetchScalarGridSpec(
            num_scalar_prefetch=1,
            grid=(2,),
            in_specs=[
                whole((width, rows)), whole((width, rows)),
                pl.BlockSpec((rows, half), lambda i, where: (0, 1 - i)),
                pl.BlockSpec((rows, third), lambda i, where: (0, 1 - i)),
            ] + [whole(v.shape) for v in vectors],
            out_specs=[whole((width, total))] * 2,
        ),
        out_shape=[jax.ShapeDtypeStruct((width, total), BF16)] * 2,
        compiler_params=params("arbitrary"),
        cost_estimate=cost(2 * 4 * width * rows * total, 2 * 4 * width * rows),
        name="project_grads",
    )(where, n1t, dattnt, dqkv, att, *vectors)


def place(out, rows, target, x, start, count):
    chunk = min(PLACE_ROWS, x.shape[1])

    def one(c, carry):
        here = pl.ds(pl.multiple_of(c * chunk, chunk), chunk)
        places = lax.broadcasted_iota(jnp.int32, (chunk, target.shape[2]), 0) + c * chunk
        hits = target[0] == places
        moved = dot(jnp.where(hits, 1.0, 0.0).astype(BF16), rows[...])
        hit = jnp.max(jnp.where(hits, 1.0, 0.0), axis=-1, keepdims=True)
        at = lax.broadcasted_iota(jnp.int32, (chunk, 1), 0) + c * chunk
        kept = (at >= start) & (at < start + count) & (hit < 0.5)
        out[0, here, :] = jnp.where(kept, x[0, here, :].astype(F32), moved).astype(BF16)
        return carry

    lax.fori_loop(0, x.shape[1] // chunk, one, 0)


def out_kernel(runs, rows, target, x, out):
    b = pl.program_id(0)
    place(out, rows, target, x, runs[0, b], runs[1, b])


def place_rows(runs, rows, target, x):
    seqs, length, width = x.shape
    slots = target.shape[2]
    big = pl.BlockSpec((1, length, width), lambda b, *_: (b, 0, 0))
    return pl.pallas_call(
        out_kernel,
        grid_spec=pltpu.PrefetchScalarGridSpec(
            num_scalar_prefetch=1,
            grid=(seqs,),
            in_specs=[
                pl.BlockSpec((slots, width), lambda b, *_: (b, 0)),
                pl.BlockSpec((1, 1, slots), lambda b, *_: (b, 0, 0)),
                big,
            ],
            out_specs=big,
        ),
        out_shape=jax.ShapeDtypeStruct(x.shape, BF16),
        compiler_params=params("arbitrary"),
        cost_estimate=cost(2 * seqs * slots * length * width, 4 * seqs * length * width),
        name="place_rows",
    )(runs, rows, target, x)


def input_kernel(
    where, runs, sel, grad, vec, stats, dmid, dqkv, target, x, *rest, layout, first
):
    own, oth = rest[: layout.pieces], rest[layout.pieces : 2 * layout.pieces]
    *_, out, w_in, moved, sem_in = rest[2 * layout.pieces :]
    b = pl.program_id(0)

    @pl.when(b == 0)
    def _():
        copies = both_halves(layout, where[0], own, oth, w_in, sem_in, 0, w_in.shape[1] // 2)
        for c in copies:
            c.start()
        for c in copies:
            c.wait()

    d_normed = dot(dqkv[...], w_in[...], 1, 1)
    d_sel = norm_pull(sel[...].astype(F32), stats[:, 0:1], vec[0:1, :] * d_normed) + dmid[...]
    moved[...] = (grad[...].astype(F32) + d_sel).astype(BF16)
    place(out, moved, target, x, runs[0, first + b], runs[1, first + b])


def input_rows(layout, where, runs, sel, grad, vec, stats, dmid, dqkv, target, x, own, oth, first, count, begun=()):
    seqs, length, width = x.shape
    slots = target.shape[2]
    blocks = len(layout.blocks)
    row = lambda w: pl.BlockSpec((slots, w), lambda b, *_: (first + b, 0))
    big = pl.BlockSpec((1, length, width), lambda b, *_: (first + b, 0, 0))
    return pl.pallas_call(
        partial(input_kernel, layout=layout, first=first),
        grid_spec=pltpu.PrefetchScalarGridSpec(
            num_scalar_prefetch=2,
            grid=(count,),
            in_specs=[
                row(width), row(width), whole(vec.shape), row(128), row(width), row(3 * width),
                pl.BlockSpec((1, 1, slots), lambda b, *_: (first + b, 0, 0)),
                big,
            ] + [ANY] * (2 * layout.pieces + len(begun)),
            out_specs=big,
            scratch_shapes=[
                pltpu.VMEM((width, 3 * width), BF16),
                pltpu.VMEM((slots, width), BF16),
                pltpu.SemaphoreType.DMA((2, blocks)),
            ],
        ),
        out_shape=jax.ShapeDtypeStruct(x.shape, BF16),
        compiler_params=params("arbitrary"),
        cost_estimate=cost(1, 1),
        input_output_aliases={10 + 2 * layout.pieces: 0} if begun else {},
        name="input_rows",
    )(where, runs, sel, grad, vec, stats, dmid, dqkv, target, x, *own, *oth, *begun)


class Paths:
    def __init__(self, wide, narrow, here):
        self.wide, self.narrow, self.depth, self.here = wide, narrow, wide // 2, here
        ids = np.arange(wide * narrow).reshape(self.depth, 4, 2)
        self.lines = ids.transpose(1, 0, 2).reshape(4, -1).tolist()
        self.planes = ids.transpose(0, 2, 1).reshape(-1, 4).tolist()

    def swap(self, value):
        return lax.ppermute(value, "narrow", [(i, i ^ 1) for i in range(self.narrow)])

    def over(self, value, step):
        if step == 1:
            return lax.ppermute(value, "narrow", [(i, i ^ 2) for i in range(self.narrow)])
        if step == 2:
            return lax.ppermute(value, "wide", [(i, i ^ 1) for i in range(self.wide)])
        mask = self.narrow ^ 2
        return lax.ppermute(value, AXES, [(i, i ^ mask) for i in range(self.wide * self.narrow)])

    def along(self, value):
        return lax.all_to_all(value, AXES, 0, 0, axis_index_groups=self.lines, tiled=True)

    def to_line(self, halves):
        shard, cols = halves[0].shape
        sent = jnp.broadcast_to(jnp.stack(halves)[None], (self.depth, 2, shard, cols))
        return sent.reshape(self.depth * 2 * shard, cols)

    def gather_halved(self, held):
        near_x, near_y = self.over(held, 1), self.over(held, 2)
        mid = held.shape[0] // 2
        return [held, near_x, near_y, self.over(near_y[:mid], 1), self.over(near_x[mid:], 2)]

    def gather_direct(self, held):
        return [held] + [self.over(held, step) for step in (1, 2, 3)]

    def swap_all(self, pieces):
        return [self.swap(p) for p in pieces]

    def chip_sums(self, own, got):
        rows = own.shape[0] // 4
        starts = [(self.here ^ step) * rows for step in range(4)]
        return [
            add_halves(
                lax.dynamic_slice(own, (start, 0), (rows, own.shape[1])),
                lax.dynamic_slice(got, (start, 0), (rows, own.shape[1])),
            )
            for start in starts
        ]

    def exchange_plane(self, both):
        return lax.all_to_all(both, AXES, 0, 0, axis_index_groups=self.planes, tiled=True)

    def send_plane(self, sums):
        return [self.over(sums[step], step) for step in (1, 2, 3)]

    def sum_plane(self, mine, got):
        total = mine.astype(F32)
        for v in got:
            total = total + v.astype(F32)
        return total.astype(BF16)

    def sum_line(self, got):
        return jnp.sum(got.reshape(self.depth, 2, -1, got.shape[1]).astype(F32), axis=0)


def halved(depth):
    return [(piece, z, piece, z) for piece in range(3) for z in range(depth)] + [
        (3 + (z >= depth // 2), z % (depth // 2), 3, z) for z in range(depth)
    ]


def direct(depth):
    return [(piece, z, piece, z) for piece in range(4) for z in range(depth)]


def add_halves(own, got):
    return (own.astype(F32) + got.astype(F32)).astype(BF16)


def tie(*values):
    return lax.optimization_barrier(values)


def per_device(
    layer_in,
    lengths,
    padding,
    picked,
    first_gain,
    project_in,
    project_out,
    second_gain,
    up_weight,
    up_bias,
    down_weight,
    down_bias,
    router,
    cotangent,
    *,
    wide,
    narrow,
):
    seqs, slots = picked.shape
    shard, in_width = project_in.shape
    width = in_width // 3
    hidden = up_weight.shape[1]
    devices = wide * narrow
    half = 3 * width // 2
    third = width // 2
    tile = hidden // 4
    fast = shard == 24 and wide % 4 == 0 and narrow == 4
    core = lax.axis_index("narrow") & 1 if fast else jnp.int32(0)
    device = lax.axis_index("wide") * narrow + lax.axis_index("narrow")

    in_split = project_in.reshape(shard, 3, 2, third)
    in_halves = [in_split[:, :, side].reshape(shard, half) for side in (0, 1)]
    out_t = project_out.T
    down_t = down_weight.T
    vectors = jnp.stack([first_gain, second_gain, down_bias, router])

    first = [
        jnp.concatenate([in_halves[side], out_t[:, side * third : (side + 1) * third]], axis=1)
        for side in (0, 1)
    ]

    def rest_of(side, part):
        at = (2 * side + part) * tile
        return jnp.concatenate([up_weight[:, at : at + tile], down_t[:, at : at + tile]], axis=1)

    def places(lengths):
        counts = lengths // 8
        valid = jnp.arange(slots)[None, :] < counts[:, None]
        target = jnp.where(valid, picked, -1)
        runs = jnp.stack([jnp.argmax(padding, axis=1).astype(jnp.int32), lengths])
        return counts, runs, target[:, :, None], target[:, None, :]

    if fast:
        here = (lax.axis_index("wide") & 1) * 2 + (lax.axis_index("narrow") >> 1)
        paths = Paths(wide, narrow, here)
        lay_one = Layout(2 * shard, 4, halved(paths.depth))
        lay_two = Layout(2 * shard, 4, direct(paths.depth))
        placed = lax.dynamic_update_slice(
            jnp.zeros((4, width), BF16), vectors, (0, device * shard)
        ).reshape(shard, 128)
        biases = lax.dynamic_update_slice(
            jnp.zeros((hidden,), BF16), up_bias, (device * 4 * shard,)
        ).reshape(shard, 128)
        sent = paths.to_line(
            [
                jnp.concatenate([first[0], placed], axis=1),
                jnp.concatenate([first[1], biases], axis=1),
            ]
        )
        sent, lengths = tie(sent, lengths)
        line = paths.along(sent)
        counts, runs, columns, target_row = places(lengths)
        rest = paths.to_line(
            [jnp.concatenate([rest_of(side, 0), rest_of(side, 1)], axis=1) for side in (0, 1)]
        )
        rest, columns = tie(rest, columns)
        sel, slot_grad = gather_rows(columns, layer_in, cotangent)
        line, rest, sel, slot_grad, runs, target_row = tie(line, rest, sel, slot_grad, runs, target_row)
        own = paths.gather_halved(line)
        oth = paths.swap_all(own)
        rest = paths.along(rest)
        own, oth, rest, sel = tie(own, oth, rest, sel)
        one_own = paths.gather_direct(rest[:, : 2 * tile])
        two_own = paths.gather_direct(rest[:, 2 * tile :])
    else:
        counts, runs, columns, target_row = places(lengths)
        here = jnp.int32(0)
        lay_one = lay_two = Layout(width, 1, [(0, 0, 0, 0)])
        packed = jnp.concatenate(
            first + [rest_of(side, part) for part in (0, 1) for side in (0, 1)], axis=1
        )
        full = lax.all_gather(packed, AXES, axis=0, tiled=True)
        cuts = [0]
        for n in (half + third,) * 2 + (2 * tile,) * 4:
            cuts.append(cuts[-1] + n)
        own, oth, one_own, one_oth, two_own, two_oth = (
            [full[:, a:b]] for a, b in zip(cuts, cuts[1:])
        )
        every = lax.all_gather(vectors, AXES, axis=1, tiled=True).reshape(-1, 128)
        biases = lax.all_gather(up_bias, AXES, axis=0, tiled=True).reshape(-1, 128)
        own, oth = (
            [jnp.concatenate([p[0], jnp.pad(v, ((0, width - v.shape[0]), (0, 0)))], axis=1)]
            for p, v in ((own, every), (oth, biases))
        )
        sel, slot_grad = gather_rows(columns, layer_in, cotangent)

    where = jnp.stack([here, core]).astype(jnp.int32)
    qkv, att, mid, n2, n2t, g, gt, n1t, stats, vec, bias, ddown_bias = forward_block(
        lay_one, hidden, where, counts, sel, slot_grad, own, oth
    )
    if fast:
        one_own, n2 = tie(one_own, n2)
        one_oth = paths.swap_all(one_own)
    mlp, dn2, d_one_own, d_one_oth, dbias_one = mlp_part(
        lay_two, where, 0, tile, n2, n2t, g, gt, one_own, one_oth, bias
    )
    if fast:
        two_own, mlp, n2 = tie(two_own, mlp, n2)
        two_oth = paths.swap_all(two_own)
        d_one_got = paths.swap(d_one_oth)
    mlp_two, dn2_two, d_two_own, d_two_oth, dbias_two = mlp_part(
        lay_two, where, 1, tile, n2, n2t, g, gt, two_own, two_oth, bias
    )
    if fast:
        d_one_got, mlp_two = tie(d_one_got, mlp_two)
        d_one = paths.chip_sums(d_one_own, d_one_got)
        d_one_plane = paths.send_plane(d_one)
        d_two = add_halves(d_two_own, paths.swap(d_two_oth))
        d_two, mlp_two = tie(d_two, mlp_two)
        d_two = paths.exchange_plane(d_two)
    dqkv, dattnt, dmid, new_rows, drouter = backward_block(
        lay_one, where, counts, sel, slot_grad, vec, qkv, mid, stats, (mlp, mlp_two, dn2, dn2_two), own, oth
    )

    proj_oth, proj_own = project_grads(
        where, n1t, dattnt, dqkv, att, dbias_one, dbias_two, ddown_bias, drouter
    )
    if fast:
        d_one_plane, d_two, proj_oth = tie(d_one_plane, d_two, proj_oth)
        proj_got = paths.swap(proj_oth)
        proj = paths.chip_sums(proj_own, proj_got)
        d_two = d_two.reshape(4, -1, 2 * tile)
        sums = jnp.concatenate(
            [paths.sum_plane(d_one[0], d_one_plane), paths.sum_plane(d_two[0], list(d_two[1:]))], axis=1
        )
        sums, proj, new_rows = tie(sums, proj, new_rows)
        proj_plane = paths.send_plane(proj)
        sums = paths.along(sums)
    layer_out = place_rows(runs, new_rows, target_row, layer_in)
    if fast:
        dmid, layer_out = tie(dmid, layer_out)
    part = seqs // 2
    input_grad = input_rows(
        lay_one, where, runs, sel, slot_grad, vec, stats, dmid, dqkv, target_row, cotangent, own, oth, 0, part
    )
    if fast:
        proj = paths.sum_plane(proj[0], proj_plane)
        sums, proj, dmid, input_grad = tie(sums, proj, dmid, input_grad)
    input_grad = input_rows(
        lay_one, where, runs, sel, slot_grad, vec, stats, dmid, dqkv, target_row, cotangent, own, oth,
        part, seqs - part, (input_grad,),
    )

    if fast:
        sums = paths.sum_line(sums)
        one, two = sums[:, :, : 2 * tile], sums[:, :, 2 * tile :]
        proj = paths.sum_line(paths.along(proj))
    else:
        flat = jnp.concatenate(
            [d_one_own, d_one_oth, d_two_own, d_two_oth, proj_own, proj_oth], axis=1
        )
        total = lax.psum_scatter(flat.astype(F32), AXES, scatter_dimension=0, tiled=True)
        p = proj_own.shape[1]
        one = total[:, : 4 * tile].reshape(shard, 2, 2 * tile).transpose(1, 0, 2)
        two = total[:, 4 * tile : 8 * tile].reshape(shard, 2, 2 * tile).transpose(1, 0, 2)
        proj = total[:, 8 * tile :].reshape(shard, 2, p).transpose(1, 0, 2)

    up_grad = jnp.concatenate(
        [v[side, :, :tile] for side in (0, 1) for v in (one, two)], axis=1
    )
    down_grad = jnp.concatenate(
        [v[side, :, tile:] for side in (0, 1) for v in (one, two)], axis=1
    ).T
    in_grad = jnp.concatenate(
        [proj[side, :, k * third : (k + 1) * third] for k in range(3) for side in (0, 1)], axis=1
    )
    out_grad = jnp.concatenate([proj[side, :, half : half + third] for side in (0, 1)], axis=1).T
    if fast:
        every, vectors = proj[0, :, half + third :], proj[1, :, half + third :]
    else:
        high = 4 * width // 128
        mine = proj_own[:high, half + third :], proj_oth[:high, half + third :]
        every, vectors = lax.psum(tuple(v.astype(F32) for v in mine), AXES)
    d_up_bias = lax.dynamic_slice(every.reshape(-1), (device * 4 * shard,), (4 * shard,))
    vectors = vectors.reshape(4, width)
    vectors = lax.dynamic_slice(vectors, (0, device * shard), (2, shard))
    gain_one = jnp.sum(project_in.astype(F32) * in_grad, axis=1) / first_gain.astype(F32)
    gain_two = jnp.sum(up_weight.astype(F32) * up_grad, axis=1) / second_gain.astype(F32)
    return (
        layer_out,
        input_grad,
        gain_one,
        in_grad,
        out_grad,
        gain_two,
        up_grad,
        d_up_bias,
        down_grad,
        vectors[0],
        vectors[1],
    )


def solution(mesh):
    both = ("wide", "narrow")
    rows3, rows2, rows1, cols = P(both, None, None), P(both, None), P(both), P(None, both)
    in_specs = (
        rows3, rows1, rows2, rows2, rows1, rows2, cols, rows1, rows2, rows1, cols, rows1, rows1, rows3,
    )
    out_specs = (rows3, rows3, rows1, rows2, cols, rows1, rows2, rows1, cols, rows1, rows1)
    return jax.shard_map(
        partial(per_device, wide=mesh.shape["wide"], narrow=mesh.shape["narrow"]),
        mesh=mesh,
        in_specs=in_specs,
        out_specs=out_specs,
        check_vma=False,
    )
```

```python
from functools import partial

import jax
import jax.numpy as jnp
import numpy as np
from jax import lax
from jax.experimental import pallas as pl
from jax.experimental.pallas import tpu as pltpu
from jax.sharding import PartitionSpec as P

HEAD_DIM = 64
EPSILON = 1e-06
NEG_FILL = -1e30
F32 = jnp.float32
BF16 = jnp.bfloat16
AXES = ("wide", "narrow")
SCALE = HEAD_DIM**-0.5
GELU_A = 0.7978845608028654
GELU_B = 0.044715
LSE_LANE = 16
MLP_CHUNKS = 4
PAIRS = 3
PLACE_ROWS = 512
ANY = pl.BlockSpec(memory_space=pl.ANY)
VMEM_LIMIT = 67043328


def dot(left, right, left_dim=1, right_dim=0):
    return lax.dot_general(
        left, right, (((left_dim,), (right_dim,)), ((), ())), preferred_element_type=F32
    )


def params(*semantics):
    return pltpu.CompilerParams(
        dimension_semantics=semantics or None, vmem_limit_bytes=VMEM_LIMIT
    )


def whole(shape):
    return pl.BlockSpec(shape, lambda *_: (0,) * len(shape))


def cost(flops, bytes_accessed):
    return pl.CostEstimate(
        flops=int(flops), bytes_accessed=int(bytes_accessed), transcendentals=0
    )


class Layout:
    def __init__(self, height, plane, blocks):
        self.height, self.plane, self.blocks = height, plane, tuple(blocks)
        self.pieces = 1 + max(piece for piece, *_ in blocks)
        self.depth = len(blocks) // plane

    def natural(self, here, step, line):
        return pl.multiple_of((line * self.plane + (here ^ step)) * self.height, 8)


def load_rows(layout, here, pieces, target, sems, source, columns):
    height = layout.height
    return [
        pltpu.make_async_copy(
            pieces[piece].at[pl.ds(at * height, height), source],
            target.at[pl.ds(layout.natural(here, step, line), height), columns],
            sems.at[j],
        )
        for j, (piece, at, step, line) in enumerate(layout.blocks)
    ]


def both_halves(layout, here, own, oth, target, sems, start, count):
    source = pl.ds(start, count)
    return load_rows(layout, here, own, target, sems.at[0], source, pl.ds(0, count)) + load_rows(
        layout, here, oth, target, sems.at[1], source, pl.ds(count, count)
    )


def store_rows(layout, target, value):
    height = layout.height
    for line in range(layout.depth):
        for owner in range(layout.plane):
            start = (owner * layout.depth + line) * height
            c = line * layout.plane + owner
            target[start : start + height, :] = value[c * height : (c + 1) * height, :]


def gather_kernel(target, x, cot, sel, grad):
    length = x.shape[1]
    places = lax.broadcasted_iota(jnp.int32, (target.shape[1], length), 1)
    chosen = jnp.where(target[0] == places, 1.0, 0.0).astype(BF16)
    sel[...] = dot(chosen, x[0]).astype(BF16)
    grad[...] = dot(chosen, cot[0]).astype(BF16)


def gather_rows(target, layer_in, cotangent):
    seqs, length, width = layer_in.shape
    slots = target.shape[1]
    big = pl.BlockSpec((1, length, width), lambda b: (b, 0, 0))
    out = pl.BlockSpec((slots, width), lambda b: (b, 0))
    return pl.pallas_call(
        gather_kernel,
        grid=(seqs,),
        in_specs=[pl.BlockSpec((1, slots, 1), lambda b: (b, 0, 0)), big, big],
        out_specs=[out, out],
        out_shape=[jax.ShapeDtypeStruct((seqs * slots, width), BF16)] * 2,
        compiler_params=params("arbitrary"),
        cost_estimate=cost(
            4 * seqs * slots * length * width, 4 * seqs * length * width
        ),
        name="gather_rows",
    )(target, layer_in, cotangent)


def allowed_keys(slots, valid):
    rows = lax.broadcasted_iota(jnp.int32, (2 * slots, slots), 0)
    rows = jnp.where(rows >= slots, rows - slots, rows)
    keys = lax.broadcasted_iota(jnp.int32, (2 * slots, slots), 1)
    return (keys <= rows) & (keys < valid)


def split_pair(pair):
    lane = lax.broadcasted_iota(jnp.int32, pair.shape, 1)
    zero = jnp.zeros_like(pair)
    first = lane < HEAD_DIM
    return jnp.concatenate(
        [jnp.where(first, pair, zero), jnp.where(first, zero, pair)], axis=0
    )


def join_pair(stacked):
    half = stacked.shape[0] // 2
    lane = lax.broadcasted_iota(jnp.int32, (half, stacked.shape[1]), 1)
    return jnp.where(lane < HEAD_DIM, stacked[:half], stacked[half:])


def pair_loop(pairs, body, carry, at_once=PAIRS):
    def step(k, carry):
        for p in range(at_once):
            carry = body(k * at_once + p, carry)
        return carry

    return lax.fori_loop(0, pairs // at_once, step, carry)


def pair_columns(pair, half_width):
    per_half = half_width // (2 * HEAD_DIM)
    base = (pair // per_half) * 3 * half_width + (pair % per_half) * 2 * HEAD_DIM
    return tuple(
        pl.ds(pl.multiple_of(base + k * half_width, 128), 2 * HEAD_DIM) for k in range(3)
    )


def forward_kernel(
    where, counts, sel, grad, *rest, layout, half, third
):
    own, oth = rest[: layout.pieces], rest[layout.pieces : 2 * layout.pieces]
    (
    qkv, att, mid, n2, n2t, g, gt, n1t, stats, vec, bias, gsum,
    w_in, w_out, w_ext, sem_in, sem_out, sem_ext,
    ) = rest[2 * layout.pieces :]
    b = pl.program_id(0)
    slots, width = sel.shape
    here = where[0]

    def in_copies():
        return both_halves(layout, here, own, oth, w_in, sem_in, 0, half)

    def out_copies():
        return both_halves(layout, here, own, oth, w_out, sem_out, half, third)

    @pl.when(b == 0)
    def _():
        small = both_halves(layout, here, own, oth, w_ext, sem_ext, half + third, 128)
        first = in_copies()
        for c in small + first + out_copies():
            c.start()
        for c in small:
            c.wait()
        per = width // 128
        high = 4 * per
        total = sum(w_ext[k * high : (k + 1) * high, :].astype(F32) for k in range(width // high))
        mine, others = total[:, :128], total[:, 128:]
        vectors = jnp.where(where[1] == 0, mine, others)
        biases = jnp.where(where[1] == 0, others, mine)
        vec[...] = jnp.zeros_like(vec)
        for v in range(4):
            for k in range(per):
                vec[v : v + 1, k * 128 : (k + 1) * 128] = vectors[v * per + k : v * per + k + 1, :]
        for k in range(bias.shape[1] // 128):
            bias[0:1, k * 128 : (k + 1) * 128] = biases[k : k + 1, :]
        for c in first:
            c.wait()

    x = sel[...].astype(F32)
    r1 = lax.rsqrt(jnp.mean(x * x, axis=-1, keepdims=True) + EPSILON)
    n1 = (x * r1 * vec[0:1, :]).astype(BF16)
    logit = jnp.sum(x * vec[3:4, :], axis=-1, keepdims=True)
    rate = jax.nn.sigmoid(logit)
    d_mlp = (rate * grad[...].astype(F32)).astype(BF16)
    g[...] = d_mlp
    gsum_now = jnp.sum(d_mlp.astype(F32), axis=0, keepdims=True)

    @pl.when(b == 0)
    def _():
        gsum[...] = gsum_now

    @pl.when(b > 0)
    def _():
        gsum[...] += gsum_now

    store_rows(layout, gt, d_mlp.T)
    store_rows(layout, n1t, n1.T)
    qkv[...] = dot(n1, w_in[...]).astype(BF16)

    allowed = allowed_keys(slots, counts[b])
    lane = lax.broadcasted_iota(jnp.int32, (slots, 128), 1)
    kept = jnp.where(lane == 0, r1, jnp.where(lane == 1, rate, 0.0))

    def attend(pair, kept):
        qc, kc, vc = pair_columns(pair, width // 2)
        scores = dot(split_pair(qkv[:, qc] * SCALE), qkv[:, kc], 1, 1)
        scores = jnp.where(allowed, scores, NEG_FILL)
        top = jnp.max(scores, axis=-1, keepdims=True)
        exps = jnp.exp(scores - top)
        total = jnp.sum(exps, axis=-1, keepdims=True)
        lse = top + jnp.log(total)
        probs = (exps * (1.0 / total)).astype(BF16)
        here_now = pl.ds(pl.multiple_of(pair * 128, 128), 128)
        att[:, here_now] = join_pair(dot(probs, qkv[:, vc])).astype(BF16)
        kept = jnp.where(lane == LSE_LANE + 2 * pair, lse[:slots], kept)
        return jnp.where(lane == LSE_LANE + 2 * pair + 1, lse[slots:], kept)

    kept = pair_loop(width // (2 * HEAD_DIM), attend, kept, 2 * PAIRS)

    @pl.when(b == 0)
    def _():
        for c in out_copies():
            c.wait()

    stream = x + dot(att[...], w_out[...], 1, 1)
    mid[...] = stream
    r2 = lax.rsqrt(jnp.mean(stream * stream, axis=-1, keepdims=True) + EPSILON)
    normed = (stream * r2 * vec[1:2, :]).astype(BF16)
    n2[...] = normed
    store_rows(layout, n2t, normed.T)
    stats[...] = jnp.where(lane == 2, r2, kept)


def forward_block(layout, hidden, where, counts, sel, grad, own, oth):
    rows, width = sel.shape
    seqs = counts.shape[0]
    slots = rows // seqs
    blocks = len(layout.blocks)
    row = lambda w: pl.BlockSpec((slots, w), lambda b, *_: (b, 0))
    col = pl.BlockSpec((width, slots), lambda b, *_: (0, b))
    shape = jax.ShapeDtypeStruct
    return pl.pallas_call(
        partial(forward_kernel, layout=layout, half=3 * width // 2, third=width // 2),
        grid_spec=pltpu.PrefetchScalarGridSpec(
            num_scalar_prefetch=2,
            grid=(seqs,),
            in_specs=[row(width), row(width)] + [ANY] * (2 * layout.pieces),
            out_specs=[
                row(3 * width), row(width), row(width), row(width), col, row(width), col, col, row(128),
                whole((8, width)), whole((1, hidden)), whole((1, width)),
            ],
            scratch_shapes=[
                pltpu.VMEM((width, 3 * width), BF16),
                pltpu.VMEM((width, width), BF16),
                pltpu.VMEM((width, 256), BF16),
                pltpu.SemaphoreType.DMA((2, blocks)),
                pltpu.SemaphoreType.DMA((2, blocks)),
                pltpu.SemaphoreType.DMA((2, blocks)),
            ],
        ),
        out_shape=[
            shape((rows, 3 * width), BF16),
            shape((rows, width), BF16),
            shape((rows, width), F32),
            shape((rows, width), BF16),
            shape((width, rows), BF16),
            shape((rows, width), BF16),
            shape((width, rows), BF16),
            shape((width, rows), BF16),
            shape((rows, 128), F32),
            shape((8, width), F32),
            shape((1, hidden), F32),
            shape((1, width), F32),
        ],
        compiler_params=params("arbitrary"),
        cost_estimate=cost(10 * rows * width * width, 30 * rows * width),
        name="forward_block",
    )(where, counts, sel, grad, *own, *oth)


def mlp_kernel(where, bias, *rest, layout, tile):
    rows_in = rest[:4]
    own, oth = rest[4 : 4 + layout.pieces], rest[4 + layout.pieces : 4 + 2 * layout.pieces]
    mlp, dn2, d_own, d_oth, dbias, *held, w_up, w_down, d_first, act, d_pre, sem_rows, sems, sem_out = rest[
        4 + 2 * layout.pieces :
    ]
    n2, n2t, g, gt, mlp_sum, dn2_sum = held
    i = pl.program_id(0)
    here = where[0]
    row_copies = [
        pltpu.make_async_copy(rows_in[k], held[k], sem_rows.at[k]) for k in range(4)
    ]
    out_copy = pltpu.make_async_copy(d_first, d_own, sem_out)

    def copies(side, kind):
        source, target = (own, oth)[side], (w_up, w_down)[kind].at[side]
        return load_rows(
            layout, here, source, target, sems.at[side, kind], pl.ds(kind * tile, tile), pl.ds(0, tile)
        )

    def wait_first(*waited):
        @pl.when(i == 0)
        def _():
            for c in waited:
                c.wait()

    @pl.when(i == 0)
    def _():
        started = copies(0, 0) + row_copies[:1] + copies(0, 1) + row_copies[2:3]
        started = started + row_copies[1:2] + row_copies[3:] + copies(1, 0) + copies(1, 1)
        for c in started:
            c.start()

    wait_first(*copies(0, 0), row_copies[0])

    @pl.when(i == 1)
    def _():
        out_copy.start()
        for c in copies(1, 0) + copies(1, 1):
            c.wait()

    wait_first(*copies(0, 1), row_copies[2])
    up_now = w_up.at[i]
    down_now = w_down.at[i]
    rows = n2.shape[0] // MLP_CHUNKS

    def chunk(c, total):
        here = pl.ds(pl.multiple_of(c * rows, rows), rows)
        pre = dot(n2[here, :], up_now[...]) + bias[...]
        square = pre * pre
        th = jnp.tanh(pre * (GELU_A + GELU_A * GELU_B * square))
        half = 0.5 * (1.0 + th)
        act_now = (pre * half).astype(BF16)
        act[here, :] = act_now
        slope = half + 0.5 * pre * (1.0 - th * th) * (GELU_A + 3 * GELU_A * GELU_B * square)
        d_pre_now = (slope * dot(g[here, :], down_now[...])).astype(BF16)
        d_pre[here, :] = d_pre_now
        mlp_now = jnp.where(i == 0, 0.0, mlp_sum[here, :]) + dot(act_now, down_now[...], 1, 1)
        mlp_sum[here, :] = mlp_now
        mlp[here, :] = mlp_now.astype(BF16)
        dn2_now = jnp.where(i == 0, 0.0, dn2_sum[here, :]) + dot(d_pre_now, up_now[...], 1, 1)
        dn2_sum[here, :] = dn2_now
        dn2[here, :] = dn2_now.astype(BF16)
        return total + jnp.sum(d_pre_now.astype(F32), axis=0, keepdims=True)

    dbias[...] = lax.fori_loop(0, MLP_CHUNKS, chunk, jnp.zeros_like(dbias))
    wait_first(row_copies[1], row_copies[3])
    dup = dot(n2t[...], d_pre[...]).astype(BF16)
    ddown = dot(gt[...], act[...]).astype(BF16)

    @pl.when(i == 0)
    def _():
        d_first[:, :tile] = dup
        d_first[:, tile:] = ddown

    @pl.when(i == 1)
    def _():
        d_oth[:, :tile] = dup
        d_oth[:, tile:] = ddown
        out_copy.wait()


def mlp_part(layout, where, part, tile, n2, n2t, g, gt, own, oth, bias):
    rows, width = n2.shape
    parts = bias.shape[1] // (2 * tile)
    blocks = len(layout.blocks)
    shape = jax.ShapeDtypeStruct
    return pl.pallas_call(
        partial(mlp_kernel, layout=layout, tile=tile),
        grid_spec=pltpu.PrefetchScalarGridSpec(
            num_scalar_prefetch=1,
            grid=(2,),
            in_specs=[
                pl.BlockSpec((1, tile), lambda i, where: (0, (where[1] ^ i) * parts + part)),
            ] + [ANY] * (4 + 2 * layout.pieces),
            out_specs=[
                whole((rows, width)), whole((rows, width)), ANY, whole((width, 2 * tile)),
                pl.BlockSpec((1, tile), lambda i, where: (0, i)),
            ],
            scratch_shapes=[
                pltpu.VMEM((rows, width), BF16),
                pltpu.VMEM((width, rows), BF16),
                pltpu.VMEM((rows, width), BF16),
                pltpu.VMEM((width, rows), BF16),
                pltpu.VMEM((rows, width), F32),
                pltpu.VMEM((rows, width), F32),
                pltpu.VMEM((2, width, tile), BF16),
                pltpu.VMEM((2, width, tile), BF16),
                pltpu.VMEM((width, 2 * tile), BF16),
                pltpu.VMEM((rows, tile), BF16),
                pltpu.VMEM((rows, tile), BF16),
                pltpu.SemaphoreType.DMA((4,)),
                pltpu.SemaphoreType.DMA((2, 2, blocks)),
                pltpu.SemaphoreType.DMA,
            ],
        ),
        out_shape=[
            shape((rows, width), BF16),
            shape((rows, width), BF16),
            shape((width, 2 * tile), BF16),
            shape((width, 2 * tile), BF16),
            shape((1, 2 * tile), F32),
        ],
        compiler_params=params("arbitrary"),
        cost_estimate=cost(24 * rows * width * tile, 8 * rows * width),
        name="mlp_part",
    )(where, bias, n2, n2t, g, gt, *own, *oth)


def norm_pull(values, inverse, scaled):
    return inverse * scaled - values * (
        inverse * inverse * inverse * jnp.mean(scaled * values, axis=-1, keepdims=True)
    )


def backward_kernel(
    where, counts, sel, grad, vec, qkv, mid, stats, mlp, mlp_two, dn2, dn2_two, *rest, layout, half, third
):
    own, oth = rest[: layout.pieces], rest[layout.pieces : 2 * layout.pieces]
    dqkv, dattnt, dmid, new_rows, drouter, w_out, d_att, sem_out = rest[2 * layout.pieces :]
    b = pl.program_id(0)
    slots, width = sel.shape
    here = where[0]

    @pl.when(b == 0)
    def _():
        copies = both_halves(layout, here, own, oth, w_out, sem_out, half, third)
        for c in copies:
            c.start()
        for c in copies:
            c.wait()

    x = sel[...].astype(F32)
    stream = mid[...]
    rate = stats[:, 1:2]
    r2 = stats[:, 2:3]
    slot_grad = grad[...].astype(F32)
    branch = (stream - x) + (mlp[...].astype(F32) + mlp_two[...].astype(F32) + vec[2:3, :])
    new_rows[...] = (x + rate * branch).astype(BF16)
    d_logit = jnp.sum(slot_grad * branch, axis=-1, keepdims=True) * (rate * (1.0 - rate))
    router_now = jnp.sum(d_logit * x, axis=0, keepdims=True)

    @pl.when(b == 0)
    def _():
        drouter[...] = router_now

    @pl.when(b > 0)
    def _():
        drouter[...] += router_now

    d_mid = norm_pull(stream, r2, vec[1:2, :] * (dn2[...].astype(F32) + dn2_two[...].astype(F32)))
    dmid[...] = d_mid + d_logit * vec[3:4, :]
    d_attn = (rate * slot_grad + d_mid).astype(BF16)
    store_rows(layout, dattnt, d_attn.T)
    d_att[...] = dot(d_attn, w_out[...]).astype(BF16)

    allowed = allowed_keys(slots, counts[b])
    lane = lax.broadcasted_iota(jnp.int32, (slots, 128), 1)

    def pull(pair, carry):
        qc, kc, vc = pair_columns(pair, width // 2)
        queries = split_pair(qkv[:, qc] * SCALE)
        keys = qkv[:, kc]
        lse = jnp.concatenate(
            [
                jnp.sum(jnp.where(lane == LSE_LANE + 2 * pair + k, stats[...], 0.0), axis=-1, keepdims=True)
                for k in (0, 1)
            ],
            axis=0,
        )
        upstream = split_pair(d_att[:, pl.ds(pl.multiple_of(pair * 128, 128), 128)])
        scores = dot(queries, keys, 1, 1)
        probs = jnp.exp(jnp.where(allowed, scores - lse, NEG_FILL))
        d_probs = dot(upstream, qkv[:, vc], 1, 1)
        d_scores = (probs * (d_probs - jnp.sum(probs * d_probs, axis=-1, keepdims=True))).astype(BF16)
        dqkv[:, qc] = (join_pair(dot(d_scores, keys)) * SCALE).astype(BF16)
        dqkv[:, kc] = dot(d_scores, queries, 0, 0).astype(BF16)
        dqkv[:, vc] = dot(probs.astype(BF16), upstream, 0, 0).astype(BF16)
        return carry

    pair_loop(width // (2 * HEAD_DIM), pull, 0)


def backward_block(layout, where, counts, sel, grad, vec, qkv, mid, stats, sums, own, oth):
    rows, width = sel.shape
    seqs = counts.shape[0]
    slots = rows // seqs
    blocks = len(layout.blocks)
    row = lambda w: pl.BlockSpec((slots, w), lambda b, *_: (b, 0))
    col = pl.BlockSpec((width, slots), lambda b, *_: (0, b))
    shape = jax.ShapeDtypeStruct
    return pl.pallas_call(
        partial(backward_kernel, layout=layout, half=3 * width // 2, third=width // 2),
        grid_spec=pltpu.PrefetchScalarGridSpec(
            num_scalar_prefetch=2,
            grid=(seqs,),
            in_specs=[
                row(width), row(width), whole(vec.shape), row(3 * width), row(width), row(128),
            ] + [row(width)] * 4 + [ANY] * (2 * layout.pieces),
            out_specs=[row(3 * width), col, row(width), row(width), whole((1, width))],
            scratch_shapes=[
                pltpu.VMEM((width, width), BF16),
                pltpu.VMEM((slots, width), BF16),
                pltpu.SemaphoreType.DMA((2, blocks)),
            ],
        ),
        out_shape=[
            shape((rows, 3 * width), BF16),
            shape((width, rows), BF16),
            shape((rows, width), F32),
            shape((rows, width), BF16),
            shape((1, width), F32),
        ],
        compiler_params=params("arbitrary"),
        cost_estimate=cost(2 * 20 * rows * width * width, 2 * 30 * rows * width),
        name="backward_block",
    )(where, counts, sel, grad, vec, qkv, mid, stats, *sums, *own, *oth)


def project_kernel(where, n1t, dattnt, dqkv, att, dbias_one, dbias_two, ddown, drouter, oth, own):
    half = dqkv.shape[1]
    third = att.shape[1]
    width = n1t.shape[0]
    high, tile = 4 * width // 128, dbias_one.shape[1] // 2
    in_now = dot(n1t[...], dqkv[...]).astype(BF16)
    out_now = dot(dattnt[...], att[...]).astype(BF16)
    first_core = where[1] == 0

    def bias_rows():
        rows = []
        for side in (0, 1):
            for part in (dbias_one, dbias_two):
                for k in range(tile // 128):
                    a, b = side * tile + k * 128, (1 - side) * tile + k * 128
                    rows.append(jnp.where(first_core, part[:, a : a + 128], part[:, b : b + 128]))
        return rows

    def vector_rows():
        rows = [v[:, k * 128 : (k + 1) * 128] for v in (ddown, drouter) for k in range(width // 128)]
        return rows + [jnp.zeros((1, 128), F32)] * (high - len(rows))

    def store(out, is_first):
        out[:, :half] = in_now
        out[:, half : half + third] = out_now
        small = jnp.where(
            is_first, jnp.concatenate(bias_rows(), axis=0), jnp.concatenate(vector_rows(), axis=0)
        )
        small = jnp.concatenate([small] * 2, axis=0).astype(BF16)
        for k in range(width // (2 * high)):
            out[2 * k * high : 2 * (k + 1) * high, half + third :] = small

    pl.when(pl.program_id(0) == 0)(lambda: store(oth, where[1] == 1))
    pl.when(pl.program_id(0) == 1)(lambda: store(own, where[1] == 0))


def project_grads(where, n1t, dattnt, dqkv, att, *vectors):
    width, rows = n1t.shape
    half, third = dqkv.shape[1] // 2, att.shape[1] // 2
    total = half + third + 128
    return pl.pallas_call(
        project_kernel,
        grid_spec=pltpu.PrefetchScalarGridSpec(
            num_scalar_prefetch=1,
            grid=(2,),
            in_specs=[
                whole((width, rows)), whole((width, rows)),
                pl.BlockSpec((rows, half), lambda i, where: (0, 1 - i)),
                pl.BlockSpec((rows, third), lambda i, where: (0, 1 - i)),
            ] + [whole(v.shape) for v in vectors],
            out_specs=[whole((width, total))] * 2,
        ),
        out_shape=[jax.ShapeDtypeStruct((width, total), BF16)] * 2,
        compiler_params=params("arbitrary"),
        cost_estimate=cost(2 * 4 * width * rows * total, 2 * 4 * width * rows),
        name="project_grads",
    )(where, n1t, dattnt, dqkv, att, *vectors)


def place(out, rows, target, x, start, count):
    chunk = min(PLACE_ROWS, x.shape[1])

    def one(c, carry):
        here = pl.ds(pl.multiple_of(c * chunk, chunk), chunk)
        places = lax.broadcasted_iota(jnp.int32, (chunk, target.shape[2]), 0) + c * chunk
        hits = target[0] == places
        moved = dot(jnp.where(hits, 1.0, 0.0).astype(BF16), rows[...])
        hit = jnp.max(jnp.where(hits, 1.0, 0.0), axis=-1, keepdims=True)
        at = lax.broadcasted_iota(jnp.int32, (chunk, 1), 0) + c * chunk
        kept = (at >= start) & (at < start + count) & (hit < 0.5)
        out[0, here, :] = jnp.where(kept, x[0, here, :].astype(F32), moved).astype(BF16)
        return carry

    lax.fori_loop(0, x.shape[1] // chunk, one, 0)


def out_kernel(runs, rows, target, x, out):
    b = pl.program_id(0)
    place(out, rows, target, x, runs[0, b], runs[1, b])


def place_rows(runs, rows, target, x):
    seqs, length, width = x.shape
    slots = target.shape[2]
    big = pl.BlockSpec((1, length, width), lambda b, *_: (b, 0, 0))
    return pl.pallas_call(
        out_kernel,
        grid_spec=pltpu.PrefetchScalarGridSpec(
            num_scalar_prefetch=1,
            grid=(seqs,),
            in_specs=[
                pl.BlockSpec((slots, width), lambda b, *_: (b, 0)),
                pl.BlockSpec((1, 1, slots), lambda b, *_: (b, 0, 0)),
                big,
            ],
            out_specs=big,
        ),
        out_shape=jax.ShapeDtypeStruct(x.shape, BF16),
        compiler_params=params("arbitrary"),
        cost_estimate=cost(2 * seqs * slots * length * width, 4 * seqs * length * width),
        name="place_rows",
    )(runs, rows, target, x)


def input_kernel(
    where, runs, sel, grad, vec, stats, dmid, dqkv, target, x, *rest, layout, first
):
    own, oth = rest[: layout.pieces], rest[layout.pieces : 2 * layout.pieces]
    *_, out, w_in, moved, sem_in = rest[2 * layout.pieces :]
    b = pl.program_id(0)

    @pl.when(b == 0)
    def _():
        copies = both_halves(layout, where[0], own, oth, w_in, sem_in, 0, w_in.shape[1] // 2)
        for c in copies:
            c.start()
        for c in copies:
            c.wait()

    d_normed = dot(dqkv[...], w_in[...], 1, 1)
    d_sel = norm_pull(sel[...].astype(F32), stats[:, 0:1], vec[0:1, :] * d_normed) + dmid[...]
    moved[...] = (grad[...].astype(F32) + d_sel).astype(BF16)
    place(out, moved, target, x, runs[0, first + b], runs[1, first + b])


def input_rows(layout, where, runs, sel, grad, vec, stats, dmid, dqkv, target, x, own, oth, first, count, begun=()):
    seqs, length, width = x.shape
    slots = target.shape[2]
    blocks = len(layout.blocks)
    row = lambda w: pl.BlockSpec((slots, w), lambda b, *_: (first + b, 0))
    big = pl.BlockSpec((1, length, width), lambda b, *_: (first + b, 0, 0))
    return pl.pallas_call(
        partial(input_kernel, layout=layout, first=first),
        grid_spec=pltpu.PrefetchScalarGridSpec(
            num_scalar_prefetch=2,
            grid=(count,),
            in_specs=[
                row(width), row(width), whole(vec.shape), row(128), row(width), row(3 * width),
                pl.BlockSpec((1, 1, slots), lambda b, *_: (first + b, 0, 0)),
                big,
            ] + [ANY] * (2 * layout.pieces + len(begun)),
            out_specs=big,
            scratch_shapes=[
                pltpu.VMEM((width, 3 * width), BF16),
                pltpu.VMEM((slots, width), BF16),
                pltpu.SemaphoreType.DMA((2, blocks)),
            ],
        ),
        out_shape=jax.ShapeDtypeStruct(x.shape, BF16),
        compiler_params=params("arbitrary"),
        cost_estimate=cost(1, 1),
        input_output_aliases={10 + 2 * layout.pieces: 0} if begun else {},
        name="input_rows",
    )(where, runs, sel, grad, vec, stats, dmid, dqkv, target, x, *own, *oth, *begun)


class Paths:
    def __init__(self, wide, narrow, here):
        self.wide, self.narrow, self.depth, self.here = wide, narrow, wide // 2, here
        ids = np.arange(wide * narrow).reshape(self.depth, 4, 2)
        self.lines = ids.transpose(1, 0, 2).reshape(4, -1).tolist()
        self.planes = ids.transpose(0, 2, 1).reshape(-1, 4).tolist()

    def swap(self, value):
        return lax.ppermute(value, "narrow", [(i, i ^ 1) for i in range(self.narrow)])

    def over(self, value, step):
        if step == 1:
            return lax.ppermute(value, "narrow", [(i, i ^ 2) for i in range(self.narrow)])
        if step == 2:
            return lax.ppermute(value, "wide", [(i, i ^ 1) for i in range(self.wide)])
        mask = self.narrow ^ 2
        return lax.ppermute(value, AXES, [(i, i ^ mask) for i in range(self.wide * self.narrow)])

    def along(self, value):
        return lax.all_to_all(value, AXES, 0, 0, axis_index_groups=self.lines, tiled=True)

    def to_line(self, halves):
        shard, cols = halves[0].shape
        sent = jnp.broadcast_to(jnp.stack(halves)[None], (self.depth, 2, shard, cols))
        return sent.reshape(self.depth * 2 * shard, cols)

    def gather_halved(self, held):
        near_x, near_y = self.over(held, 1), self.over(held, 2)
        mid = held.shape[0] // 2
        return [held, near_x, near_y, self.over(near_y[:mid], 1), self.over(near_x[mid:], 2)]

    def gather_direct(self, held):
        return [held] + [self.over(held, step) for step in (1, 2, 3)]

    def swap_all(self, pieces):
        return [self.swap(p) for p in pieces]

    def chip_sums(self, own, got):
        rows = own.shape[0] // 4
        starts = [(self.here ^ step) * rows for step in range(4)]
        return [
            add_halves(
                lax.dynamic_slice(own, (start, 0), (rows, own.shape[1])),
                lax.dynamic_slice(got, (start, 0), (rows, own.shape[1])),
            )
            for start in starts
        ]

    def exchange_plane(self, both):
        return lax.all_to_all(both, AXES, 0, 0, axis_index_groups=self.planes, tiled=True)

    def send_plane(self, sums):
        return [self.over(sums[step], step) for step in (1, 2, 3)]

    def sum_plane(self, mine, got):
        total = mine.astype(F32)
        for v in got:
            total = total + v.astype(F32)
        return total.astype(BF16)

    def sum_line(self, got):
        return jnp.sum(got.reshape(self.depth, 2, -1, got.shape[1]).astype(F32), axis=0)


def halved(depth):
    return [(piece, z, piece, z) for piece in range(3) for z in range(depth)] + [
        (3 + (z >= depth // 2), z % (depth // 2), 3, z) for z in range(depth)
    ]


def direct(depth):
    return [(piece, z, piece, z) for piece in range(4) for z in range(depth)]


def add_halves(own, got):
    return (own.astype(F32) + got.astype(F32)).astype(BF16)


def tie(*values):
    return lax.optimization_barrier(values)


def per_device(
    layer_in,
    lengths,
    padding,
    picked,
    first_gain,
    project_in,
    project_out,
    second_gain,
    up_weight,
    up_bias,
    down_weight,
    down_bias,
    router,
    cotangent,
    *,
    wide,
    narrow,
):
    seqs, slots = picked.shape
    shard, in_width = project_in.shape
    width = in_width // 3
    hidden = up_weight.shape[1]
    devices = wide * narrow
    half = 3 * width // 2
    third = width // 2
    tile = hidden // 4
    fast = shard == 24 and wide % 4 == 0 and narrow == 4
    core = lax.axis_index("narrow") & 1 if fast else jnp.int32(0)
    device = lax.axis_index("wide") * narrow + lax.axis_index("narrow")

    in_split = project_in.reshape(shard, 3, 2, third)
    in_halves = [in_split[:, :, side].reshape(shard, half) for side in (0, 1)]
    out_t = project_out.T
    down_t = down_weight.T
    vectors = jnp.stack([first_gain, second_gain, down_bias, router])

    first = [
        jnp.concatenate([in_halves[side], out_t[:, side * third : (side + 1) * third]], axis=1)
        for side in (0, 1)
    ]

    def rest_of(side, part):
        at = (2 * side + part) * tile
        return jnp.concatenate([up_weight[:, at : at + tile], down_t[:, at : at + tile]], axis=1)

    def places(lengths):
        counts = lengths // 8
        valid = jnp.arange(slots)[None, :] < counts[:, None]
        target = jnp.where(valid, picked, -1)
        runs = jnp.stack([jnp.argmax(padding, axis=1).astype(jnp.int32), lengths])
        return counts, runs, target[:, :, None], target[:, None, :]

    if fast:
        here = (lax.axis_index("wide") & 1) * 2 + (lax.axis_index("narrow") >> 1)
        paths = Paths(wide, narrow, here)
        lay_one = Layout(2 * shard, 4, halved(paths.depth))
        lay_two = Layout(2 * shard, 4, direct(paths.depth))
        placed = lax.dynamic_update_slice(
            jnp.zeros((4, width), BF16), vectors, (0, device * shard)
        ).reshape(shard, 128)
        biases = lax.dynamic_update_slice(
            jnp.zeros((hidden,), BF16), up_bias, (device * 4 * shard,)
        ).reshape(shard, 128)
        sent = paths.to_line(
            [
                jnp.concatenate([first[0], placed], axis=1),
                jnp.concatenate([first[1], biases], axis=1),
            ]
        )
        sent, lengths = tie(sent, lengths)
        line = paths.along(sent)
        counts, runs, columns, target_row = places(lengths)
        rest = paths.to_line(
            [jnp.concatenate([rest_of(side, 0), rest_of(side, 1)], axis=1) for side in (0, 1)]
        )
        rest, columns = tie(rest, columns)
        sel, slot_grad = gather_rows(columns, layer_in, cotangent)
        line, rest, sel, slot_grad, runs, target_row = tie(line, rest, sel, slot_grad, runs, target_row)
        own = paths.gather_halved(line)
        oth = paths.swap_all(own)
        rest = paths.along(rest)
        own, oth, rest, sel = tie(own, oth, rest, sel)
        one_own = paths.gather_direct(rest[:, : 2 * tile])
        two_own = paths.gather_direct(rest[:, 2 * tile :])
    else:
        counts, runs, columns, target_row = places(lengths)
        here = jnp.int32(0)
        lay_one = lay_two = Layout(width, 1, [(0, 0, 0, 0)])
        packed = jnp.concatenate(
            first + [rest_of(side, part) for part in (0, 1) for side in (0, 1)], axis=1
        )
        full = lax.all_gather(packed, AXES, axis=0, tiled=True)
        cuts = [0]
        for n in (half + third,) * 2 + (2 * tile,) * 4:
            cuts.append(cuts[-1] + n)
        own, oth, one_own, one_oth, two_own, two_oth = (
            [full[:, a:b]] for a, b in zip(cuts, cuts[1:])
        )
        every = lax.all_gather(vectors, AXES, axis=1, tiled=True).reshape(-1, 128)
        biases = lax.all_gather(up_bias, AXES, axis=0, tiled=True).reshape(-1, 128)
        own, oth = (
            [jnp.concatenate([p[0], jnp.pad(v, ((0, width - v.shape[0]), (0, 0)))], axis=1)]
            for p, v in ((own, every), (oth, biases))
        )
        sel, slot_grad = gather_rows(columns, layer_in, cotangent)

    where = jnp.stack([here, core]).astype(jnp.int32)
    qkv, att, mid, n2, n2t, g, gt, n1t, stats, vec, bias, ddown_bias = forward_block(
        lay_one, hidden, where, counts, sel, slot_grad, own, oth
    )
    if fast:
        one_own, n2 = tie(one_own, n2)
        one_oth = paths.swap_all(one_own)
        two_first, n2 = tie(paths.swap(two_own[0]), n2)
    mlp, dn2, d_one_own, d_one_oth, dbias_one = mlp_part(
        lay_two, where, 0, tile, n2, n2t, g, gt, one_own, one_oth, bias
    )
    if fast:
        two_own, mlp, n2 = tie(two_own, mlp, n2)
        two_oth = [two_first] + paths.swap_all(two_own[1:])
        d_one_got = paths.swap(d_one_oth)
    mlp_two, dn2_two, d_two_own, d_two_oth, dbias_two = mlp_part(
        lay_two, where, 1, tile, n2, n2t, g, gt, two_own, two_oth, bias
    )
    if fast:
        d_one_got, mlp_two = tie(d_one_got, mlp_two)
        d_one = paths.chip_sums(d_one_own, d_one_got)
        d_one_plane = paths.send_plane(d_one)
        d_two = add_halves(d_two_own, paths.swap(d_two_oth))
        d_two, mlp_two = tie(d_two, mlp_two)
        d_two = paths.exchange_plane(d_two)
    dqkv, dattnt, dmid, new_rows, drouter = backward_block(
        lay_one, where, counts, sel, slot_grad, vec, qkv, mid, stats, (mlp, mlp_two, dn2, dn2_two), own, oth
    )

    proj_oth, proj_own = project_grads(
        where, n1t, dattnt, dqkv, att, dbias_one, dbias_two, ddown_bias, drouter
    )
    if fast:
        d_one_plane, d_two, proj_oth = tie(d_one_plane, d_two, proj_oth)
        proj_got = paths.swap(proj_oth)
        proj = paths.chip_sums(proj_own, proj_got)
        d_two = d_two.reshape(4, -1, 2 * tile)
        sums = jnp.concatenate(
            [paths.sum_plane(d_one[0], d_one_plane), paths.sum_plane(d_two[0], list(d_two[1:]))], axis=1
        )
        sums, proj, new_rows = tie(sums, proj, new_rows)
        proj_plane = paths.send_plane(proj)
        sums = paths.along(sums)
    layer_out = place_rows(runs, new_rows, target_row, layer_in)
    if fast:
        dmid, layer_out = tie(dmid, layer_out)
    part = seqs // 2
    input_grad = input_rows(
        lay_one, where, runs, sel, slot_grad, vec, stats, dmid, dqkv, target_row, cotangent, own, oth, 0, part
    )
    if fast:
        proj = paths.sum_plane(proj[0], proj_plane)
        sums, proj, dmid, input_grad = tie(sums, proj, dmid, input_grad)
    input_grad = input_rows(
        lay_one, where, runs, sel, slot_grad, vec, stats, dmid, dqkv, target_row, cotangent, own, oth,
        part, seqs - part, (input_grad,),
    )

    if fast:
        sums = paths.sum_line(sums)
        one, two = sums[:, :, : 2 * tile], sums[:, :, 2 * tile :]
        proj = paths.sum_line(paths.along(proj))
    else:
        flat = jnp.concatenate(
            [d_one_own, d_one_oth, d_two_own, d_two_oth, proj_own, proj_oth], axis=1
        )
        total = lax.psum_scatter(flat.astype(F32), AXES, scatter_dimension=0, tiled=True)
        p = proj_own.shape[1]
        one = total[:, : 4 * tile].reshape(shard, 2, 2 * tile).transpose(1, 0, 2)
        two = total[:, 4 * tile : 8 * tile].reshape(shard, 2, 2 * tile).transpose(1, 0, 2)
        proj = total[:, 8 * tile :].reshape(shard, 2, p).transpose(1, 0, 2)

    up_grad = jnp.concatenate(
        [v[side, :, :tile] for side in (0, 1) for v in (one, two)], axis=1
    )
    down_grad = jnp.concatenate(
        [v[side, :, tile:] for side in (0, 1) for v in (one, two)], axis=1
    ).T
    in_grad = jnp.concatenate(
        [proj[side, :, k * third : (k + 1) * third] for k in range(3) for side in (0, 1)], axis=1
    )
    out_grad = jnp.concatenate([proj[side, :, half : half + third] for side in (0, 1)], axis=1).T
    if fast:
        every, vectors = proj[0, :, half + third :], proj[1, :, half + third :]
    else:
        high = 4 * width // 128
        mine = proj_own[:high, half + third :], proj_oth[:high, half + third :]
        every, vectors = lax.psum(tuple(v.astype(F32) for v in mine), AXES)
    d_up_bias = lax.dynamic_slice(every.reshape(-1), (device * 4 * shard,), (4 * shard,))
    vectors = vectors.reshape(4, width)
    vectors = lax.dynamic_slice(vectors, (0, device * shard), (2, shard))
    gain_one = jnp.sum(project_in.astype(F32) * in_grad, axis=1) / first_gain.astype(F32)
    gain_two = jnp.sum(up_weight.astype(F32) * up_grad, axis=1) / second_gain.astype(F32)
    return (
        layer_out,
        input_grad,
        gain_one,
        in_grad,
        out_grad,
        gain_two,
        up_grad,
        d_up_bias,
        down_grad,
        vectors[0],
        vectors[1],
    )


def solution(mesh):
    both = ("wide", "narrow")
    rows3, rows2, rows1, cols = P(both, None, None), P(both, None), P(both), P(None, both)
    in_specs = (
        rows3, rows1, rows2, rows2, rows1, rows2, cols, rows1, rows2, rows1, cols, rows1, rows1, rows3,
    )
    out_specs = (rows3, rows3, rows1, rows2, cols, rows1, rows2, rows1, cols, rows1, rows1)
    return jax.shard_map(
        partial(per_device, wide=mesh.shape["wide"], narrow=mesh.shape["narrow"]),
        mesh=mesh,
        in_specs=in_specs,
        out_specs=out_specs,
        check_vma=False,
    )
```
